32 devices in a mesh: tm: 8 (over z, x), series: 4 (over y, core).
Axes of the slice: x: 2, y: 2, z: 4, core: 2. Of those that a mesh axis runs over, the one named last changes fastest.
Arguments:
- readings: bfloat16 [128, 4096], P('tm', 'series'), may hold values from -8 to 8
- present: int32 [128, 4096], P('tm', 'series'), may hold values 0 or 1
- loadings: bfloat16 [4096, 128], P('series'), may hold values from -1 to 1
- noise_precision: float32 [4096], P('series'), may hold values from 0.5 to 2
- update_gain: float32 [128], replicated, may hold values from 3.125e-05 to 0.03125
- factor_rate: float32 [128], replicated, may hold values from 0.0001 to 0.01
- smooth_rate: float32 [128], replicated, may hold values from 0.0001 to 0.05
- regions: int32 [4096], P('series'), may hold values from 0 to 15
Outputs:
- smoothed: float32 [128, 128], P('tm')
- histogram: float32 [16, 20], replicated
The draws below stay inside these ranges and needn't reach their ends.
All inputs are finite; a program needn't handle non-finite values. No bound on the sum of `present` on one device may be relied on, other than what follows from the above.
Results may differ from the reference program's by a relative error of at most 0.0004.
Values sent between devices are 32-bit elements; how exact they have to be, the bound alone decides.
A program may use at most 64 MiB of HBM per device.

```python
import math
import jax
import jax.numpy as jnp
from jax import lax

K = 128
BINS = 20
GROUPS = 16
T_SIZE = 128
NS = 4096


def model_draw(key):
    base = jax.random.fold_in(key, 7001)
    rate_key = jax.random.fold_in(base, 1)
    start_key = jax.random.fold_in(base, 2)
    shock_key = jax.random.fold_in(base, 3)
    load_key = jax.random.fold_in(base, 4)
    noise_key = jax.random.fold_in(base, 5)
    one_minus = jnp.exp(jax.random.uniform(rate_key, (K,), jnp.float32, math.log(0.001), math.log(0.1)))
    coef = 1.0 - one_minus
    innov = jnp.sqrt(one_minus * (2.0 - one_minus))
    start = jax.random.normal(start_key, (K,), jnp.float32)
    shocks = jax.random.normal(shock_key, (T_SIZE, K), jnp.float32)

    def advance(level, shock):
        level = coef * level + innov * shock
        return (level, level)
    _, path = lax.scan(advance, start, shocks)
    loadings = jnp.clip(jax.random.normal(load_key, (NS, K), jnp.float32) * (2.0 * K) ** (-0.5), -1.0, 1.0)
    noise = jax.random.normal(noise_key, (T_SIZE, NS), jnp.float32) * 0.7
    common = jnp.dot(path, loadings.T, precision=lax.Precision.HIGHEST)
    readings = jnp.clip(common + noise, -8.0, 8.0)
    return (readings, loadings)


def draw_readings(key, part):
    readings, _ = model_draw(key)
    return readings.astype(jnp.bfloat16)


def draw_loadings(key, part):
    _, loadings = model_draw(key)
    return loadings.astype(jnp.bfloat16)


def with_ends(entries, own_key, smallest, largest):
    shape = entries.shape
    spot = [jax.random.randint(jax.random.fold_in(own_key, axis), (), 0, shape[axis]) for axis in range(len(shape))]
    entries = entries.at[tuple(spot)].set(smallest)
    longest = shape.index(max(shape))
    spot[longest] = (spot[longest] + 1) % shape[longest]
    return entries.at[tuple(spot)].set(largest)


def levels(rng, dims, cuts, smallest, high):
    def one(axis_at, blocks):
        steps = jax.random.uniform(jax.random.fold_in(jax.random.fold_in(rng, 6), axis_at), (blocks,), jnp.float32, smallest / len(cuts), high / len(cuts))
        return jnp.repeat(jnp.exp(steps), dims[axis_at] // blocks).reshape((-1,) + (1,) * (len(dims) - axis_at - 1))

    level = one(*cuts[0])
    for cut in cuts[1:]:
        level = level * one(*cut)
    return level


def setup_inputs(seed: int = 0) -> dict:
    splits = jax.random.split(jax.random.key(seed), 9)
    return {
        "readings": draw_readings(jax.random.fold_in(splits[8], 71), 0),
        "present": with_ends((jax.random.randint(splits[1], (T_SIZE, NS), 0, 5) < 4).astype(jnp.int32), jax.random.fold_in(splits[1], 1), 0, 1),
        "loadings": draw_loadings(jax.random.fold_in(splits[8], 71), 0),
        "noise_precision": jnp.clip(jnp.exp(math.log(2.0) - 1.3862944 * jax.random.uniform(splits[3], (NS,), jnp.float32) ** levels(splits[3], (NS,), ((0, 4),), -0.2, 0.2)), 0.5, 2.0),
        "update_gain": jnp.clip(jnp.exp(jax.random.uniform(splits[4], (K,), jnp.float32, math.log(3.125000148429535e-05), math.log(0.03125))), 3.125000148429535e-05, 0.03125),
        "factor_rate": jnp.clip(jnp.exp(jax.random.uniform(splits[5], (K,), jnp.float32, math.log(0.0001), math.log(0.01))), 0.0001, 0.01),
        "smooth_rate": jnp.clip(jnp.exp(jax.random.uniform(splits[6], (K,), jnp.float32, math.log(0.0001), math.log(0.05))), 0.0001, 0.05),
        "regions": with_ends(jax.random.randint(splits[7], (NS,), 0, GROUPS), jax.random.fold_in(splits[7], 1), 0, GROUPS - 1).astype(jnp.int32),
    }


highest = lax.Precision.HIGHEST

def normal_cdf(values):
    return 0.5 * (1.0 + lax.erf(values * 0.7071067811865476))

def reference(readings, present, loadings, noise_precision, update_gain, factor_rate, smooth_rate, regions):
    weight = present.astype(jnp.float32) * noise_precision[None, :]

    def per_hour(hour):
        scaled = (loadings * weight[hour][:, None]).astype(jnp.bfloat16)
        inform = lax.dot_general(scaled, loadings, (((0,), (0,)), ((), ())), preferred_element_type=jnp.float32)
        scores = jnp.dot(readings[hour], scaled, preferred_element_type=jnp.float32)
        return (inform, scores)
    inform, scores = lax.map(per_hour, jnp.arange(T_SIZE))
    decays = jnp.exp(-factor_rate)
    retain = jnp.exp(-smooth_rate)
    identity = jnp.eye(K, dtype=jnp.float32)

    def forward(current, stepped):
        inform_t, scores_t = stepped
        transit = (identity - update_gain[:, None] * inform_t) * decays[None, :]
        current = jnp.dot(transit, current, precision=highest) + update_gain * scores_t
        return (current, current)
    _, filtered = lax.scan(forward, jnp.zeros((K,), jnp.float32), (inform, scores))
    boundary = decays * filtered[-1]

    def backward(following, filter_row):
        smooth_row = (1.0 - retain * decays) * filter_row + retain * following
        return (smooth_row, smooth_row)
    _, smoothed = lax.scan(backward, boundary, filtered, reverse=True)
    fitted = lax.dot_general(smoothed.astype(jnp.bfloat16), loadings, (((1,), (1,)), ((), ())), preferred_element_type=jnp.float32)
    standard = (readings.astype(jnp.float32) - fitted) * jnp.sqrt(noise_precision)[None, :]
    probab = normal_cdf(standard)
    observed = present.astype(jnp.float32)
    member = (regions[:, None] == jnp.arange(GROUPS)[None, :]).astype(jnp.float32)
    binned = []
    for bin_index in range(BINS):
        kernel = jnp.maximum(0.0, 1.0 - BINS * jnp.abs(probab - (bin_index + 0.5) / BINS))
        binned.append(lax.optimization_barrier(jnp.sum(observed * kernel, axis=0)))
    bin_table = jnp.stack(binned)
    tallies = jnp.dot(bin_table, member, precision=highest)
    histogram = tallies.T * (BINS * GROUPS / (T_SIZE * NS))
    return (smoothed, histogram)
```

```python
import functools

import jax
import jax.numpy as jnp
from jax import lax
from jax.experimental import pallas as pl
from jax.experimental.pallas import tpu as pltpu
from jax.sharding import PartitionSpec as P

BINS = 20
GROUPS = 16
MESH = pl.DeviceIdType.MESH
F32 = jnp.float32
BF16 = jnp.bfloat16


def split2(x):
    high = x.astype(BF16)
    return high, (x - high.astype(F32)).astype(BF16)


def halves(right):
    high, low = split2(right)
    return jnp.concatenate([high, low], axis=0)


def dot_halves(left, right):
    high, low = split2(left)
    both = jnp.concatenate(
        [
            jnp.concatenate([high, high], axis=1),
            jnp.concatenate([low, jnp.zeros_like(low)], axis=1),
        ],
        axis=0,
    )
    out = jnp.dot(both, right, preferred_element_type=F32)
    return out[: left.shape[0]] + out[left.shape[0] :]


def dot3(left, right):
    return dot_halves(left, halves(right))


def compose(earlier, later, factors):
    out = dot3(earlier, later[:factors])
    return jnp.concatenate([out[:factors], out[factors:] + later[factors:]], axis=0)


def kernel(
    tms, sers,
    readings_in, present_in, loadings_in, prec_in, gain_in, frate_in, srate_in, regions_in,
    smoothed_ref, hist_ref,
    readings_ref, present_ref, loadings_ref, prec_ref, gain_ref, frate_ref, srate_ref, regions_ref,
    lt_s, sl_s, mem_s, score_s, send1, recv1, acc, recv2, cum, dmap, drecv, emaps, esend, smaps, ssend, lead_s,
    vin, vout, vcur, tsend, trecv, fown, fall, shown, shifts, table, hown, hall,
    ins, s1s, s1r, s2s, s2r, ds, dr, es, er, ss, sr, vs, vr, ts, tr, fs, fr, cs, cr, hs, hr,
):
    tm, ser = lax.axis_index("tm"), lax.axis_index("series")
    y, core = ser // 2, ser % 2
    ys = sers // 2
    local = readings_ref.shape[0]
    factors = loadings_ref.shape[1]
    rows = factors + 8
    hours = local // sers
    n = tms * sers
    me = tm * sers + ser
    pair, a = tm // 2, tm % 2
    pairs = tms // 2
    chips = 2 * ys
    g = a * ys + y

    barrier = pltpu.get_barrier_semaphore()

    plane = 2 * sers
    place_in = a * sers + ser

    def plane_peer(k):
        at = lax.rem(place_in + k, plane)
        return pair * 2 + at // sers, lax.rem(at, sers)

    for k in range(1, plane):
        pl.semaphore_signal(barrier, inc=1, device_id=plane_peer(k), device_id_type=MESH)
    inputs = [
        pltpu.make_async_copy(src, dst, ins.at[i])
        for i, (src, dst) in enumerate(
            [
                (loadings_in, loadings_ref), (prec_in, prec_ref), (present_in, present_ref),
                (readings_in, readings_ref), (gain_in, gain_ref), (frate_in, frate_ref),
                (srate_in, srate_ref), (regions_in, regions_ref),
            ]
        )
    ]

    @pl.when(pair > 0)
    def _():
        pl.semaphore_signal(barrier, inc=1, device_id=(tm - 2, ser), device_id_type=MESH)

    @pl.when(pair < pairs - 1)
    def _():
        pl.semaphore_signal(barrier, inc=1, device_id=(tm + 2, ser), device_id_type=MESH)

    @pl.when(pair > 1)
    def _():
        pl.semaphore_signal(barrier, inc=1, device_id=(tm - 4, ser), device_id_type=MESH)

    @pl.when(pair < pairs - 2)
    def _():
        pl.semaphore_signal(barrier, inc=1, device_id=(tm + 4, ser), device_id_type=MESH)

    for item in inputs:
        item.start()
    for item in inputs[:2]:
        item.wait()

    ltf = loadings_ref[...].astype(F32).T
    lt_s[...] = ltf.astype(BF16)
    sl_s[...] = (ltf * prec_ref[...]).T.astype(BF16)
    for item in inputs[2:4]:
        item.wait()
    present = present_ref[...].astype(F32)
    read_f = readings_ref[...].astype(F32)
    score_s[0:local] = jnp.dot(
        (read_f * present).astype(BF16), sl_s[...], preferred_element_type=F32
    )
    score_s[local:] = jnp.zeros_like(score_s[local:])

    half = factors // 2
    together_h = 2 if hours % 2 == 0 else 1
    sets = hours // together_h
    low_at = together_h * half

    def hour_terms(hour, dst):
        lower = []
        line = lax.broadcasted_iota(jnp.int32, (8, factors), 0)
        score = jnp.zeros((8, factors), F32)
        for j in range(together_h):
            mask = present_ref[pl.ds(hour + j, 1), :].astype(F32)
            mask = jnp.broadcast_to(mask, (16, mask.shape[1])).astype(BF16)
            left = lt_s[...].reshape(factors // 16, 16, mask.shape[1]) * mask[None]
            out = jnp.dot(
                left.reshape(factors, mask.shape[1]), sl_s[...], preferred_element_type=F32
            )
            dst[j * half : (j + 1) * half] = out[:half]
            lower.append(out[half:])
            row = jnp.broadcast_to(score_s[pl.ds(hour + j, 1), :], (8, factors))
            score = jnp.where(line == j, row, score)
        if together_h == 2:
            lane = lax.broadcasted_iota(jnp.int32, (half, factors), 1)
            dst[low_at : low_at + half] = jnp.where(
                lane >= half, lower[0], pltpu.roll(lower[1], half, 1)
            )
        else:
            dst[low_at : low_at + half] = lower[0]
        dst[low_at + half :] = score

    def unpack(packed, j):
        upper = packed[j * half : (j + 1) * half]
        lower = packed[low_at : low_at + half]
        right = lower[:, half:] if j == 0 else lower[:, :half]
        matrix = jnp.concatenate(
            [upper, jnp.concatenate([upper[:, half:].T, right], axis=1)], axis=0
        )
        first = lax.broadcasted_iota(jnp.int32, (8, factors), 0) == 0
        row = jnp.broadcast_to(packed[low_at + half + j : low_at + half + j + 1], (8, factors))
        return matrix, jnp.where(first, row, 0.0)

    def copy1(k, h):
        return pltpu.make_async_remote_copy(
            send1.at[k, h], recv1.at[k, h], s1s.at[k, h], s1r.at[k, h],
            device_id=(tm, y * 2 + (1 - core)), device_id_type=MESH,
        )

    def copy2(k, h):
        return pltpu.make_async_remote_copy(
            acc.at[k, h], recv2.at[k, h], s2s.at[k, h], s2r.at[k, h],
            device_id=(tm, lax.rem(y + k, ys) * 2 + core), device_id_type=MESH,
        )

    order = list(range(1, ys)) + [0]
    for place, k in enumerate(order):
        owner = lax.rem(y + k, ys) * 2
        for h in range(sets):
            hour_terms((owner + (1 - core)) * hours + h * together_h, send1.at[k, h])
            if place == 0 and h == 0:
                before = jnp.where(pair > 0, 1, 0) + jnp.where(pair > 1, 1, 0)
                behind = jnp.where(pair < pairs - 1, 1, 0) + jnp.where(pair < pairs - 2, 1, 0)
                pl.semaphore_wait(barrier, plane - 1 + before + behind)
            copy1(k, h).start()
        for h in range(sets):
            hour_terms((owner + core) * hours + h * together_h, acc.at[k, h])
            if k:
                copy1(k, h).wait_recv()
                acc[k, h] = acc[k, h] + recv1[k, h]
                copy2(k, h).start()

    for item in inputs[4:]:
        item.wait()
    wide = lax.broadcasted_iota(jnp.int32, (factors, regions_ref.shape[1]), 0) % GROUPS
    mem_s[...] = jnp.where(wide == regions_ref[...], 1.0, 0.0).astype(F32).T.astype(BF16)
    gain = gain_ref[...]
    decays = jnp.exp(-frate_ref[...])
    srate = srate_ref[...]
    retain = jnp.exp(-srate)
    keep = 1.0 - retain * decays
    eye = (
        lax.broadcasted_iota(jnp.int32, (factors, factors), 0)
        == lax.broadcasted_iota(jnp.int32, (factors, factors), 1)
    )
    eye_f = jnp.where(eye, 1.0, 0.0).astype(F32)
    decay_col = jnp.sum(jnp.where(eye, decays, 0.0), axis=1, keepdims=True)
    for h in range(sets):
        copy1(0, h).wait_recv()

    maps = []
    for h in range(sets):
        total = acc[0, h] + recv1[0, h]
        for k in range(1, ys):
            copy2(k, h).wait_recv()
            total = total + recv2[k, h]
        for j in range(together_h):
            inform, scores = unpack(total, j)
            maps.append(
                jnp.concatenate([decay_col * (eye_f - gain * inform), gain * scores], axis=0)
            )
    step = 1
    while step < hours:
        maps = [
            compose(maps[h - step], maps[h], factors) if h >= step else maps[h]
            for h in range(hours)
        ]
        step *= 2
    dmap[0] = maps[-1]
    adds = keep * maps[0]
    for h in range(1, hours):
        adds = adds + keep * jnp.exp(-float(h) * srate) * maps[h]
    dmap[1] = adds
    dcopy = pltpu.make_async_remote_copy(
        dmap, drecv, ds, dr, device_id=(tm, y * 2 + (1 - core)), device_id_type=MESH
    )
    dcopy.start()
    for h in range(hours):
        cum[:, h * factors : (h + 1) * factors] = maps[h]
    dcopy.wait_recv()
    mine, other = dmap[0], drecv[0]
    leads = core == 0
    whole = compose(jnp.where(leads, mine, other), jnp.where(leads, other, mine), factors)
    esend[...] = whole

    def ecopy(k):
        to = lax.rem(g + k, chips)
        return pltpu.make_async_remote_copy(
            esend, emaps.at[k], es.at[k], er.at[k],
            device_id=(pair * 2 + to // ys, lax.rem(to, ys) * 2 + core), device_id_type=MESH,
        )

    for k in range(1, chips):
        ecopy(k).start()
    emaps[0] = whole
    first = jnp.where(leads, mine, other)
    mine_adds, other_adds = dmap[1], drecv[1]
    chip_adds = jnp.where(leads, mine_adds, other_adds) + jnp.exp(-float(hours) * srate) * compose(
        first, jnp.where(leads, other_adds, mine_adds), factors
    )
    ssend[...] = chip_adds

    def scopy(k):
        to = lax.rem(g + k, chips)
        return pltpu.make_async_remote_copy(
            ssend, smaps.at[k], ss.at[k], sr.at[k],
            device_id=(pair * 2 + to // ys, lax.rem(to, ys) * 2 + core), device_id_type=MESH,
        )

    for k in range(1, chips):
        scopy(k).start()
    smaps[0] = chip_adds
    span = 2 * local
    after = (a + 1) * local
    hour_at = (
        lax.broadcasted_iota(jnp.int32, (plane, hours, factors), 0) * hours
        + lax.broadcasted_iota(jnp.int32, (plane, hours, factors), 1)
    )
    far = (hour_at - after).astype(F32)
    tail_w = jnp.where(far >= 0.0, keep[None] * jnp.exp(-jnp.maximum(far, 0.0) * srate[None]), 0.0)
    end_w = jnp.exp(-(span - after).astype(F32) * srate)
    span_w = jnp.exp(-float(span) * srate)
    for k in range(1, chips):
        ecopy(k).wait_recv()
    parts = [emaps[lax.rem(g - at + chips, chips)] for at in range(chips)]
    level = parts
    while len(level) > 1:
        level = [
            compose(level[i], level[i + 1], factors) if i + 1 < len(level) else level[i]
            for i in range(0, len(level), 2)
        ]
    total = level[0]

    def vcopy(far):
        return pltpu.make_async_remote_copy(
            vout, vin, vs.at[far - 1], vr,
            device_id=(lax.rem(tm + 2 * far, tms), ser), device_id_type=MESH,
        )

    tcopy = pltpu.make_async_remote_copy(
        tsend, trecv, ts, tr, device_id=(lax.rem(tm + 2, tms), ser), device_id_type=MESH
    )
    odd = pair % 2 == 1
    hands_map = (pair % 2 == 0) & (pair > 0) & (pair < pairs - 1)

    @pl.when(hands_map)
    def _():
        tsend[...] = total
        tcopy.start()

    @pl.when(pair == 0)
    def _():
        vcur[...] = jnp.zeros_like(vcur)
        vout[...] = total[factors : factors + 1]
        vcopy(1).start()

    def carry(vector, matrix, shift):
        column = jnp.sum(jnp.where(eye, vector, 0.0), axis=1, keepdims=True)
        return jnp.sum(column * matrix, axis=0, keepdims=True) + shift

    def forward():
        vcopy(1).wait_recv()
        vcur[...] = vin[...]

        @pl.when(odd & (pair > 1))
        def _():
            tcopy.wait_recv()
            vcur[...] = carry(vin[...], trecv[0:factors], trecv[factors : factors + 1])

        @pl.when(odd & (pair < pairs - 1))
        def _():
            vout[...] = carry(vcur[...], total[:factors], total[factors : factors + 1])
            vcopy(1).start()

            @pl.when(pair < pairs - 2)
            def _():
                vcopy(2).start()

    @pl.when(pair == 1)
    def _():
        forward()

    unit = jnp.concatenate([eye_f, jnp.zeros((8, factors), F32)], axis=0)
    start_map = unit
    before_chip = [parts[0]]
    for at in range(1, chips):
        start_map = jnp.where(g == at, before_chip[-1], start_map)
        if at + 1 < chips:
            before_chip.append(compose(before_chip[-1], parts[at], factors))
    start_map = jnp.where(leads, start_map, compose(start_map, other, factors))
    cums = cum[...]
    lead = dot3(start_map, cums[:factors])
    wide_at = hours * factors
    lead_s[:, :wide_at] = halves(lead[:factors])
    lead_b = lead[factors:] + cums[factors:]
    at_end = pair == pairs - 1
    for k in range(1, chips):
        scopy(k).wait_recv()
    group_adds = smaps[lax.rem(g, chips)] + jnp.where(at_end, span_w * decays, 0.0) * total
    for at in range(1, chips):
        group_adds = group_adds + jnp.exp(-float(2 * hours * at) * srate) * compose(
            before_chip[at - 1], smaps[lax.rem(g - at + chips, chips)], factors
        )
    lead_s[:, wide_at:] = halves(group_adds[:factors])
    lead_b = jnp.concatenate([lead_b, group_adds[factors:]], axis=1)

    @pl.when(pair > 1)
    def _():
        forward()

    current = jnp.broadcast_to(vcur[...], (8, factors))
    filtered = dot_halves(current, lead_s[...]) + lead_b
    for h in range(hours):
        row = filtered[0:1, h * factors : (h + 1) * factors]
        fown[h : h + 1, :] = row
    shown[...] = filtered[:, hours * factors :]

    def ccopy(to, of):
        return pltpu.make_async_remote_copy(
            shown, shifts.at[of], cs.at[to], cr.at[of],
            device_id=(to * 2 + a, ser), device_id_type=MESH,
        )

    @pl.loop(0, pair)
    def _(to):
        ccopy(to, pair).start()

    fall[place_in] = fown[...]

    def fcopy(k):
        return pltpu.make_async_remote_copy(
            fown, fall.at[place_in], fs.at[k], fr.at[k],
            device_id=plane_peer(k), device_id_type=MESH,
        )

    for k in range(1, plane):
        fcopy(k).start()
    prec_root = jnp.sqrt(prec_ref[...])
    for k in range(1, plane):
        fcopy(k).wait_recv()
    together = fall[...]
    ending = decays * together[plane - 1][hours - 1 : hours]
    follow = jnp.sum(jnp.sum(together * tail_w, axis=0), axis=0, keepdims=True)

    def gather(of, held):
        total, weight = held
        ccopy(pair, of).wait_recv()
        return total + weight * shifts[of][0:1], weight * span_w

    beyond, _ = lax.fori_loop(
        pair + 1, pairs, gather, (jnp.where(at_end, ending, 0.0), jnp.ones_like(span_w))
    )
    follow = follow + end_w * beyond
    for s in range(sers - 1, -1, -1):
        block = fall[a * sers + s]
        for h in range(hours - 1, -1, -1):
            follow = keep * block[h : h + 1] + retain * follow
            smoothed_ref[s * hours + h : s * hours + h + 1, :] = follow

    fitted = jnp.dot(smoothed_ref[...].astype(BF16), lt_s[...], preferred_element_type=F32)
    standard = (readings_ref[...].astype(F32) - fitted) * prec_root
    probab = 0.5 * (1.0 + lax.erf(standard * 0.7071067811865476))
    spot = jnp.where(present_ref[...] > 0, probab * BINS - 0.5, -4.0)
    for b in range(BINS):
        table[b : b + 1, :] = jnp.sum(
            jnp.maximum(0.0, 1.0 - jnp.abs(spot - b)), axis=0, keepdims=True
        )
    padded = table.shape[0]
    if padded > BINS:
        table[BINS:, :] = jnp.zeros_like(table[BINS:, :])
    th, tl = split2(table[...])
    tally = jnp.dot(
        jnp.concatenate([th, tl], axis=0), mem_s[...], preferred_element_type=F32
    )
    tally = tally[:padded] + tally[padded:]
    lane = lax.broadcasted_iota(jnp.int32, tally.shape, 1) // GROUPS
    sub = lax.broadcasted_iota(jnp.int32, tally.shape, 0) % 8
    tally = jnp.where(lane == sub, tally, 0.0).reshape(padded // 8, 8, tally.shape[1])
    hown[...] = jnp.sum(tally, axis=1)
    hall[me] = hown[...]

    def hsend(k):
        at = lax.rem(place_in + (plane - 1 - k % plane), plane)
        to = lax.rem(pair + (pairs - 1 - k // plane), pairs)
        pltpu.make_async_remote_copy(
            hown, hall.at[me], hs, hr,
            device_id=(to * 2 + at // sers, lax.rem(at, sers)), device_id_type=MESH,
        ).start()

    if n <= 64:
        for k in range(n - 1):
            hsend(k)
    else:
        pl.loop(0, n - 1)(hsend)

    for k in range(ys):
        for h in range(sets):
            copy1(k, h).wait_send()
            if k:
                copy2(k, h).wait_send()
    dcopy.wait_send()
    for k in range(1, chips):
        ecopy(k).wait_send()
        scopy(k).wait_send()

    @pl.when((odd | (pair == 0)) & (pair < pairs - 1))
    def _():
        vcopy(1).wait_send()

    @pl.when(odd & (pair < pairs - 2))
    def _():
        vcopy(2).wait_send()

    @pl.when(hands_map)
    def _():
        tcopy.wait_send()

    for k in range(1, plane):
        fcopy(k).wait_send()

    @pl.loop(0, pair)
    def _(to):
        ccopy(to, pair).wait_send()

    hdrain = pltpu.make_async_remote_copy(
        hall.at[pl.ds(0, n - 1)], hall.at[pl.ds(0, n - 1)], hs, hr,
        device_id=(tm, lax.rem(ser + 1, sers)), device_id_type=MESH,
    )
    hdrain.wait_recv()
    hdrain.wait_send()
    hist_ref[...] = jnp.sum(hall[...], axis=0)


def solution(mesh):
    tms, sers = mesh.shape["tm"], mesh.shape["series"]

    def body(readings, present, loadings, prec, gain, frate, srate, regions):
        local, series = readings.shape
        factors = loadings.shape[1]
        hours = local // sers
        n, ys = tms * sers, sers // 2
        chips = 2 * ys
        rows = factors + 8
        padded = -(-BINS // 8) * 8
        together = 2 if hours % 2 == 0 else 1
        sets, packed_rows = hours // together, (together + 1) * (factors // 2) + 8
        vm = pltpu.VMEM
        dma = pltpu.SemaphoreType.DMA
        smoothed, packed = pl.pallas_call(
            functools.partial(kernel, tms, sers),
            out_shape=(
                vm((local, factors), F32),
                vm((padded // 8, 8 * GROUPS), F32),
            ),
            in_specs=[pl.BlockSpec(memory_space=pl.ANY)] * 8,
            out_specs=(pl.BlockSpec(memory_space=vm),) * 2,
            scratch_shapes=[
                vm((local, series), readings.dtype),
                vm((local, series), present.dtype),
                vm((series, factors), loadings.dtype),
                vm((1, series), F32),
                vm((1, factors), F32),
                vm((1, factors), F32),
                vm((1, factors), F32),
                vm((1, series), regions.dtype),
                vm((factors, series), BF16),
                vm((series, factors), BF16),
                vm((series, 8 * GROUPS), BF16),
                vm((local + 8, factors), F32),
                vm((ys, sets, packed_rows, factors), F32),
                vm((ys, sets, packed_rows, factors), F32),
                vm((ys, sets, packed_rows, factors), F32),
                vm((ys, sets, packed_rows, factors), F32),
                vm((rows, hours * factors), F32),
                vm((2, rows, factors), F32),
                vm((2, rows, factors), F32),
                vm((chips, rows, factors), F32),
                vm((rows, factors), F32),
                vm((chips, rows, factors), F32),
                vm((rows, factors), F32),
                vm((2 * factors, (hours + 1) * factors), BF16),
                vm((1, factors), F32),
                vm((1, factors), F32),
                vm((1, factors), F32),
                vm((rows, factors), F32),
                vm((rows, factors), F32),
                vm((hours, factors), F32),
                vm((2 * sers, hours, factors), F32),
                vm((8, factors), F32),
                vm((tms // 2, 8, factors), F32),
                vm((padded, series), F32),
                vm((padded // 8, 8 * GROUPS), F32),
                vm((n, padded // 8, 8 * GROUPS), F32),
                dma((8,)),
                dma((ys, sets)),
                dma((ys, sets)),
                dma((ys, sets)),
                dma((ys, sets)),
                dma, dma,
                dma((chips,)),
                dma((chips,)),
                dma((chips,)),
                dma((chips,)),
                dma((2,)), dma, dma, dma,
                dma((2 * sers,)),
                dma((2 * sers,)),
                dma((tms // 2,)),
                dma((tms // 2,)),
                dma, dma,
            ],
            compiler_params=pltpu.CompilerParams(collective_id=0, has_side_effects=True),
        )(
            readings, present, loadings, prec.reshape(1, -1), gain.reshape(1, -1),
            frate.reshape(1, -1), srate.reshape(1, -1), regions.reshape(1, -1),
        )
        scale = BINS * GROUPS / (local * tms * series * sers)
        histogram = packed.reshape(-1, GROUPS)[:BINS].T * scale
        return smoothed, histogram

    in_specs = (
        P("tm", "series"), P("tm", "series"), P("series", None), P("series"),
        P(), P(), P(), P("series"),
    )
    return jax.shard_map(
        body, mesh=mesh, in_specs=in_specs, out_specs=(P("tm", None), P()), check_vma=False
    )
```

```python
import functools

import jax
import jax.numpy as jnp
from jax import lax
from jax.experimental import pallas as pl
from jax.experimental.pallas import tpu as pltpu
from jax.sharding import PartitionSpec as P

BINS = 20
GROUPS = 16
MESH = pl.DeviceIdType.MESH
F32 = jnp.float32
BF16 = jnp.bfloat16


def split2(x):
    high = x.astype(BF16)
    return high, (x - high.astype(F32)).astype(BF16)


def halves(right):
    high, low = split2(right)
    return jnp.concatenate([high, low], axis=0)


def dot_halves(left, right):
    high, low = split2(left)
    both = jnp.concatenate(
        [
            jnp.concatenate([high, high], axis=1),
            jnp.concatenate([low, jnp.zeros_like(low)], axis=1),
        ],
        axis=0,
    )
    out = jnp.dot(both, right, preferred_element_type=F32)
    return out[: left.shape[0]] + out[left.shape[0] :]


def dot3(left, right):
    return dot_halves(left, halves(right))


def compose(earlier, later, factors):
    out = dot3(earlier, later[:factors])
    return jnp.concatenate([out[:factors], out[factors:] + later[factors:]], axis=0)


def kernel(
    tms, sers,
    readings_in, present_in, loadings_in, prec_in, gain_in, frate_in, srate_in, regions_in,
    smoothed_ref, hist_ref,
    readings_ref, present_ref, loadings_ref, prec_ref, gain_ref, frate_ref, srate_ref, regions_ref,
    lt_s, sl_s, mem_s, score_s, send1, recv1, acc, recv2, cum, dmap, drecv, emaps, esend, smaps, ssend, lead_s,
    vin, vout, vcur, bin_s, tsend, trecv, fown, fall, shown, shifts, table, hown, hall,
    ins, s1s, s1r, s2s, s2r, ds, dr, es, er, ss, sr, vs, vr, vls, bs, br, ts, tr, fs, fr, cs, cr, hs, hr,
):
    tm, ser = lax.axis_index("tm"), lax.axis_index("series")
    y, core = ser // 2, ser % 2
    ys = sers // 2
    local = readings_ref.shape[0]
    factors = loadings_ref.shape[1]
    rows = factors + 8
    hours = local // sers
    n = tms * sers
    me = tm * sers + ser
    pair, a = tm // 2, tm % 2
    pairs = tms // 2
    chips = 2 * ys
    g = a * ys + y
    leader = (pair == 0) & (g == chips - 1)

    inputs = [
        pltpu.make_async_copy(src, dst, ins.at[i])
        for i, (src, dst) in enumerate(
            [
                (loadings_in, loadings_ref), (prec_in, prec_ref), (present_in, present_ref),
                (readings_in, readings_ref), (gain_in, gain_ref), (frate_in, frate_ref),
                (srate_in, srate_ref), (regions_in, regions_ref),
            ]
        )
    ]
    for item in inputs:
        item.start()

    barrier = pltpu.get_barrier_semaphore()

    plane = 2 * sers
    place_in = a * sers + ser

    def plane_peer(k):
        at = lax.rem(place_in + k, plane)
        return pair * 2 + at // sers, lax.rem(at, sers)

    for k in range(1, plane):
        pl.semaphore_signal(barrier, inc=1, device_id=plane_peer(k), device_id_type=MESH)
    @pl.when(pair > 0)
    def _():
        pl.semaphore_signal(barrier, inc=1, device_id=(tm - 2, ser), device_id_type=MESH)

    @pl.when(pair < pairs - 1)
    def _():
        pl.semaphore_signal(barrier, inc=1, device_id=(tm + 2, ser), device_id_type=MESH)

    @pl.when(pair > 1)
    def _():
        pl.semaphore_signal(barrier, inc=1, device_id=(tm - 4, ser), device_id_type=MESH)

    @pl.when(pair < pairs - 2)
    def _():
        pl.semaphore_signal(barrier, inc=1, device_id=(tm + 4, ser), device_id_type=MESH)

    @pl.when((pair == 1) & (g < chips - 1))
    def _():
        pl.semaphore_signal(
            barrier, inc=1, device_id=(1, (ys - 1) * 2 + core), device_id_type=MESH
        )

    for item in inputs[:2]:
        item.wait()

    ltf = loadings_ref[...].astype(F32).T
    lt_s[...] = ltf.astype(BF16)
    sl_s[...] = (ltf * prec_ref[...]).T.astype(BF16)
    for item in inputs[2:4]:
        item.wait()
    present = present_ref[...].astype(F32)
    read_f = readings_ref[...].astype(F32)
    score_s[0:local] = jnp.dot(
        (read_f * present).astype(BF16), sl_s[...], preferred_element_type=F32
    )
    score_s[local:] = jnp.zeros_like(score_s[local:])

    together_h = 2 if hours % 2 == 0 else 1
    sets = hours // together_h
    sub = lax.broadcasted_iota(jnp.int32, (factors, factors), 0)
    lane = lax.broadcasted_iota(jnp.int32, (factors, factors), 1)
    eye = sub == lane
    upper = lane > sub
    line = lax.broadcasted_iota(jnp.int32, (8, factors), 0)

    def hour_terms(base, dst):
        lefts = []
        for j in range(hours):
            mask = present_ref[pl.ds(base + j, 1), :].astype(F32)
            mask = jnp.broadcast_to(mask, (16, mask.shape[1])).astype(BF16)
            left = lt_s[...].reshape(factors // 16, 16, mask.shape[1]) * mask[None]
            lefts.append(left.reshape(factors, mask.shape[1]))
        out = jnp.dot(
            jnp.concatenate(lefts, axis=0), sl_s[...], preferred_element_type=F32
        )
        for h in range(sets):
            at = h * together_h
            first = out[at * factors : (at + 1) * factors]
            tail = jnp.zeros((8, factors), F32)
            if together_h == 2:
                second = out[(at + 1) * factors : (at + 2) * factors]
                dst[h, :factors] = jnp.where(upper, first, second)
                corner = jnp.sum(jnp.where(eye, first, 0.0), axis=0, keepdims=True)
                tail = jnp.where(line == together_h, corner, tail)
            else:
                dst[h, :factors] = first
            for j in range(together_h):
                row = jnp.broadcast_to(score_s[pl.ds(base + at + j, 1), :], (8, factors))
                tail = jnp.where(line == j, row, tail)
            dst[h, factors:] = tail

    def unpack(packed):
        block, tail = packed[:factors], packed[factors:]
        if together_h == 1:
            matrices = [block]
        else:
            turned = block.T
            matrices = [
                jnp.where(eye, tail[together_h : together_h + 1], jnp.where(upper, block, turned)),
                jnp.where(upper, turned, block),
            ]
        return [
            (matrices[j], jnp.where(line == 0, tail[j : j + 1], 0.0)) for j in range(together_h)
        ]

    def copy1(k, h):
        return pltpu.make_async_remote_copy(
            send1.at[k, h], recv1.at[k, h], s1s.at[k, h], s1r.at[k, h],
            device_id=(tm, y * 2 + (1 - core)), device_id_type=MESH,
        )

    def copy2(k, h):
        return pltpu.make_async_remote_copy(
            acc.at[k, h], recv2.at[k, h], s2s.at[k, h], s2r.at[k, h],
            device_id=(tm, lax.rem(y + k, ys) * 2 + core), device_id_type=MESH,
        )

    order = list(range(1, ys)) + [0]
    for place, k in enumerate(order):
        owner = lax.rem(y + k, ys) * 2
        hour_terms((owner + (1 - core)) * hours, send1.at[k])
        if place == 0:
            before = jnp.where(pair > 0, 1, 0) + jnp.where(pair > 1, 1, 0)
            behind = jnp.where(pair < pairs - 1, 1, 0) + jnp.where(pair < pairs - 2, 1, 0)
            extra = jnp.where(leader, chips - 1, 0)
            pl.semaphore_wait(barrier, plane - 1 + before + behind + extra)
        for h in range(sets):
            copy1(k, h).start()
        hour_terms((owner + core) * hours, acc.at[k])
        if k:
            for h in range(sets):
                copy1(k, h).wait_recv()
                acc[k, h] = acc[k, h] + recv1[k, h]
                copy2(k, h).start()

    for item in inputs[4:]:
        item.wait()
    wide = lax.broadcasted_iota(jnp.int32, (factors, regions_ref.shape[1]), 0) % GROUPS
    mem_s[...] = jnp.where(wide == regions_ref[...], 1.0, 0.0).astype(F32).T.astype(BF16)
    gain = gain_ref[...]
    decays = jnp.exp(-frate_ref[...])
    srate = srate_ref[...]
    retain = jnp.exp(-srate)
    keep = 1.0 - retain * decays
    eye_f = jnp.where(eye, 1.0, 0.0).astype(F32)
    decay_col = jnp.sum(jnp.where(eye, decays, 0.0), axis=1, keepdims=True)
    for h in range(sets):
        copy1(0, h).wait_recv()

    maps = []
    for h in range(sets):
        total = acc[0, h] + recv1[0, h]
        for k in range(1, ys):
            copy2(k, h).wait_recv()
            total = total + recv2[k, h]
        fresh = [
            jnp.concatenate([decay_col * (eye_f - gain * inform), gain * scores], axis=0)
            for inform, scores in unpack(total)
        ]
        if together_h == 2:
            fresh[1] = compose(fresh[0], fresh[1], factors)
        if maps:
            fresh = [compose(maps[-1], item, factors) for item in fresh]
        maps += fresh
    dmap[0] = maps[-1]

    def dcopy(part):
        return pltpu.make_async_remote_copy(
            dmap.at[part], drecv.at[part], ds.at[part], dr.at[part],
            device_id=(tm, y * 2 + (1 - core)), device_id_type=MESH,
        )

    dcopy(0).start()
    adds = keep * maps[0]
    for h in range(1, hours):
        adds = adds + keep * jnp.exp(-float(h) * srate) * maps[h]
    dmap[1] = adds
    dcopy(1).start()
    for h in range(hours):
        cum[:, h * factors : (h + 1) * factors] = maps[h]
    dcopy(0).wait_recv()
    mine, other = dmap[0], drecv[0]
    leads = core == 0
    whole = compose(jnp.where(leads, mine, other), jnp.where(leads, other, mine), factors)
    esend[...] = whole

    def slot_peer(slot):
        return pair * 2 + (a + slot // ys) % 2, lax.rem(y + slot % ys, ys) * 2 + core

    def slot_of(at):
        return ((a + 2 - at // ys) % 2) * ys + lax.rem(y + ys - at % ys, ys)

    def ecopy(slot):
        return pltpu.make_async_remote_copy(
            esend, emaps.at[slot], es.at[slot], er.at[slot],
            device_id=slot_peer(slot), device_id_type=MESH,
        )

    bcopy = pltpu.make_async_remote_copy(
        esend.at[pl.ds(factors, 1)], bin_s, bs, br,
        device_id=(1, (ys - 1) * 2 + core), device_id_type=MESH,
    )
    heads = (pair == 0) & (g == 0)

    @pl.when(heads)
    def _():
        bcopy.start()

    slots = [ys] + [slot for slot in range(1, chips) if slot != ys]
    for slot in slots:
        ecopy(slot).start()
    emaps[0] = whole
    first = jnp.where(leads, mine, other)
    dcopy(1).wait_recv()
    mine_adds, other_adds = dmap[1], drecv[1]
    chip_adds = jnp.where(leads, mine_adds, other_adds) + jnp.exp(-float(hours) * srate) * compose(
        first, jnp.where(leads, other_adds, mine_adds), factors
    )
    ssend[...] = chip_adds

    def scopy(slot):
        return pltpu.make_async_remote_copy(
            ssend, smaps.at[slot], ss.at[slot], sr.at[slot],
            device_id=slot_peer(slot), device_id_type=MESH,
        )

    for slot in slots:
        scopy(slot).start()
    smaps[0] = chip_adds
    span = 2 * local
    after = (a + 1) * local
    hour_at = (
        lax.broadcasted_iota(jnp.int32, (plane, hours, factors), 0) * hours
        + lax.broadcasted_iota(jnp.int32, (plane, hours, factors), 1)
    )
    far = (hour_at - after).astype(F32)
    tail_w = jnp.where(far >= 0.0, keep[None] * jnp.exp(-jnp.maximum(far, 0.0) * srate[None]), 0.0)
    end_w = jnp.exp(-(span - after).astype(F32) * srate)
    span_w = jnp.exp(-float(span) * srate)
    def vcopy(far):
        return pltpu.make_async_remote_copy(
            vout, vin, vs.at[far - 1], vr,
            device_id=(lax.rem(tm + 2 * far, tms), ser), device_id_type=MESH,
        )

    def vstart(to):
        return pltpu.make_async_remote_copy(
            vout, vin, vls.at[to], vr,
            device_id=(2 + to // ys, (to % ys) * 2 + core), device_id_type=MESH,
        )

    def carry(vector, matrix, shift):
        column = jnp.sum(jnp.where(eye, vector, 0.0), axis=1, keepdims=True)
        return jnp.sum(column * matrix, axis=0, keepdims=True) + shift

    for slot in slots[:-1]:
        ecopy(slot).wait_recv()

    @pl.when(leader)
    def _():
        bcopy.wait_recv()
        state = bin_s[...]
        for at in range(1, chips):
            step = emaps[slot_of(at)]
            state = carry(state, step[:factors], step[factors : factors + 1])
        vout[...] = state
        if pairs > 1:
            for to in range(chips - 1, -1, -1):
                vstart(to).start()

    ecopy(slots[-1]).wait_recv()
    parts = [emaps[slot_of(at)] for at in range(chips)]
    level = parts
    while len(level) > 1:
        level = [
            compose(level[i], level[i + 1], factors) if i + 1 < len(level) else level[i]
            for i in range(0, len(level), 2)
        ]
    total = level[0]

    tcopy = pltpu.make_async_remote_copy(
        tsend, trecv, ts, tr, device_id=(lax.rem(tm + 2, tms), ser), device_id_type=MESH
    )
    odd = pair % 2 == 1
    hands_map = (pair % 2 == 0) & (pair > 0) & (pair < pairs - 1)

    @pl.when(hands_map)
    def _():
        tsend[...] = total
        tcopy.start()

    @pl.when(pair == 0)
    def _():
        vcur[...] = jnp.zeros_like(vcur)

    def forward():
        vcopy(1).wait_recv()
        vcur[...] = vin[...]

        @pl.when(odd & (pair > 1))
        def _():
            tcopy.wait_recv()
            vcur[...] = carry(vin[...], trecv[0:factors], trecv[factors : factors + 1])

        @pl.when(odd & (pair < pairs - 1))
        def _():
            vout[...] = carry(vcur[...], total[:factors], total[factors : factors + 1])
            vcopy(1).start()

            @pl.when(pair < pairs - 2)
            def _():
                vcopy(2).start()

    @pl.when(pair == 1)
    def _():
        forward()

    unit = jnp.concatenate([eye_f, jnp.zeros((8, factors), F32)], axis=0)
    start_map = unit
    before_chip = [parts[0]]
    for at in range(1, chips):
        start_map = jnp.where(g == at, before_chip[-1], start_map)
        if at + 1 < chips:
            before_chip.append(compose(before_chip[-1], parts[at], factors))
    start_map = jnp.where(leads, start_map, compose(start_map, other, factors))
    cums = cum[...]
    lead = dot3(start_map, cums[:factors])
    wide_at = hours * factors
    lead_s[:, :wide_at] = halves(lead[:factors])
    lead_b = lead[factors:] + cums[factors:]
    at_end = pair == pairs - 1
    for k in range(1, chips):
        scopy(k).wait_recv()
    group_adds = smaps[slot_of(0)] + jnp.where(at_end, span_w * decays, 0.0) * total
    for at in range(1, chips):
        group_adds = group_adds + jnp.exp(-float(2 * hours * at) * srate) * compose(
            before_chip[at - 1], smaps[slot_of(at)], factors
        )
    lead_s[:, wide_at:] = halves(group_adds[:factors])
    lead_b = jnp.concatenate([lead_b, group_adds[factors:]], axis=1)

    @pl.when(pair > 1)
    def _():
        forward()

    current = jnp.broadcast_to(vcur[...], (8, factors))
    filtered = dot_halves(current, lead_s[...]) + lead_b
    for h in range(hours):
        row = filtered[0:1, h * factors : (h + 1) * factors]
        fown[h : h + 1, :] = row
    shown[...] = filtered[:, hours * factors :]

    def ccopy(to, of):
        return pltpu.make_async_remote_copy(
            shown, shifts.at[of], cs.at[to], cr.at[of],
            device_id=(to * 2 + a, ser), device_id_type=MESH,
        )

    @pl.loop(0, pair)
    def _(to):
        ccopy(to, pair).start()

    fall[place_in] = fown[...]

    def fcopy(k):
        return pltpu.make_async_remote_copy(
            fown, fall.at[place_in], fs.at[k], fr.at[k],
            device_id=plane_peer(k), device_id_type=MESH,
        )

    for k in range(1, plane):
        fcopy(k).start()
    prec_root = jnp.sqrt(prec_ref[...])
    for k in range(1, plane):
        fcopy(k).wait_recv()
    together = fall[...]
    ending = decays * together[plane - 1][hours - 1 : hours]
    follow = jnp.sum(jnp.sum(together * tail_w, axis=0), axis=0, keepdims=True)

    def gather(of, held):
        total, weight = held
        ccopy(pair, of).wait_recv()
        return total + weight * shifts[of][0:1], weight * span_w

    beyond, _ = lax.fori_loop(
        pair + 1, pairs, gather, (jnp.where(at_end, ending, 0.0), jnp.ones_like(span_w))
    )
    follow = follow + end_w * beyond
    for s in range(sers - 1, -1, -1):
        block = fall[a * sers + s]
        for h in range(hours - 1, -1, -1):
            follow = keep * block[h : h + 1] + retain * follow
            smoothed_ref[s * hours + h : s * hours + h + 1, :] = follow

    fitted = jnp.dot(smoothed_ref[...].astype(BF16), lt_s[...], preferred_element_type=F32)
    standard = (readings_ref[...].astype(F32) - fitted) * prec_root
    probab = 0.5 * (1.0 + lax.erf(standard * 0.7071067811865476))
    spot = jnp.where(present_ref[...] > 0, probab * BINS - 0.5, -4.0)
    for b in range(BINS):
        table[b : b + 1, :] = jnp.sum(
            jnp.maximum(0.0, 1.0 - jnp.abs(spot - b)), axis=0, keepdims=True
        )
    padded = table.shape[0]
    if padded > BINS:
        table[BINS:, :] = jnp.zeros_like(table[BINS:, :])
    th, tl = split2(table[...])
    tally = jnp.dot(
        jnp.concatenate([th, tl], axis=0), mem_s[...], preferred_element_type=F32
    )
    tally = tally[:padded] + tally[padded:]
    lane = lax.broadcasted_iota(jnp.int32, tally.shape, 1) // GROUPS
    sub = lax.broadcasted_iota(jnp.int32, tally.shape, 0) % 8
    tally = jnp.where(lane == sub, tally, 0.0).reshape(padded // 8, 8, tally.shape[1])
    hown[...] = jnp.sum(tally, axis=1)
    hall[me] = hown[...]

    def hsend(k):
        at = lax.rem(place_in + (plane - 1 - k % plane), plane)
        to = lax.rem(pair + (pairs - 1 - k // plane), pairs)
        pltpu.make_async_remote_copy(
            hown, hall.at[me], hs, hr,
            device_id=(to * 2 + at // sers, lax.rem(at, sers)), device_id_type=MESH,
        ).start()

    if n <= 64:
        for k in range(n - 1):
            hsend(k)
    else:
        pl.loop(0, n - 1)(hsend)

    for k in range(ys):
        for h in range(sets):
            copy1(k, h).wait_send()
            if k:
                copy2(k, h).wait_send()
    dcopy(0).wait_send()
    dcopy(1).wait_send()
    for k in range(1, chips):
        ecopy(k).wait_send()
        scopy(k).wait_send()

    @pl.when(odd & (pair < pairs - 1))
    def _():
        vcopy(1).wait_send()

    @pl.when(heads)
    def _():
        bcopy.wait_send()

    if pairs > 1:

        @pl.when(leader)
        def _():
            for to in range(chips):
                vstart(to).wait_send()

    @pl.when(odd & (pair < pairs - 2))
    def _():
        vcopy(2).wait_send()

    @pl.when(hands_map)
    def _():
        tcopy.wait_send()

    for k in range(1, plane):
        fcopy(k).wait_send()

    @pl.loop(0, pair)
    def _(to):
        ccopy(to, pair).wait_send()

    hdrain = pltpu.make_async_remote_copy(
        hall.at[pl.ds(0, n - 1)], hall.at[pl.ds(0, n - 1)], hs, hr,
        device_id=(tm, lax.rem(ser + 1, sers)), device_id_type=MESH,
    )
    hdrain.wait_recv()
    hdrain.wait_send()
    hist_ref[...] = jnp.sum(hall[...], axis=0)


def solution(mesh):
    tms, sers = mesh.shape["tm"], mesh.shape["series"]

    def body(readings, present, loadings, prec, gain, frate, srate, regions):
        local, series = readings.shape
        factors = loadings.shape[1]
        hours = local // sers
        n, ys = tms * sers, sers // 2
        chips = 2 * ys
        rows = factors + 8
        padded = -(-BINS // 8) * 8
        together = 2 if hours % 2 == 0 else 1
        sets, packed_rows = hours // together, factors + 8
        vm = pltpu.VMEM
        dma = pltpu.SemaphoreType.DMA
        smoothed, packed = pl.pallas_call(
            functools.partial(kernel, tms, sers),
            out_shape=(
                vm((local, factors), F32),
                vm((padded // 8, 8 * GROUPS), F32),
            ),
            in_specs=[pl.BlockSpec(memory_space=pl.ANY)] * 8,
            out_specs=(pl.BlockSpec(memory_space=vm),) * 2,
            scratch_shapes=[
                vm((local, series), readings.dtype),
                vm((local, series), present.dtype),
                vm((series, factors), loadings.dtype),
                vm((1, series), F32),
                vm((1, factors), F32),
                vm((1, factors), F32),
                vm((1, factors), F32),
                vm((1, series), regions.dtype),
                vm((factors, series), BF16),
                vm((series, factors), BF16),
                vm((series, 8 * GROUPS), BF16),
                vm((local + 8, factors), F32),
                vm((ys, sets, packed_rows, factors), F32),
                vm((ys, sets, packed_rows, factors), F32),
                vm((ys, sets, packed_rows, factors), F32),
                vm((ys, sets, packed_rows, factors), F32),
                vm((rows, hours * factors), F32),
                vm((2, rows, factors), F32),
                vm((2, rows, factors), F32),
                vm((chips, rows, factors), F32),
                vm((rows, factors), F32),
                vm((chips, rows, factors), F32),
                vm((rows, factors), F32),
                vm((2 * factors, (hours + 1) * factors), BF16),
                vm((1, factors), F32),
                vm((1, factors), F32),
                vm((1, factors), F32),
                vm((1, factors), F32),
                vm((rows, factors), F32),
                vm((rows, factors), F32),
                vm((hours, factors), F32),
                vm((2 * sers, hours, factors), F32),
                vm((8, factors), F32),
                vm((tms // 2, 8, factors), F32),
                vm((padded, series), F32),
                vm((padded // 8, 8 * GROUPS), F32),
                vm((n, padded // 8, 8 * GROUPS), F32),
                dma((8,)),
                dma((ys, sets)),
                dma((ys, sets)),
                dma((ys, sets)),
                dma((ys, sets)),
                dma((2,)),
                dma((2,)),
                dma((chips,)),
                dma((chips,)),
                dma((chips,)),
                dma((chips,)),
                dma((2,)), dma, dma((chips,)), dma, dma, dma, dma,
                dma((2 * sers,)),
                dma((2 * sers,)),
                dma((tms // 2,)),
                dma((tms // 2,)),
                dma, dma,
            ],
            compiler_params=pltpu.CompilerParams(collective_id=0, has_side_effects=True),
        )(
            readings, present, loadings, prec.reshape(1, -1), gain.reshape(1, -1),
            frate.reshape(1, -1), srate.reshape(1, -1), regions.reshape(1, -1),
        )
        scale = BINS * GROUPS / (local * tms * series * sers)
        histogram = packed.reshape(-1, GROUPS)[:BINS].T * scale
        return smoothed, histogram

    in_specs = (
        P("tm", "series"), P("tm", "series"), P("series", None), P("series"),
        P(), P(), P(), P("series"),
    )
    return jax.shard_map(
        body, mesh=mesh, in_specs=in_specs, out_specs=(P("tm", None), P()), check_vma=False
    )
```

```python
import functools

import jax
import jax.numpy as jnp
from jax import lax
from jax.experimental import pallas as pl
from jax.experimental.pallas import tpu as pltpu
from jax.sharding import PartitionSpec as P

BINS = 20
GROUPS = 16
MESH = pl.DeviceIdType.MESH
F32 = jnp.float32
BF16 = jnp.bfloat16


def split2(x):
    high = x.astype(BF16)
    return high, (x - high.astype(F32)).astype(BF16)


def halves(right):
    high, low = split2(right)
    return jnp.concatenate([high, low], axis=0)


def dot_halves(left, right):
    high, low = split2(left)
    both = jnp.concatenate(
        [
            jnp.concatenate([high, high], axis=1),
            jnp.concatenate([low, jnp.zeros_like(low)], axis=1),
        ],
        axis=0,
    )
    out = jnp.dot(both, right, preferred_element_type=F32)
    return out[: left.shape[0]] + out[left.shape[0] :]


def dot_t(left, right):
    return lax.dot_general(left, right, (((1,), (1,)), ((), ())), preferred_element_type=F32)


def dot3(left, right):
    return dot_halves(left, halves(right))


def compose(earlier, later, factors):
    out = dot3(earlier, later[:factors])
    return jnp.concatenate([out[:factors], out[factors:] + later[factors:]], axis=0)


def kernel(
    tms, sers,
    readings_in, present_in, loadings_in, prec_in, gain_in, frate_in, srate_in, regions_in,
    smoothed_ref, hist_ref,
    readings_ref, present_ref, loadings_ref, prec_ref, gain_ref, frate_ref, srate_ref, regions_ref,
    lt_s, sl_s, mem_s, score_s, send1, recv1, acc, recv2, cum, dmap, drecv, emaps, esend, smaps, ssend, lead_s,
    vin, vout, vcur, bin_s, tsend, trecv, fown, fall, shown, shifts, table, hown, hall,
    ins, s1s, s1r, s2s, s2r, ds, dr, es, er, ss, sr, vs, vr, vls, bs, br, ts, tr, fs, fr, cs, cr, hs, hr,
):
    tm, ser = lax.axis_index("tm"), lax.axis_index("series")
    y, core = ser // 2, ser % 2
    ys = sers // 2
    local = readings_ref.shape[0]
    factors = loadings_ref.shape[1]
    rows = factors + 8
    hours = local // sers
    n = tms * sers
    me = tm * sers + ser
    pair, a = tm // 2, tm % 2
    pairs = tms // 2
    chips = 2 * ys
    g = a * ys + y
    leader = (pair == 0) & (g == chips - 1)

    inputs = [
        pltpu.make_async_copy(src, dst, ins.at[i])
        for i, (src, dst) in enumerate(
            [
                (loadings_in, loadings_ref), (prec_in, prec_ref), (present_in, present_ref),
                (readings_in, readings_ref), (gain_in, gain_ref), (frate_in, frate_ref),
                (srate_in, srate_ref), (regions_in, regions_ref),
            ]
        )
    ]
    for item in inputs:
        item.start()

    barrier = pltpu.get_barrier_semaphore()

    plane = 2 * sers
    place_in = a * sers + ser

    def plane_peer(k):
        at = lax.rem(place_in + k, plane)
        return pair * 2 + at // sers, lax.rem(at, sers)

    for k in range(1, plane):
        pl.semaphore_signal(barrier, inc=1, device_id=plane_peer(k), device_id_type=MESH)
    @pl.when(pair > 0)
    def _():
        pl.semaphore_signal(barrier, inc=1, device_id=(tm - 2, ser), device_id_type=MESH)

    @pl.when(pair < pairs - 1)
    def _():
        pl.semaphore_signal(barrier, inc=1, device_id=(tm + 2, ser), device_id_type=MESH)

    @pl.when(pair > 1)
    def _():
        pl.semaphore_signal(barrier, inc=1, device_id=(tm - 4, ser), device_id_type=MESH)

    @pl.when(pair < pairs - 2)
    def _():
        pl.semaphore_signal(barrier, inc=1, device_id=(tm + 4, ser), device_id_type=MESH)

    @pl.when((pair == 1) & (g < chips - 1))
    def _():
        pl.semaphore_signal(
            barrier, inc=1, device_id=(1, (ys - 1) * 2 + core), device_id_type=MESH
        )

    for item in inputs[:2]:
        item.wait()

    ltf = loadings_ref[...].astype(F32).T
    lt_s[...] = ltf.astype(BF16)
    sl_s[...] = (ltf * prec_ref[...]).astype(BF16)
    for item in inputs[2:4]:
        item.wait()
    present = present_ref[...].astype(F32)
    read_f = readings_ref[...].astype(F32)
    score_s[0:local] = dot_t((read_f * present).astype(BF16), sl_s[...])
    score_s[local:] = jnp.zeros_like(score_s[local:])

    together_h = 2 if hours % 2 == 0 else 1
    sets = hours // together_h
    sub = lax.broadcasted_iota(jnp.int32, (factors, factors), 0)
    lane = lax.broadcasted_iota(jnp.int32, (factors, factors), 1)
    eye = sub == lane
    upper = lane > sub
    line = lax.broadcasted_iota(jnp.int32, (8, factors), 0)

    def hour_terms(base, dst, held):
        rights = []
        for j in range(len(held) * together_h):
            mask = present_ref[pl.ds(base + j, 1), :].astype(F32)
            mask = jnp.broadcast_to(mask, (16, mask.shape[1])).astype(BF16)
            right = sl_s[...].reshape(factors // 16, 16, mask.shape[1]) * mask[None]
            rights.append(right.reshape(factors, mask.shape[1]))
        out = dot_t(lt_s[...], jnp.concatenate(rights, axis=0))
        for place, h in enumerate(held):
            at = place * together_h
            first = out[:, at * factors : (at + 1) * factors]
            tail = jnp.zeros((8, factors), F32)
            if together_h == 2:
                second = out[:, (at + 1) * factors : (at + 2) * factors]
                dst[h, :factors] = jnp.where(upper, first, second)
                corner = jnp.sum(jnp.where(eye, first, 0.0), axis=0, keepdims=True)
                tail = jnp.where(line == together_h, corner, tail)
            else:
                dst[h, :factors] = first
            for j in range(together_h):
                row = jnp.broadcast_to(score_s[pl.ds(base + at + j, 1), :], (8, factors))
                tail = jnp.where(line == j, row, tail)
            dst[h, factors:] = tail

    def unpack(packed):
        block, tail = packed[:factors], packed[factors:]
        if together_h == 1:
            matrices = [block]
        else:
            turned = block.T
            matrices = [
                jnp.where(eye, tail[together_h : together_h + 1], jnp.where(upper, block, turned)),
                jnp.where(upper, turned, block),
            ]
        return [
            (matrices[j], jnp.where(line == 0, tail[j : j + 1], 0.0)) for j in range(together_h)
        ]

    def copy1(k, h):
        return pltpu.make_async_remote_copy(
            send1.at[k, h], recv1.at[k, h], s1s.at[k, h], s1r.at[k, h],
            device_id=(tm, y * 2 + (1 - core)), device_id_type=MESH,
        )

    def copy2(k, h):
        return pltpu.make_async_remote_copy(
            acc.at[k, h], recv2.at[k, h], s2s.at[k, h], s2r.at[k, h],
            device_id=(tm, lax.rem(y + k, ys) * 2 + core), device_id_type=MESH,
        )

    order = list(range(1, ys)) + [0]
    for place, k in enumerate(order):
        owner = lax.rem(y + k, ys) * 2
        theirs, ours = (owner + (1 - core)) * hours, (owner + core) * hours
        groups = [[h] for h in range(sets)] if k else [list(range(sets))]
        for held in groups:
            hour_terms(theirs + held[0] * together_h, send1.at[k], held)
            if place == 0 and held[0] == 0:
                before = jnp.where(pair > 0, 1, 0) + jnp.where(pair > 1, 1, 0)
                behind = jnp.where(pair < pairs - 1, 1, 0) + jnp.where(pair < pairs - 2, 1, 0)
                extra = jnp.where(leader, chips - 1, 0)
                pl.semaphore_wait(barrier, plane - 1 + before + behind + extra)
            for h in held:
                copy1(k, h).start()
        for held in groups:
            hour_terms(ours + held[0] * together_h, acc.at[k], held)
            for h in held if k else []:
                copy1(k, h).wait_recv()
                acc[k, h] = acc[k, h] + recv1[k, h]
                copy2(k, h).start()

    for item in inputs[4:]:
        item.wait()
    wide = lax.broadcasted_iota(jnp.int32, (factors, regions_ref.shape[1]), 0) % GROUPS
    mem_s[...] = jnp.where(wide == regions_ref[...], 1.0, 0.0).astype(F32).T.astype(BF16)
    gain = gain_ref[...]
    decays = jnp.exp(-frate_ref[...])
    srate = srate_ref[...]
    retain = jnp.exp(-srate)
    keep = 1.0 - retain * decays
    eye_f = jnp.where(eye, 1.0, 0.0).astype(F32)
    decay_col = jnp.sum(jnp.where(eye, decays, 0.0), axis=1, keepdims=True)
    for h in range(sets):
        copy1(0, h).wait_recv()

    maps = []
    for h in range(sets):
        total = acc[0, h] + recv1[0, h]
        for k in range(1, ys):
            copy2(k, h).wait_recv()
            total = total + recv2[k, h]
        fresh = [
            jnp.concatenate([decay_col * (eye_f - gain * inform), gain * scores], axis=0)
            for inform, scores in unpack(total)
        ]
        if together_h == 2:
            fresh[1] = compose(fresh[0], fresh[1], factors)
        if maps:
            fresh = [compose(maps[-1], item, factors) for item in fresh]
        maps += fresh
    dmap[0] = maps[-1]

    def dcopy(part):
        return pltpu.make_async_remote_copy(
            dmap.at[part], drecv.at[part], ds.at[part], dr.at[part],
            device_id=(tm, y * 2 + (1 - core)), device_id_type=MESH,
        )

    dcopy(0).start()
    adds = keep * maps[0]
    for h in range(1, hours):
        adds = adds + keep * jnp.exp(-float(h) * srate) * maps[h]
    dmap[1] = adds
    dcopy(1).start()
    for h in range(hours):
        cum[:, h * factors : (h + 1) * factors] = maps[h]
    dcopy(0).wait_recv()
    mine, other = dmap[0], drecv[0]
    leads = core == 0
    whole = compose(jnp.where(leads, mine, other), jnp.where(leads, other, mine), factors)
    esend[...] = whole

    def slot_peer(slot):
        return pair * 2 + (a + slot // ys) % 2, lax.rem(y + slot % ys, ys) * 2 + core

    def slot_of(at):
        return ((a + 2 - at // ys) % 2) * ys + lax.rem(y + ys - at % ys, ys)

    def ecopy(slot):
        return pltpu.make_async_remote_copy(
            esend, emaps.at[slot], es.at[slot], er.at[slot],
            device_id=slot_peer(slot), device_id_type=MESH,
        )

    bcopy = pltpu.make_async_remote_copy(
        esend.at[pl.ds(factors, 1)], bin_s, bs, br,
        device_id=(1, (ys - 1) * 2 + core), device_id_type=MESH,
    )
    heads = (pair == 0) & (g == 0)

    @pl.when(heads)
    def _():
        bcopy.start()

    slots = [ys] + [slot for slot in range(1, chips) if slot != ys]
    for slot in slots:
        ecopy(slot).start()
    emaps[0] = whole
    first = jnp.where(leads, mine, other)
    dcopy(1).wait_recv()
    mine_adds, other_adds = dmap[1], drecv[1]
    chip_adds = jnp.where(leads, mine_adds, other_adds) + jnp.exp(-float(hours) * srate) * compose(
        first, jnp.where(leads, other_adds, mine_adds), factors
    )
    ssend[...] = chip_adds

    def scopy(slot):
        return pltpu.make_async_remote_copy(
            ssend, smaps.at[slot], ss.at[slot], sr.at[slot],
            device_id=slot_peer(slot), device_id_type=MESH,
        )

    for slot in slots:
        scopy(slot).start()
    smaps[0] = chip_adds
    span = 2 * local
    after = (a + 1) * local
    hour_at = (
        lax.broadcasted_iota(jnp.int32, (plane, hours, factors), 0) * hours
        + lax.broadcasted_iota(jnp.int32, (plane, hours, factors), 1)
    )
    far = (hour_at - after).astype(F32)
    tail_w = jnp.where(far >= 0.0, keep[None] * jnp.exp(-jnp.maximum(far, 0.0) * srate[None]), 0.0)
    end_w = jnp.exp(-(span - after).astype(F32) * srate)
    span_w = jnp.exp(-float(span) * srate)
    def vcopy(far):
        return pltpu.make_async_remote_copy(
            vout, vin, vs.at[far - 1], vr,
            device_id=(lax.rem(tm + 2 * far, tms), ser), device_id_type=MESH,
        )

    def vstart(to):
        return pltpu.make_async_remote_copy(
            vout, vin, vls.at[to], vr,
            device_id=(2 + to // ys, (to % ys) * 2 + core), device_id_type=MESH,
        )

    def carry(vector, matrix, shift):
        column = jnp.sum(jnp.where(eye, vector, 0.0), axis=1, keepdims=True)
        return jnp.sum(column * matrix, axis=0, keepdims=True) + shift

    for slot in slots[:-1]:
        ecopy(slot).wait_recv()

    @pl.when(leader)
    def _():
        bcopy.wait_recv()
        state = bin_s[...]
        for at in range(1, chips):
            step = emaps[slot_of(at)]
            state = carry(state, step[:factors], step[factors : factors + 1])
        vout[...] = state
        if pairs > 1:
            for to in range(chips - 1, -1, -1):
                vstart(to).start()

    ecopy(slots[-1]).wait_recv()
    parts = [emaps[slot_of(at)] for at in range(chips)]
    level = parts
    while len(level) > 1:
        level = [
            compose(level[i], level[i + 1], factors) if i + 1 < len(level) else level[i]
            for i in range(0, len(level), 2)
        ]
    total = level[0]

    tcopy = pltpu.make_async_remote_copy(
        tsend, trecv, ts, tr, device_id=(lax.rem(tm + 2, tms), ser), device_id_type=MESH
    )
    odd = pair % 2 == 1
    hands_map = (pair % 2 == 0) & (pair > 0) & (pair < pairs - 1)

    @pl.when(hands_map)
    def _():
        tsend[...] = total
        tcopy.start()

    @pl.when(pair == 0)
    def _():
        vcur[...] = jnp.zeros_like(vcur)

    def forward():
        vcopy(1).wait_recv()
        vcur[...] = vin[...]

        @pl.when(odd & (pair > 1))
        def _():
            tcopy.wait_recv()
            vcur[...] = carry(vin[...], trecv[0:factors], trecv[factors : factors + 1])

        @pl.when(odd & (pair < pairs - 1))
        def _():
            vout[...] = carry(vcur[...], total[:factors], total[factors : factors + 1])
            vcopy(1).start()

            @pl.when(pair < pairs - 2)
            def _():
                vcopy(2).start()

    @pl.when(pair == 1)
    def _():
        forward()

    unit = jnp.concatenate([eye_f, jnp.zeros((8, factors), F32)], axis=0)
    start_map = unit
    before_chip = [parts[0]]
    for at in range(1, chips):
        start_map = jnp.where(g == at, before_chip[-1], start_map)
        if at + 1 < chips:
            before_chip.append(compose(before_chip[-1], parts[at], factors))
    start_map = jnp.where(leads, start_map, compose(start_map, other, factors))
    cums = cum[...]
    lead = dot3(start_map, cums[:factors])
    wide_at = hours * factors
    lead_s[:, :wide_at] = halves(lead[:factors])
    lead_b = lead[factors:] + cums[factors:]
    at_end = pair == pairs - 1
    for k in range(1, chips):
        scopy(k).wait_recv()
    group_adds = smaps[slot_of(0)] + jnp.where(at_end, span_w * decays, 0.0) * total
    for at in range(1, chips):
        group_adds = group_adds + jnp.exp(-float(2 * hours * at) * srate) * compose(
            before_chip[at - 1], smaps[slot_of(at)], factors
        )
    lead_s[:, wide_at:] = halves(group_adds[:factors])
    lead_b = jnp.concatenate([lead_b, group_adds[factors:]], axis=1)

    @pl.when(pair > 1)
    def _():
        forward()

    current = jnp.broadcast_to(vcur[...], (8, factors))
    filtered = dot_halves(current, lead_s[...]) + lead_b
    for h in range(hours):
        row = filtered[0:1, h * factors : (h + 1) * factors]
        fown[h : h + 1, :] = row
    shown[...] = filtered[:, hours * factors :]

    def ccopy(to, of):
        return pltpu.make_async_remote_copy(
            shown, shifts.at[of], cs.at[to], cr.at[of],
            device_id=(to * 2 + a, ser), device_id_type=MESH,
        )

    @pl.loop(0, pair)
    def _(to):
        ccopy(to, pair).start()

    fall[place_in] = fown[...]

    def fcopy(k):
        return pltpu.make_async_remote_copy(
            fown, fall.at[place_in], fs.at[k], fr.at[k],
            device_id=plane_peer(k), device_id_type=MESH,
        )

    for k in range(1, plane):
        fcopy(k).start()
    prec_root = jnp.sqrt(prec_ref[...])
    for k in range(1, plane):
        fcopy(k).wait_recv()
    together = fall[...]
    ending = decays * together[plane - 1][hours - 1 : hours]
    follow = jnp.sum(jnp.sum(together * tail_w, axis=0), axis=0, keepdims=True)

    def gather(of, held):
        total, weight = held
        ccopy(pair, of).wait_recv()
        return total + weight * shifts[of][0:1], weight * span_w

    beyond, _ = lax.fori_loop(
        pair + 1, pairs, gather, (jnp.where(at_end, ending, 0.0), jnp.ones_like(span_w))
    )
    follow = follow + end_w * beyond
    for s in range(sers - 1, -1, -1):
        block = fall[a * sers + s]
        for h in range(hours - 1, -1, -1):
            follow = keep * block[h : h + 1] + retain * follow
            smoothed_ref[s * hours + h : s * hours + h + 1, :] = follow

    fitted = jnp.dot(smoothed_ref[...].astype(BF16), lt_s[...], preferred_element_type=F32)
    standard = (readings_ref[...].astype(F32) - fitted) * prec_root
    probab = 0.5 * (1.0 + lax.erf(standard * 0.7071067811865476))
    spot = jnp.where(present_ref[...] > 0, probab * BINS - 0.5, -4.0)
    for b in range(BINS):
        table[b : b + 1, :] = jnp.sum(
            jnp.maximum(0.0, 1.0 - jnp.abs(spot - b)), axis=0, keepdims=True
        )
    padded = table.shape[0]
    if padded > BINS:
        table[BINS:, :] = jnp.zeros_like(table[BINS:, :])
    th, tl = split2(table[...])
    tally = jnp.dot(
        jnp.concatenate([th, tl], axis=0), mem_s[...], preferred_element_type=F32
    )
    tally = tally[:padded] + tally[padded:]
    lane = lax.broadcasted_iota(jnp.int32, tally.shape, 1) // GROUPS
    sub = lax.broadcasted_iota(jnp.int32, tally.shape, 0) % 8
    tally = jnp.where(lane == sub, tally, 0.0).reshape(padded // 8, 8, tally.shape[1])
    hown[...] = jnp.sum(tally, axis=1)
    hall[me] = hown[...]

    def hsend(k):
        at = lax.rem(place_in + (plane - 1 - k % plane), plane)
        to = lax.rem(pair + (pairs - 1 - k // plane), pairs)
        pltpu.make_async_remote_copy(
            hown, hall.at[me], hs, hr,
            device_id=(to * 2 + at // sers, lax.rem(at, sers)), device_id_type=MESH,
        ).start()

    if n <= 64:
        for k in range(n - 1):
            hsend(k)
    else:
        pl.loop(0, n - 1)(hsend)

    for k in range(ys):
        for h in range(sets):
            copy1(k, h).wait_send()
            if k:
                copy2(k, h).wait_send()
    dcopy(0).wait_send()
    dcopy(1).wait_send()
    for k in range(1, chips):
        ecopy(k).wait_send()
        scopy(k).wait_send()

    @pl.when(odd & (pair < pairs - 1))
    def _():
        vcopy(1).wait_send()

    @pl.when(heads)
    def _():
        bcopy.wait_send()

    if pairs > 1:

        @pl.when(leader)
        def _():
            for to in range(chips):
                vstart(to).wait_send()

    @pl.when(odd & (pair < pairs - 2))
    def _():
        vcopy(2).wait_send()

    @pl.when(hands_map)
    def _():
        tcopy.wait_send()

    for k in range(1, plane):
        fcopy(k).wait_send()

    @pl.loop(0, pair)
    def _(to):
        ccopy(to, pair).wait_send()

    hdrain = pltpu.make_async_remote_copy(
        hall.at[pl.ds(0, n - 1)], hall.at[pl.ds(0, n - 1)], hs, hr,
        device_id=(tm, lax.rem(ser + 1, sers)), device_id_type=MESH,
    )
    hdrain.wait_recv()
    hdrain.wait_send()
    hist_ref[...] = jnp.sum(hall[...], axis=0)


def solution(mesh):
    tms, sers = mesh.shape["tm"], mesh.shape["series"]

    def body(readings, present, loadings, prec, gain, frate, srate, regions):
        local, series = readings.shape
        factors = loadings.shape[1]
        hours = local // sers
        n, ys = tms * sers, sers // 2
        chips = 2 * ys
        rows = factors + 8
        padded = -(-BINS // 8) * 8
        together = 2 if hours % 2 == 0 else 1
        sets, packed_rows = hours // together, factors + 8
        vm = pltpu.VMEM
        dma = pltpu.SemaphoreType.DMA
        smoothed, packed = pl.pallas_call(
            functools.partial(kernel, tms, sers),
            out_shape=(
                vm((local, factors), F32),
                vm((padded // 8, 8 * GROUPS), F32),
            ),
            in_specs=[pl.BlockSpec(memory_space=pl.ANY)] * 8,
            out_specs=(pl.BlockSpec(memory_space=vm),) * 2,
            scratch_shapes=[
                vm((local, series), readings.dtype),
                vm((local, series), present.dtype),
                vm((series, factors), loadings.dtype),
                vm((1, series), F32),
                vm((1, factors), F32),
                vm((1, factors), F32),
                vm((1, factors), F32),
                vm((1, series), regions.dtype),
                vm((factors, series), BF16),
                vm((factors, series), BF16),
                vm((series, 8 * GROUPS), BF16),
                vm((local + 8, factors), F32),
                vm((ys, sets, packed_rows, factors), F32),
                vm((ys, sets, packed_rows, factors), F32),
                vm((ys, sets, packed_rows, factors), F32),
                vm((ys, sets, packed_rows, factors), F32),
                vm((rows, hours * factors), F32),
                vm((2, rows, factors), F32),
                vm((2, rows, factors), F32),
                vm((chips, rows, factors), F32),
                vm((rows, factors), F32),
                vm((chips, rows, factors), F32),
                vm((rows, factors), F32),
                vm((2 * factors, (hours + 1) * factors), BF16),
                vm((1, factors), F32),
                vm((1, factors), F32),
                vm((1, factors), F32),
                vm((1, factors), F32),
                vm((rows, factors), F32),
                vm((rows, factors), F32),
                vm((hours, factors), F32),
                vm((2 * sers, hours, factors), F32),
                vm((8, factors), F32),
                vm((tms // 2, 8, factors), F32),
                vm((padded, series), F32),
                vm((padded // 8, 8 * GROUPS), F32),
                vm((n, padded // 8, 8 * GROUPS), F32),
                dma((8,)),
                dma((ys, sets)),
                dma((ys, sets)),
                dma((ys, sets)),
                dma((ys, sets)),
                dma((2,)),
                dma((2,)),
                dma((chips,)),
                dma((chips,)),
                dma((chips,)),
                dma((chips,)),
                dma((2,)), dma, dma((chips,)), dma, dma, dma, dma,
                dma((2 * sers,)),
                dma((2 * sers,)),
                dma((tms // 2,)),
                dma((tms // 2,)),
                dma, dma,
            ],
            compiler_params=pltpu.CompilerParams(collective_id=0, has_side_effects=True),
        )(
            readings, present, loadings, prec.reshape(1, -1), gain.reshape(1, -1),
            frate.reshape(1, -1), srate.reshape(1, -1), regions.reshape(1, -1),
        )
        scale = BINS * GROUPS / (local * tms * series * sers)
        histogram = packed.reshape(-1, GROUPS)[:BINS].T * scale
        return smoothed, histogram

    in_specs = (
        P("tm", "series"), P("tm", "series"), P("series", None), P("series"),
        P(), P(), P(), P("series"),
    )
    return jax.shard_map(
        body, mesh=mesh, in_specs=in_specs, out_specs=(P("tm", None), P()), check_vma=False
    )
```

```python
import functools

import jax
import jax.numpy as jnp
from jax import lax
from jax.experimental import pallas as pl
from jax.experimental.pallas import tpu as pltpu
from jax.sharding import PartitionSpec as P

BINS = 20
GROUPS = 16
MESH = pl.DeviceIdType.MESH
F32 = jnp.float32
BF16 = jnp.bfloat16


def split2(x):
    high = x.astype(BF16)
    return high, (x - high.astype(F32)).astype(BF16)


def halves(right):
    high, low = split2(right)
    return jnp.concatenate([high, low], axis=0)


def dot_halves(left, right):
    high, low = split2(left)
    both = jnp.concatenate(
        [
            jnp.concatenate([high, high], axis=1),
            jnp.concatenate([low, jnp.zeros_like(low)], axis=1),
        ],
        axis=0,
    )
    out = jnp.dot(both, right, preferred_element_type=F32)
    return out[: left.shape[0]] + out[left.shape[0] :]


def dot_t(left, right):
    return lax.dot_general(left, right, (((1,), (1,)), ((), ())), preferred_element_type=F32)


def dot3(left, right):
    return dot_halves(left, halves(right))


def compose(earlier, later, factors):
    out = dot3(earlier, later[:factors])
    return jnp.concatenate([out[:factors], out[factors:] + later[factors:]], axis=0)


LINES = -(-BINS // 8)


def bin_row(b):
    return b % LINES * 8 + b // LINES


def finish(scale, rows_ref, packed_ref, smoothed_ref, hist_ref, held, sems):
    rows_out = pltpu.make_async_copy(rows_ref, smoothed_ref, sems.at[0])
    rows_out.start()
    packed = packed_ref[...] * scale
    tall = jnp.concatenate(
        [packed, jnp.zeros((packed.shape[1] - LINES, packed.shape[1]), F32)], axis=0
    ).T
    total = tall[:GROUPS]
    for j in range(1, 8):
        total = total + pltpu.roll(tall[j * GROUPS : (j + 1) * GROUPS], LINES * j, 1)
    held[...] = total[:, :BINS]
    hist_out = pltpu.make_async_copy(held, hist_ref, sems.at[1])
    hist_out.start()
    rows_out.wait()
    hist_out.wait()


def kernel(
    tms, sers,
    readings_in, present_in, loadings_in, prec_in, gain_in, frate_in, srate_in, regions_in,
    smoothed_ref, hist_ref,
    readings_ref, present_ref, loadings_ref, prec_ref, gain_ref, frate_ref, srate_ref, regions_ref,
    lt_s, sl_s, mem_s, score_s, send1, recv1, acc, recv2, cum, dmap, drecv, emaps, esend, smaps, ssend, lead_s,
    vin, vout, vcur, bin_s, tsend, trecv, fown, fall, shown, shifts, table, hown, hall,
    ins, s1s, s1r, s2s, s2r, ds, dr, es, er, ss, sr, vs, vr, vls, bs, br, ts, tr, fs, fr, cs, cr, hs, hr,
):
    tm, ser = lax.axis_index("tm"), lax.axis_index("series")
    y, core = ser // 2, ser % 2
    ys = sers // 2
    local = readings_ref.shape[0]
    factors = loadings_ref.shape[1]
    rows = factors + 8
    hours = local // sers
    n = tms * sers
    me = tm * sers + ser
    pair, a = tm // 2, tm % 2
    pairs = tms // 2
    chips = 2 * ys
    g = a * ys + y
    leader = (pair == 0) & (g == chips - 1)

    inputs = [
        pltpu.make_async_copy(src, dst, ins.at[i])
        for i, (src, dst) in enumerate(
            [
                (loadings_in, loadings_ref), (prec_in, prec_ref), (present_in, present_ref),
                (readings_in, readings_ref), (gain_in, gain_ref), (frate_in, frate_ref),
                (srate_in, srate_ref), (regions_in, regions_ref),
            ]
        )
    ]
    for item in inputs:
        item.start()

    barrier = pltpu.get_barrier_semaphore()

    plane = 2 * sers
    place_in = a * sers + ser

    def plane_peer(k):
        at = lax.rem(place_in + k, plane)
        return pair * 2 + at // sers, lax.rem(at, sers)

    for k in range(1, plane):
        pl.semaphore_signal(barrier, inc=1, device_id=plane_peer(k), device_id_type=MESH)
    @pl.when(pair > 0)
    def _():
        pl.semaphore_signal(barrier, inc=1, device_id=(tm - 2, ser), device_id_type=MESH)

    @pl.when(pair < pairs - 1)
    def _():
        pl.semaphore_signal(barrier, inc=1, device_id=(tm + 2, ser), device_id_type=MESH)

    @pl.when(pair > 1)
    def _():
        pl.semaphore_signal(barrier, inc=1, device_id=(tm - 4, ser), device_id_type=MESH)

    @pl.when(pair < pairs - 2)
    def _():
        pl.semaphore_signal(barrier, inc=1, device_id=(tm + 4, ser), device_id_type=MESH)

    @pl.when((pair == 1) & (g < chips - 1))
    def _():
        pl.semaphore_signal(
            barrier, inc=1, device_id=(1, (ys - 1) * 2 + core), device_id_type=MESH
        )

    for item in inputs[:2]:
        item.wait()

    ltf = loadings_ref[...].astype(F32).T
    lt_s[...] = ltf.astype(BF16)
    sl_s[...] = (ltf * prec_ref[...]).astype(BF16)
    for item in inputs[2:4]:
        item.wait()
    present = present_ref[...].astype(F32)
    read_f = readings_ref[...].astype(F32)
    score_s[0:local] = dot_t((read_f * present).astype(BF16), sl_s[...])
    score_s[local:] = jnp.zeros_like(score_s[local:])

    together_h = 2 if hours % 2 == 0 else 1
    sets = hours // together_h
    sub = lax.broadcasted_iota(jnp.int32, (factors, factors), 0)
    lane = lax.broadcasted_iota(jnp.int32, (factors, factors), 1)
    eye = sub == lane
    upper = lane > sub
    line = lax.broadcasted_iota(jnp.int32, (8, factors), 0)

    def hour_terms(base, dst, held):
        rights = []
        for j in range(len(held) * together_h):
            mask = present_ref[pl.ds(base + j, 1), :].astype(F32)
            mask = jnp.broadcast_to(mask, (16, mask.shape[1])).astype(BF16)
            right = sl_s[...].reshape(factors // 16, 16, mask.shape[1]) * mask[None]
            rights.append(right.reshape(factors, mask.shape[1]))
        out = dot_t(lt_s[...], jnp.concatenate(rights, axis=0))
        for place, h in enumerate(held):
            at = place * together_h
            first = out[:, at * factors : (at + 1) * factors]
            tail = jnp.zeros((8, factors), F32)
            if together_h == 2:
                second = out[:, (at + 1) * factors : (at + 2) * factors]
                dst[h, :factors] = jnp.where(upper, first, second)
                corner = jnp.sum(jnp.where(eye, first, 0.0), axis=0, keepdims=True)
                tail = jnp.where(line == together_h, corner, tail)
            else:
                dst[h, :factors] = first
            for j in range(together_h):
                row = jnp.broadcast_to(score_s[pl.ds(base + at + j, 1), :], (8, factors))
                tail = jnp.where(line == j, row, tail)
            dst[h, factors:] = tail

    def unpack(packed):
        block, tail = packed[:factors], packed[factors:]
        if together_h == 1:
            matrices = [block]
        else:
            turned = block.T
            matrices = [
                jnp.where(eye, tail[together_h : together_h + 1], jnp.where(upper, block, turned)),
                jnp.where(upper, turned, block),
            ]
        return [
            (matrices[j], jnp.where(line == 0, tail[j : j + 1], 0.0)) for j in range(together_h)
        ]

    def copy1(k, h):
        return pltpu.make_async_remote_copy(
            send1.at[k, h], recv1.at[k, h], s1s.at[k, h], s1r.at[k, h],
            device_id=(tm, y * 2 + (1 - core)), device_id_type=MESH,
        )

    def copy2(k, h):
        return pltpu.make_async_remote_copy(
            acc.at[k, h], recv2.at[k, h], s2s.at[k, h], s2r.at[k, h],
            device_id=(tm, lax.rem(y + k, ys) * 2 + core), device_id_type=MESH,
        )

    order = list(range(1, ys)) + [0]
    for place, k in enumerate(order):
        owner = lax.rem(y + k, ys) * 2
        theirs, ours = (owner + (1 - core)) * hours, (owner + core) * hours
        groups = [[h] for h in range(sets)] if k else [list(range(sets))]
        for held in groups:
            hour_terms(theirs + held[0] * together_h, send1.at[k], held)
            if place == 0 and held[0] == 0:
                before = jnp.where(pair > 0, 1, 0) + jnp.where(pair > 1, 1, 0)
                behind = jnp.where(pair < pairs - 1, 1, 0) + jnp.where(pair < pairs - 2, 1, 0)
                extra = jnp.where(leader, chips - 1, 0)
                pl.semaphore_wait(barrier, plane - 1 + before + behind + extra)
            for h in held:
                copy1(k, h).start()
        for held in groups:
            hour_terms(ours + held[0] * together_h, acc.at[k], held)
            for h in held if k else []:
                copy1(k, h).wait_recv()
                acc[k, h] = acc[k, h] + recv1[k, h]
                copy2(k, h).start()

    for item in inputs[4:]:
        item.wait()
    wide = lax.broadcasted_iota(jnp.int32, (factors, regions_ref.shape[1]), 0) % GROUPS
    mem_s[...] = jnp.where(wide == regions_ref[...], 1.0, 0.0).astype(F32).T.astype(BF16)
    gain = gain_ref[...]
    decays = jnp.exp(-frate_ref[...])
    srate = srate_ref[...]
    retain = jnp.exp(-srate)
    keep = 1.0 - retain * decays
    eye_f = jnp.where(eye, 1.0, 0.0).astype(F32)
    decay_col = jnp.sum(jnp.where(eye, decays, 0.0), axis=1, keepdims=True)
    for h in range(sets):
        copy1(0, h).wait_recv()

    maps = []
    for h in range(sets):
        total = acc[0, h] + recv1[0, h]
        for k in range(1, ys):
            copy2(k, h).wait_recv()
            total = total + recv2[k, h]
        fresh = [
            jnp.concatenate([decay_col * (eye_f - gain * inform), gain * scores], axis=0)
            for inform, scores in unpack(total)
        ]
        if together_h == 2:
            fresh[1] = compose(fresh[0], fresh[1], factors)
        if maps:
            fresh = [compose(maps[-1], item, factors) for item in fresh]
        maps += fresh
    dmap[0] = maps[-1]

    def dcopy(part):
        return pltpu.make_async_remote_copy(
            dmap.at[part], drecv.at[part], ds.at[part], dr.at[part],
            device_id=(tm, y * 2 + (1 - core)), device_id_type=MESH,
        )

    dcopy(0).start()
    adds = keep * maps[0]
    for h in range(1, hours):
        adds = adds + keep * jnp.exp(-float(h) * srate) * maps[h]
    dmap[1] = adds
    dcopy(1).start()
    for h in range(hours):
        cum[:, h * factors : (h + 1) * factors] = maps[h]
    dcopy(0).wait_recv()
    mine, other = dmap[0], drecv[0]
    leads = core == 0
    whole = compose(jnp.where(leads, mine, other), jnp.where(leads, other, mine), factors)
    esend[...] = whole

    def slot_peer(slot):
        return pair * 2 + (a + slot // ys) % 2, lax.rem(y + slot % ys, ys) * 2 + core

    def slot_of(at):
        return ((a + 2 - at // ys) % 2) * ys + lax.rem(y + ys - at % ys, ys)

    def ecopy(slot):
        return pltpu.make_async_remote_copy(
            esend, emaps.at[slot], es.at[slot], er.at[slot],
            device_id=slot_peer(slot), device_id_type=MESH,
        )

    bcopy = pltpu.make_async_remote_copy(
        esend.at[pl.ds(factors, 1)], bin_s, bs, br,
        device_id=(1, (ys - 1) * 2 + core), device_id_type=MESH,
    )
    heads = (pair == 0) & (g == 0)

    @pl.when(heads)
    def _():
        bcopy.start()

    slots = [ys] + [slot for slot in range(1, chips) if slot != ys]
    for slot in slots:
        ecopy(slot).start()
    emaps[0] = whole
    first = jnp.where(leads, mine, other)
    dcopy(1).wait_recv()
    mine_adds, other_adds = dmap[1], drecv[1]
    chip_adds = jnp.where(leads, mine_adds, other_adds) + jnp.exp(-float(hours) * srate) * compose(
        first, jnp.where(leads, other_adds, mine_adds), factors
    )
    ssend[...] = chip_adds

    def scopy(slot):
        return pltpu.make_async_remote_copy(
            ssend, smaps.at[slot], ss.at[slot], sr.at[slot],
            device_id=slot_peer(slot), device_id_type=MESH,
        )

    for slot in slots:
        scopy(slot).start()
    smaps[0] = chip_adds
    span = 2 * local
    after = (a + 1) * local
    hour_at = (
        lax.broadcasted_iota(jnp.int32, (plane, hours, factors), 0) * hours
        + lax.broadcasted_iota(jnp.int32, (plane, hours, factors), 1)
    )
    far = (hour_at - after).astype(F32)
    tail_w = jnp.where(far >= 0.0, keep[None] * jnp.exp(-jnp.maximum(far, 0.0) * srate[None]), 0.0)
    end_w = jnp.exp(-(span - after).astype(F32) * srate)
    span_w = jnp.exp(-float(span) * srate)
    def vcopy(far):
        return pltpu.make_async_remote_copy(
            vout, vin, vs.at[far - 1], vr,
            device_id=(lax.rem(tm + 2 * far, tms), ser), device_id_type=MESH,
        )

    def vstart(to):
        return pltpu.make_async_remote_copy(
            vout, vin, vls.at[to], vr,
            device_id=(2 + to // ys, (to % ys) * 2 + core), device_id_type=MESH,
        )

    def carry(vector, matrix, shift):
        column = jnp.sum(jnp.where(eye, vector, 0.0), axis=1, keepdims=True)
        return jnp.sum(column * matrix, axis=0, keepdims=True) + shift

    for slot in slots[:-1]:
        ecopy(slot).wait_recv()

    @pl.when(leader)
    def _():
        bcopy.wait_recv()
        state = bin_s[...]
        for at in range(1, chips):
            step = emaps[slot_of(at)]
            state = carry(state, step[:factors], step[factors : factors + 1])
        vout[...] = state
        if pairs > 1:
            for to in range(chips - 1, -1, -1):
                vstart(to).start()

    ecopy(slots[-1]).wait_recv()
    parts = [emaps[slot_of(at)] for at in range(chips)]
    level = parts
    while len(level) > 1:
        level = [
            compose(level[i], level[i + 1], factors) if i + 1 < len(level) else level[i]
            for i in range(0, len(level), 2)
        ]
    total = level[0]

    tcopy = pltpu.make_async_remote_copy(
        tsend, trecv, ts, tr, device_id=(lax.rem(tm + 2, tms), ser), device_id_type=MESH
    )
    odd = pair % 2 == 1
    hands_map = (pair % 2 == 0) & (pair > 0) & (pair < pairs - 1)

    @pl.when(hands_map)
    def _():
        tsend[...] = total
        tcopy.start()

    @pl.when(pair == 0)
    def _():
        vcur[...] = jnp.zeros_like(vcur)

    def forward():
        vcopy(1).wait_recv()
        vcur[...] = vin[...]

        @pl.when(odd & (pair > 1))
        def _():
            tcopy.wait_recv()
            vcur[...] = carry(vin[...], trecv[0:factors], trecv[factors : factors + 1])

        @pl.when(odd & (pair < pairs - 1))
        def _():
            vout[...] = carry(vcur[...], total[:factors], total[factors : factors + 1])
            vcopy(1).start()

            @pl.when(pair < pairs - 2)
            def _():
                vcopy(2).start()

    @pl.when(pair == 1)
    def _():
        forward()

    unit = jnp.concatenate([eye_f, jnp.zeros((8, factors), F32)], axis=0)
    start_map = unit
    before_chip = [parts[0]]
    for at in range(1, chips):
        start_map = jnp.where(g == at, before_chip[-1], start_map)
        if at + 1 < chips:
            before_chip.append(compose(before_chip[-1], parts[at], factors))
    start_map = jnp.where(leads, start_map, compose(start_map, other, factors))
    cums = cum[...]
    lead = dot3(start_map, cums[:factors])
    wide_at = hours * factors
    lead_s[:, :wide_at] = halves(lead[:factors])
    lead_b = lead[factors:] + cums[factors:]
    at_end = pair == pairs - 1
    for k in range(1, chips):
        scopy(k).wait_recv()
    group_adds = smaps[slot_of(0)] + jnp.where(at_end, span_w * decays, 0.0) * total
    for at in range(1, chips):
        group_adds = group_adds + jnp.exp(-float(2 * hours * at) * srate) * compose(
            before_chip[at - 1], smaps[slot_of(at)], factors
        )
    lead_s[:, wide_at:] = halves(group_adds[:factors])
    lead_b = jnp.concatenate([lead_b, group_adds[factors:]], axis=1)

    @pl.when(pair > 1)
    def _():
        forward()

    current = jnp.broadcast_to(vcur[...], (8, factors))
    filtered = dot_halves(current, lead_s[...]) + lead_b
    for h in range(hours):
        row = filtered[0:1, h * factors : (h + 1) * factors]
        fown[h : h + 1, :] = row
    shown[...] = filtered[:, hours * factors :]

    def ccopy(to, of):
        return pltpu.make_async_remote_copy(
            shown, shifts.at[of], cs.at[to], cr.at[of],
            device_id=(to * 2 + a, ser), device_id_type=MESH,
        )

    @pl.loop(0, pair)
    def _(to):
        ccopy(to, pair).start()

    fall[place_in] = fown[...]

    def fcopy(k):
        return pltpu.make_async_remote_copy(
            fown, fall.at[place_in], fs.at[k], fr.at[k],
            device_id=plane_peer(k), device_id_type=MESH,
        )

    for k in range(1, plane):
        fcopy(k).start()
    prec_root = jnp.sqrt(prec_ref[...])
    for k in range(1, plane):
        fcopy(k).wait_recv()
    together = fall[...]
    ending = decays * together[plane - 1][hours - 1 : hours]
    follow = jnp.sum(jnp.sum(together * tail_w, axis=0), axis=0, keepdims=True)

    def gather(of, held):
        total, weight = held
        ccopy(pair, of).wait_recv()
        return total + weight * shifts[of][0:1], weight * span_w

    beyond, _ = lax.fori_loop(
        pair + 1, pairs, gather, (jnp.where(at_end, ending, 0.0), jnp.ones_like(span_w))
    )
    follow = follow + end_w * beyond
    for s in range(sers - 1, -1, -1):
        block = fall[a * sers + s]
        for h in range(hours - 1, -1, -1):
            follow = keep * block[h : h + 1] + retain * follow
            smoothed_ref[s * hours + h : s * hours + h + 1, :] = follow

    fitted = jnp.dot(smoothed_ref[...].astype(BF16), lt_s[...], preferred_element_type=F32)
    standard = (readings_ref[...].astype(F32) - fitted) * prec_root
    probab = 0.5 * (1.0 + lax.erf(standard * 0.7071067811865476))
    spot = jnp.where(present_ref[...] > 0, probab * BINS - 0.5, -4.0)
    for b in range(BINS):
        at = bin_row(b)
        table[at : at + 1, :] = jnp.sum(
            jnp.maximum(0.0, 1.0 - jnp.abs(spot - b)), axis=0, keepdims=True
        )
    padded = table.shape[0]
    for b in range(BINS, padded):
        at = bin_row(b)
        table[at : at + 1, :] = jnp.zeros_like(table[at : at + 1, :])
    th, tl = split2(table[...])
    tally = jnp.dot(
        jnp.concatenate([th, tl], axis=0), mem_s[...], preferred_element_type=F32
    )
    tally = tally[:padded] + tally[padded:]
    lane = lax.broadcasted_iota(jnp.int32, tally.shape, 1) // GROUPS
    sub = lax.broadcasted_iota(jnp.int32, tally.shape, 0) % 8
    tally = jnp.where(lane == sub, tally, 0.0).reshape(padded // 8, 8, tally.shape[1])
    hown[...] = jnp.sum(tally, axis=1)
    hall[me] = hown[...]

    def hsend(k):
        at = lax.rem(place_in + (plane - 1 - k % plane), plane)
        to = lax.rem(pair + (pairs - 1 - k // plane), pairs)
        pltpu.make_async_remote_copy(
            hown, hall.at[me], hs, hr,
            device_id=(to * 2 + at // sers, lax.rem(at, sers)), device_id_type=MESH,
        ).start()

    if n <= 64:
        for k in range(n - 1):
            hsend(k)
    else:
        pl.loop(0, n - 1)(hsend)

    for k in range(ys):
        for h in range(sets):
            copy1(k, h).wait_send()
            if k:
                copy2(k, h).wait_send()
    dcopy(0).wait_send()
    dcopy(1).wait_send()
    for k in range(1, chips):
        ecopy(k).wait_send()
        scopy(k).wait_send()

    @pl.when(odd & (pair < pairs - 1))
    def _():
        vcopy(1).wait_send()

    @pl.when(heads)
    def _():
        bcopy.wait_send()

    if pairs > 1:

        @pl.when(leader)
        def _():
            for to in range(chips):
                vstart(to).wait_send()

    @pl.when(odd & (pair < pairs - 2))
    def _():
        vcopy(2).wait_send()

    @pl.when(hands_map)
    def _():
        tcopy.wait_send()

    for k in range(1, plane):
        fcopy(k).wait_send()

    @pl.loop(0, pair)
    def _(to):
        ccopy(to, pair).wait_send()

    hdrain = pltpu.make_async_remote_copy(
        hall.at[pl.ds(0, n - 1)], hall.at[pl.ds(0, n - 1)], hs, hr,
        device_id=(tm, lax.rem(ser + 1, sers)), device_id_type=MESH,
    )
    hdrain.wait_recv()
    hdrain.wait_send()
    hist_ref[...] = jnp.sum(hall[...], axis=0)


def solution(mesh):
    tms, sers = mesh.shape["tm"], mesh.shape["series"]

    def body(readings, present, loadings, prec, gain, frate, srate, regions):
        local, series = readings.shape
        factors = loadings.shape[1]
        hours = local // sers
        n, ys = tms * sers, sers // 2
        chips = 2 * ys
        rows = factors + 8
        padded = -(-BINS // 8) * 8
        together = 2 if hours % 2 == 0 else 1
        sets, packed_rows = hours // together, factors + 8
        vm = pltpu.VMEM
        dma = pltpu.SemaphoreType.DMA
        smoothed, packed = pl.pallas_call(
            functools.partial(kernel, tms, sers),
            out_shape=(
                vm((local, factors), F32),
                vm((padded // 8, 8 * GROUPS), F32),
            ),
            in_specs=[pl.BlockSpec(memory_space=pl.ANY)] * 8,
            out_specs=(pl.BlockSpec(memory_space=vm),) * 2,
            scratch_shapes=[
                vm((local, series), readings.dtype),
                vm((local, series), present.dtype),
                vm((series, factors), loadings.dtype),
                vm((1, series), F32),
                vm((1, factors), F32),
                vm((1, factors), F32),
                vm((1, factors), F32),
                vm((1, series), regions.dtype),
                vm((factors, series), BF16),
                vm((factors, series), BF16),
                vm((series, 8 * GROUPS), BF16),
                vm((local + 8, factors), F32),
                vm((ys, sets, packed_rows, factors), F32),
                vm((ys, sets, packed_rows, factors), F32),
                vm((ys, sets, packed_rows, factors), F32),
                vm((ys, sets, packed_rows, factors), F32),
                vm((rows, hours * factors), F32),
                vm((2, rows, factors), F32),
                vm((2, rows, factors), F32),
                vm((chips, rows, factors), F32),
                vm((rows, factors), F32),
                vm((chips, rows, factors), F32),
                vm((rows, factors), F32),
                vm((2 * factors, (hours + 1) * factors), BF16),
                vm((1, factors), F32),
                vm((1, factors), F32),
                vm((1, factors), F32),
                vm((1, factors), F32),
                vm((rows, factors), F32),
                vm((rows, factors), F32),
                vm((hours, factors), F32),
                vm((2 * sers, hours, factors), F32),
                vm((8, factors), F32),
                vm((tms // 2, 8, factors), F32),
                vm((padded, series), F32),
                vm((padded // 8, 8 * GROUPS), F32),
                vm((n, padded // 8, 8 * GROUPS), F32),
                dma((8,)),
                dma((ys, sets)),
                dma((ys, sets)),
                dma((ys, sets)),
                dma((ys, sets)),
                dma((2,)),
                dma((2,)),
                dma((chips,)),
                dma((chips,)),
                dma((chips,)),
                dma((chips,)),
                dma((2,)), dma, dma((chips,)), dma, dma, dma, dma,
                dma((2 * sers,)),
                dma((2 * sers,)),
                dma((tms // 2,)),
                dma((tms // 2,)),
                dma, dma,
            ],
            compiler_params=pltpu.CompilerParams(collective_id=0, has_side_effects=True),
        )(
            readings, present, loadings, prec.reshape(1, -1), gain.reshape(1, -1),
            frate.reshape(1, -1), srate.reshape(1, -1), regions.reshape(1, -1),
        )
        scale = BINS * GROUPS / (local * tms * series * sers)
        return pl.pallas_call(
            functools.partial(finish, scale),
            out_shape=(
                jax.ShapeDtypeStruct((local, factors), F32),
                jax.ShapeDtypeStruct((GROUPS, BINS), F32),
            ),
            in_specs=[pl.BlockSpec(memory_space=vm)] * 2,
            out_specs=(pl.BlockSpec(memory_space=pl.ANY),) * 2,
            scratch_shapes=[vm((GROUPS, BINS), F32), dma((2,))],
        )(*(pltpu.with_memory_space_constraint(part, vm) for part in (smoothed, packed)))

    in_specs = (
        P("tm", "series"), P("tm", "series"), P("series", None), P("series"),
        P(), P(), P(), P("series"),
    )
    return jax.shard_map(
        body, mesh=mesh, in_specs=in_specs, out_specs=(P("tm", None), P()), check_vma=False
    )
```

```python
import functools

import jax
import jax.numpy as jnp
from jax import lax
from jax.experimental import pallas as pl
from jax.experimental.pallas import tpu as pltpu
from jax.sharding import PartitionSpec as P

BINS = 20
GROUPS = 16
MESH = pl.DeviceIdType.MESH
F32 = jnp.float32
BF16 = jnp.bfloat16


def split2(x):
    high = x.astype(BF16)
    return high, (x - high.astype(F32)).astype(BF16)


def halves(right):
    high, low = split2(right)
    return jnp.concatenate([high, low], axis=0)


def dot_halves(left, right):
    high, low = split2(left)
    both = jnp.concatenate(
        [
            jnp.concatenate([high, high], axis=1),
            jnp.concatenate([low, jnp.zeros_like(low)], axis=1),
        ],
        axis=0,
    )
    out = jnp.dot(both, right, preferred_element_type=F32)
    return out[: left.shape[0]] + out[left.shape[0] :]


def dot_t(left, right):
    return lax.dot_general(left, right, (((1,), (1,)), ((), ())), preferred_element_type=F32)


def dot3(left, right):
    return dot_halves(left, halves(right))


def compose(earlier, later, factors):
    out = dot3(earlier, later[:factors])
    return jnp.concatenate([out[:factors], out[factors:] + later[factors:]], axis=0)


LINES = -(-(BINS + 2) // 8)


def finish(scale, rows_ref, packed_ref, smoothed_ref, hist_ref, held, sems):
    rows_out = pltpu.make_async_copy(rows_ref, smoothed_ref, sems.at[0])
    rows_out.start()
    packed = packed_ref[...] * scale
    width = packed.shape[1]
    parts = []
    for at in range(LINES):
        parts += [packed[at : at + 1], jnp.zeros((7, width), F32)]
    tall = jnp.concatenate(parts + [jnp.zeros((width - 8 * LINES, width), F32)], axis=0).T
    total = tall[:GROUPS]
    for j in range(1, 8):
        total = total + pltpu.roll(tall[j * GROUPS : (j + 1) * GROUPS], j, 1)
    held[...] = total[:, :BINS]
    hist_out = pltpu.make_async_copy(held, hist_ref, sems.at[1])
    hist_out.start()
    rows_out.wait()
    hist_out.wait()


def kernel(
    tms, sers,
    readings_in, present_in, loadings_in, prec_in, gain_in, frate_in, srate_in, regions_in,
    smoothed_ref, hist_ref,
    readings_ref, present_ref, loadings_ref, prec_ref, gain_ref, frate_ref, srate_ref, regions_ref,
    lt_s, sl_s, mem_s, score_s, send1, recv1, acc, recv2, cum, dmap, emaps, esend, smaps, ssend, lead_s,
    vin, vout, vcur, bin_s, tsend, trecv, fown, fall, shown, shifts, table, hown, hall,
    ins, s1s, s1r, s2s, s2r, ds, dr, es, er, ss, sr, vs, vr, vls, bs, br, ts, tr, there, fs, fr, cs, cr, hs, hr,
):
    tm, ser = lax.axis_index("tm"), lax.axis_index("series")
    y, core = ser // 2, ser % 2
    ys = sers // 2
    local = readings_ref.shape[0]
    factors = loadings_ref.shape[1]
    rows = factors + 8
    hours = local // sers
    n = tms * sers
    me = tm * sers + ser
    pair, a = tm // 2, tm % 2
    pairs = tms // 2
    chips = 2 * ys
    g = a * ys + y
    leader = (pair == 0) & (g == chips - 1)
    odd = pair % 2 == 1
    hands_map = (pair % 2 == 0) & (pair > 0) & (pair < pairs - 1)

    inputs = [
        pltpu.make_async_copy(src, dst, ins.at[i])
        for i, (src, dst) in enumerate(
            [
                (loadings_in, loadings_ref), (prec_in, prec_ref), (present_in, present_ref),
                (readings_in, readings_ref), (gain_in, gain_ref), (frate_in, frate_ref),
                (srate_in, srate_ref), (regions_in, regions_ref),
            ]
        )
    ]
    for item in inputs:
        item.start()

    barrier = pltpu.get_barrier_semaphore()

    plane = 2 * sers
    place_in = a * sers + ser

    def plane_peer(k):
        at = lax.rem(place_in + k, plane)
        return pair * 2 + at // sers, lax.rem(at, sers)

    for k in range(1, plane):
        pl.semaphore_signal(barrier, inc=1, device_id=plane_peer(k), device_id_type=MESH)
    @pl.when(pair > 0)
    def _():
        pl.semaphore_signal(barrier, inc=1, device_id=(tm - 2, ser), device_id_type=MESH)

    @pl.when(pair < pairs - 1)
    def _():
        pl.semaphore_signal(barrier, inc=1, device_id=(tm + 2, ser), device_id_type=MESH)

    @pl.when((pair == 1) & (g < chips - 1))
    def _():
        pl.semaphore_signal(
            barrier, inc=1, device_id=(1, (ys - 1) * 2 + core), device_id_type=MESH
        )

    for item in inputs[:2]:
        item.wait()

    ltf = loadings_ref[...].astype(F32).T
    lt_s[...] = ltf.astype(BF16)
    sl_s[...] = (ltf * prec_ref[...]).astype(BF16)
    for item in inputs[2:4]:
        item.wait()
    present = present_ref[...].astype(F32)
    read_f = readings_ref[...].astype(F32)
    score_s[0:local] = dot_t((read_f * present).astype(BF16), sl_s[...])
    score_s[local:] = jnp.zeros_like(score_s[local:])

    together_h = 2 if hours % 2 == 0 else 1
    sets = hours // together_h
    sub = lax.broadcasted_iota(jnp.int32, (factors, factors), 0)
    lane = lax.broadcasted_iota(jnp.int32, (factors, factors), 1)
    eye = sub == lane
    upper = lane > sub
    line = lax.broadcasted_iota(jnp.int32, (8, factors), 0)

    def hour_terms(base, dst, held):
        rights = []
        for j in range(len(held) * together_h):
            mask = present_ref[pl.ds(base + j, 1), :].astype(F32)
            mask = jnp.broadcast_to(mask, (16, mask.shape[1])).astype(BF16)
            right = sl_s[...].reshape(factors // 16, 16, mask.shape[1]) * mask[None]
            rights.append(right.reshape(factors, mask.shape[1]))
        out = dot_t(lt_s[...], jnp.concatenate(rights, axis=0))
        for place, h in enumerate(held):
            at = place * together_h
            first = out[:, at * factors : (at + 1) * factors]
            tail = jnp.zeros((8, factors), F32)
            if together_h == 2:
                second = out[:, (at + 1) * factors : (at + 2) * factors]
                dst[h, :factors] = jnp.where(upper, first, second)
                corner = jnp.sum(jnp.where(eye, first, 0.0), axis=0, keepdims=True)
                tail = jnp.where(line == together_h, corner, tail)
            else:
                dst[h, :factors] = first
            for j in range(together_h):
                row = jnp.broadcast_to(score_s[pl.ds(base + at + j, 1), :], (8, factors))
                tail = jnp.where(line == j, row, tail)
            dst[h, factors:] = tail

    def unpack(packed):
        block, tail = packed[:factors], packed[factors:]
        if together_h == 1:
            matrices = [block]
        else:
            turned = block.T
            matrices = [
                jnp.where(eye, tail[together_h : together_h + 1], jnp.where(upper, block, turned)),
                jnp.where(upper, turned, block),
            ]
        return [
            (matrices[j], jnp.where(line == 0, tail[j : j + 1], 0.0)) for j in range(together_h)
        ]

    def copy1(k, h):
        return pltpu.make_async_remote_copy(
            send1.at[k, h], recv1.at[k, h], s1s.at[k, h], s1r.at[k, h],
            device_id=(tm, y * 2 + (1 - core)), device_id_type=MESH,
        )

    def copy2(k, h):
        return pltpu.make_async_remote_copy(
            acc.at[k, h], recv2.at[k, h], s2s.at[k, h], s2r.at[k, h],
            device_id=(tm, lax.rem(y + k, ys) * 2 + core), device_id_type=MESH,
        )

    order = list(range(1, ys)) + [0]
    for place, k in enumerate(order):
        owner = lax.rem(y + k, ys) * 2
        theirs, ours = (owner + (1 - core)) * hours, (owner + core) * hours
        groups = [[h] for h in range(sets)] if k else [list(range(sets))]
        for held in groups:
            hour_terms(theirs + held[0] * together_h, send1.at[k], held)
            if place == 0 and held[0] == 0:
                before = jnp.where(pair > 0, 1, 0)
                behind = jnp.where(pair < pairs - 1, 1, 0)
                extra = jnp.where(leader, chips - 1, 0)
                pl.semaphore_wait(barrier, plane - 1 + before + behind + extra)

                @pl.when(hands_map)
                def _():
                    pl.semaphore_signal(there, inc=1, device_id=(tm - 2, ser), device_id_type=MESH)

            for h in held:
                copy1(k, h).start()
        for held in groups:
            hour_terms(ours + held[0] * together_h, acc.at[k], held)
            for h in held if k else []:
                copy1(k, h).wait_recv()
                acc[k, h] = acc[k, h] + recv1[k, h]
                copy2(k, h).start()

    for item in inputs[4:]:
        item.wait()
    wide = lax.broadcasted_iota(jnp.int32, (factors, regions_ref.shape[1]), 0) % GROUPS
    mem_s[...] = jnp.where(wide == regions_ref[...], 1.0, 0.0).astype(F32).T.astype(BF16)
    gain = gain_ref[...]
    decays = jnp.exp(-frate_ref[...])
    srate = srate_ref[...]
    retain = jnp.exp(-srate)
    keep = 1.0 - retain * decays
    eye_f = jnp.where(eye, 1.0, 0.0).astype(F32)
    decay_col = jnp.sum(jnp.where(eye, decays, 0.0), axis=1, keepdims=True)
    for h in range(sets):
        copy1(0, h).wait_recv()

    maps = []
    for h in range(sets):
        total = acc[0, h] + recv1[0, h]
        for k in range(1, ys):
            copy2(k, h).wait_recv()
            total = total + recv2[k, h]
        fresh = [
            jnp.concatenate([decay_col * (eye_f - gain * inform), gain * scores], axis=0)
            for inform, scores in unpack(total)
        ]
        if together_h == 2:
            fresh[1] = compose(fresh[0], fresh[1], factors)
        if maps:
            fresh = [compose(maps[-1], item, factors) for item in fresh]
        maps += fresh
    dmap[core, 0] = maps[-1]

    def dcopy(part):
        return pltpu.make_async_remote_copy(
            dmap.at[core, part], dmap.at[core, part], ds.at[part], dr.at[part],
            device_id=(tm, y * 2 + (1 - core)), device_id_type=MESH,
        )

    dcopy(0).start()
    adds = keep * maps[0]
    for h in range(1, hours):
        adds = adds + keep * jnp.exp(-float(h) * srate) * maps[h]
    dmap[core, 1] = adds
    dcopy(1).start()
    for h in range(hours):
        cum[:, h * factors : (h + 1) * factors] = maps[h]
    dcopy(0).wait_recv()
    leads = core == 0
    first = dmap[0, 0]
    whole = compose(first, dmap[1, 0], factors)
    esend[...] = whole

    def slot_peer(slot):
        return pair * 2 + (a + slot // ys) % 2, lax.rem(y + slot % ys, ys) * 2 + core

    def slot_of(at):
        return ((a + 2 - at // ys) % 2) * ys + lax.rem(y + ys - at % ys, ys)

    def ecopy(slot):
        return pltpu.make_async_remote_copy(
            esend, emaps.at[slot], es.at[slot], er.at[slot],
            device_id=slot_peer(slot), device_id_type=MESH,
        )

    bcopy = pltpu.make_async_remote_copy(
        esend.at[pl.ds(factors, 1)], bin_s, bs, br,
        device_id=(1, (ys - 1) * 2 + core), device_id_type=MESH,
    )
    heads = (pair == 0) & (g == 0)

    @pl.when(heads)
    def _():
        bcopy.start()

    slots = [ys] + [slot for slot in range(1, chips) if slot != ys]
    for slot in slots:
        ecopy(slot).start()
    emaps[0] = whole
    dcopy(1).wait_recv()
    chip_adds = dmap[0, 1] + jnp.exp(-float(hours) * srate) * compose(first, dmap[1, 1], factors)
    ssend[...] = chip_adds

    def scopy(slot):
        return pltpu.make_async_remote_copy(
            ssend, smaps.at[slot], ss.at[slot], sr.at[slot],
            device_id=slot_peer(slot), device_id_type=MESH,
        )

    for slot in slots:
        scopy(slot).start()
    smaps[0] = chip_adds
    span = 2 * local
    after = (a + 1) * local
    hour_at = (
        lax.broadcasted_iota(jnp.int32, (plane, hours, factors), 0) * hours
        + lax.broadcasted_iota(jnp.int32, (plane, hours, factors), 1)
    )
    far = (hour_at - after).astype(F32)
    tail_w = jnp.where(far >= 0.0, keep[None] * jnp.exp(-jnp.maximum(far, 0.0) * srate[None]), 0.0)
    end_w = jnp.exp(-(span - after).astype(F32) * srate)
    span_w = jnp.exp(-float(span) * srate)
    def vcopy(far):
        return pltpu.make_async_remote_copy(
            vout, vin, vs.at[far - 1], vr,
            device_id=(lax.rem(tm + 2 * far, tms), ser), device_id_type=MESH,
        )

    def vstart(to):
        return pltpu.make_async_remote_copy(
            vout, vin, vls.at[to], vr,
            device_id=(2 + to // ys, (to % ys) * 2 + core), device_id_type=MESH,
        )

    def carry(vector, matrix, shift):
        column = jnp.sum(jnp.where(eye, vector, 0.0), axis=1, keepdims=True)
        return jnp.sum(column * matrix, axis=0, keepdims=True) + shift

    for slot in slots[:-1]:
        ecopy(slot).wait_recv()

    @pl.when(leader)
    def _():
        bcopy.wait_recv()
        state = bin_s[...]
        for at in range(1, chips):
            step = emaps[slot_of(at)]
            state = carry(state, step[:factors], step[factors : factors + 1])
        vout[...] = state
        if pairs > 1:
            for to in range(chips - 1, -1, -1):
                vstart(to).start()

    ecopy(slots[-1]).wait_recv()
    parts = [emaps[slot_of(at)] for at in range(chips)]
    level = parts
    while len(level) > 1:
        level = [
            compose(level[i], level[i + 1], factors) if i + 1 < len(level) else level[i]
            for i in range(0, len(level), 2)
        ]
    total = level[0]

    tcopy = pltpu.make_async_remote_copy(
        tsend, trecv, ts, tr, device_id=(lax.rem(tm + 2, tms), ser), device_id_type=MESH
    )

    @pl.when(hands_map)
    def _():
        tsend[...] = total
        tcopy.start()

    @pl.when(pair == 0)
    def _():
        vcur[...] = jnp.zeros_like(vcur)

    def forward():
        vcopy(1).wait_recv()
        vcur[...] = vin[...]

        @pl.when(odd & (pair > 1))
        def _():
            tcopy.wait_recv()
            vcur[...] = carry(vin[...], trecv[0:factors], trecv[factors : factors + 1])

        @pl.when(odd & (pair < pairs - 1))
        def _():
            vout[...] = carry(vcur[...], total[:factors], total[factors : factors + 1])
            vcopy(1).start()

            @pl.when(pair < pairs - 2)
            def _():
                pl.semaphore_wait(there, 1)
                vcopy(2).start()

    @pl.when(pair == 1)
    def _():
        forward()

    unit = jnp.concatenate([eye_f, jnp.zeros((8, factors), F32)], axis=0)
    start_map = unit
    before_chip = [parts[0]]
    for at in range(1, chips):
        start_map = jnp.where(g == at, before_chip[-1], start_map)
        if at + 1 < chips:
            before_chip.append(compose(before_chip[-1], parts[at], factors))
    start_map = jnp.where(leads, start_map, compose(start_map, first, factors))
    cums = cum[...]
    lead = dot3(start_map, cums[:factors])
    wide_at = hours * factors
    lead_s[:, :wide_at] = halves(lead[:factors])
    lead_b = lead[factors:] + cums[factors:]
    at_end = pair == pairs - 1
    for k in range(1, chips):
        scopy(k).wait_recv()
    group_adds = smaps[slot_of(0)] + jnp.where(at_end, span_w * decays, 0.0) * total
    for at in range(1, chips):
        group_adds = group_adds + jnp.exp(-float(2 * hours * at) * srate) * compose(
            before_chip[at - 1], smaps[slot_of(at)], factors
        )
    lead_s[:, wide_at:] = halves(group_adds[:factors])
    lead_b = jnp.concatenate([lead_b, group_adds[factors:]], axis=1)

    @pl.when(pair > 1)
    def _():
        forward()

    current = jnp.broadcast_to(vcur[...], (8, factors))
    filtered = dot_halves(current, lead_s[...]) + lead_b
    for h in range(hours):
        row = filtered[0:1, h * factors : (h + 1) * factors]
        fown[h : h + 1, :] = row
    shown[...] = filtered[:, hours * factors :]

    def ccopy(to, of):
        return pltpu.make_async_remote_copy(
            shown, shifts.at[of], cs.at[to], cr.at[of],
            device_id=(to * 2 + a, ser), device_id_type=MESH,
        )

    @pl.loop(0, pair)
    def _(to):
        ccopy(to, pair).start()

    fall[place_in] = fown[...]

    def fcopy(k):
        return pltpu.make_async_remote_copy(
            fown, fall.at[place_in], fs.at[k], fr.at[k],
            device_id=plane_peer(k), device_id_type=MESH,
        )

    for k in range(1, plane):
        fcopy(k).start()
    prec_root = jnp.sqrt(prec_ref[...])
    for k in range(1, plane):
        fcopy(k).wait_recv()
    together = fall[...]
    ending = decays * together[plane - 1][hours - 1 : hours]
    follow = jnp.sum(jnp.sum(together * tail_w, axis=0), axis=0, keepdims=True)

    def gather(of, held):
        total, weight = held
        ccopy(pair, of).wait_recv()
        return total + weight * shifts[of][0:1], weight * span_w

    beyond, _ = lax.fori_loop(
        pair + 1, pairs, gather, (jnp.where(at_end, ending, 0.0), jnp.ones_like(span_w))
    )
    follow = follow + end_w * beyond
    for s in range(sers - 1, -1, -1):
        block = fall[a * sers + s]
        for h in range(hours - 1, -1, -1):
            follow = keep * block[h : h + 1] + retain * follow
            smoothed_ref[s * hours + h : s * hours + h + 1, :] = follow

    fitted = jnp.dot(smoothed_ref[...].astype(BF16), lt_s[...], preferred_element_type=F32)
    standard = (readings_ref[...].astype(F32) - fitted) * prec_root
    probab = 0.5 * (1.0 + lax.erf(standard * 0.7071067811865476))
    spot = jnp.where(present_ref[...] > 0, probab * BINS - 0.5, -4.0)
    padded = table.shape[0]
    across = lax.broadcasted_iota(jnp.int32, (8, spot.shape[1]), 0)
    picks = [across % 2 == 0, across // 2 % 2 == 0, across < 4]

    def above(knot):
        if knot > BINS:
            return jnp.zeros((8, spot.shape[1]), F32)
        over = jnp.maximum(0.0, spot - knot)
        total = over[:8]
        for at in range(8, local, 8):
            total = total + over[at : at + 8]
        return total

    for at in range(0, padded, 8):
        level = [above(at + i - 1) for i in range(8)]
        for pick, shift in zip(picks, (1, 2, 4)):
            level = [
                jnp.where(pick, x, z) + pltpu.roll(jnp.where(pick, z, x), shift, 0)
                for x, z in zip(level[::2], level[1::2])
            ]
        table[at : at + 8, :] = level[0]
    sums = table[...]
    next_sums = pltpu.roll(sums, padded - 1, 0)
    bins = sums - 2.0 * next_sums + pltpu.roll(sums, padded - 2, 0)
    bins = jnp.where(lax.broadcasted_iota(jnp.int32, bins.shape, 0) < BINS, bins, 0.0)
    th, tl = split2(bins)
    tally = jnp.dot(
        jnp.concatenate([th, tl], axis=0), mem_s[...], preferred_element_type=F32
    )
    tally = tally[:padded] + tally[padded:]
    lane = lax.broadcasted_iota(jnp.int32, tally.shape, 1) // GROUPS
    sub = lax.broadcasted_iota(jnp.int32, tally.shape, 0) % 8
    tally = jnp.where(lane == sub, tally, 0.0).reshape(padded // 8, 8, tally.shape[1])
    hown[...] = jnp.sum(tally, axis=1)
    hall[me] = hown[...]

    def hsend(k):
        at = lax.rem(place_in + (plane - 1 - k % plane), plane)
        to = lax.rem(pair + (pairs - 1 - k // plane), pairs)
        pltpu.make_async_remote_copy(
            hown, hall.at[me], hs, hr,
            device_id=(to * 2 + at // sers, lax.rem(at, sers)), device_id_type=MESH,
        ).start()

    if n <= 64:
        for k in range(n - 1):
            hsend(k)
    else:
        pl.loop(0, n - 1)(hsend)

    for k in range(ys):
        for h in range(sets):
            copy1(k, h).wait_send()
            if k:
                copy2(k, h).wait_send()
    dcopy(0).wait_send()
    dcopy(1).wait_send()
    for k in range(1, chips):
        ecopy(k).wait_send()
        scopy(k).wait_send()

    @pl.when(odd & (pair < pairs - 1))
    def _():
        vcopy(1).wait_send()

    @pl.when(heads)
    def _():
        bcopy.wait_send()

    if pairs > 1:

        @pl.when(leader)
        def _():
            for to in range(chips):
                vstart(to).wait_send()

    @pl.when(odd & (pair < pairs - 2))
    def _():
        vcopy(2).wait_send()

    @pl.when(hands_map)
    def _():
        tcopy.wait_send()

    for k in range(1, plane):
        fcopy(k).wait_send()

    @pl.loop(0, pair)
    def _(to):
        ccopy(to, pair).wait_send()

    hdrain = pltpu.make_async_remote_copy(
        hall.at[pl.ds(0, n - 1)], hall.at[pl.ds(0, n - 1)], hs, hr,
        device_id=(tm, lax.rem(ser + 1, sers)), device_id_type=MESH,
    )
    hdrain.wait_recv()
    hdrain.wait_send()
    hist_ref[...] = jnp.sum(hall[...], axis=0)


def solution(mesh):
    tms, sers = mesh.shape["tm"], mesh.shape["series"]

    def body(readings, present, loadings, prec, gain, frate, srate, regions):
        local, series = readings.shape
        factors = loadings.shape[1]
        hours = local // sers
        n, ys = tms * sers, sers // 2
        chips = 2 * ys
        rows = factors + 8
        padded = -(-(BINS + 2) // 8) * 8
        together = 2 if hours % 2 == 0 else 1
        sets, packed_rows = hours // together, factors + 8
        vm = pltpu.VMEM
        dma = pltpu.SemaphoreType.DMA
        smoothed, packed = pl.pallas_call(
            functools.partial(kernel, tms, sers),
            out_shape=(
                vm((local, factors), F32),
                vm((padded // 8, 8 * GROUPS), F32),
            ),
            in_specs=[pl.BlockSpec(memory_space=pl.ANY)] * 8,
            out_specs=(pl.BlockSpec(memory_space=vm),) * 2,
            scratch_shapes=[
                vm((local, series), readings.dtype),
                vm((local, series), present.dtype),
                vm((series, factors), loadings.dtype),
                vm((1, series), F32),
                vm((1, factors), F32),
                vm((1, factors), F32),
                vm((1, factors), F32),
                vm((1, series), regions.dtype),
                vm((factors, series), BF16),
                vm((factors, series), BF16),
                vm((series, 8 * GROUPS), BF16),
                vm((local + 8, factors), F32),
                vm((ys, sets, packed_rows, factors), F32),
                vm((ys, sets, packed_rows, factors), F32),
                vm((ys, sets, packed_rows, factors), F32),
                vm((ys, sets, packed_rows, factors), F32),
                vm((rows, hours * factors), F32),
                vm((2, 2, rows, factors), F32),
                vm((chips, rows, factors), F32),
                vm((rows, factors), F32),
                vm((chips, rows, factors), F32),
                vm((rows, factors), F32),
                vm((2 * factors, (hours + 1) * factors), BF16),
                vm((1, factors), F32),
                vm((1, factors), F32),
                vm((1, factors), F32),
                vm((1, factors), F32),
                vm((rows, factors), F32),
                vm((rows, factors), F32),
                vm((hours, factors), F32),
                vm((2 * sers, hours, factors), F32),
                vm((8, factors), F32),
                vm((tms // 2, 8, factors), F32),
                vm((padded, series), F32),
                vm((padded // 8, 8 * GROUPS), F32),
                vm((n, padded // 8, 8 * GROUPS), F32),
                dma((8,)),
                dma((ys, sets)),
                dma((ys, sets)),
                dma((ys, sets)),
                dma((ys, sets)),
                dma((2,)),
                dma((2,)),
                dma((chips,)),
                dma((chips,)),
                dma((chips,)),
                dma((chips,)),
                dma((2,)), dma, dma((chips,)), dma, dma, dma, dma, pltpu.SemaphoreType.REGULAR,
                dma((2 * sers,)),
                dma((2 * sers,)),
                dma((tms // 2,)),
                dma((tms // 2,)),
                dma, dma,
            ],
            compiler_params=pltpu.CompilerParams(collective_id=0, has_side_effects=True),
        )(
            readings, present, loadings, prec.reshape(1, -1), gain.reshape(1, -1),
            frate.reshape(1, -1), srate.reshape(1, -1), regions.reshape(1, -1),
        )
        scale = BINS * GROUPS / (local * tms * series * sers)
        return pl.pallas_call(
            functools.partial(finish, scale),
            out_shape=(
                jax.ShapeDtypeStruct((local, factors), F32),
                jax.ShapeDtypeStruct((GROUPS, BINS), F32),
            ),
            in_specs=[pl.BlockSpec(memory_space=vm)] * 2,
            out_specs=(pl.BlockSpec(memory_space=pl.ANY),) * 2,
            scratch_shapes=[vm((GROUPS, BINS), F32), dma((2,))],
        )(*(pltpu.with_memory_space_constraint(part, vm) for part in (smoothed, packed)))

    in_specs = (
        P("tm", "series"), P("tm", "series"), P("series", None), P("series"),
        P(), P(), P(), P("series"),
    )
    return jax.shard_map(
        body, mesh=mesh, in_specs=in_specs, out_specs=(P("tm", None), P()), check_vma=False
    )
```

```python
import functools

import jax
import jax.numpy as jnp
from jax import lax
from jax.experimental import pallas as pl
from jax.experimental.pallas import tpu as pltpu
from jax.sharding import PartitionSpec as P

BINS = 20
GROUPS = 16
MESH = pl.DeviceIdType.MESH
F32 = jnp.float32
BF16 = jnp.bfloat16


def split2(x):
    high = x.astype(BF16)
    return high, (x - high.astype(F32)).astype(BF16)


def halves(right):
    high, low = split2(right)
    return jnp.concatenate([high, low, high], axis=0)


def dot_halves(left, right):
    high, low = split2(left)
    return jnp.dot(
        jnp.concatenate([high, high, low], axis=1), right, preferred_element_type=F32
    )


def dot_t(left, right):
    return lax.dot_general(left, right, (((1,), (1,)), ((), ())), preferred_element_type=F32)


def dot3(left, right):
    return dot_halves(left, halves(right))


def compose(earlier, later, factors):
    out = dot3(earlier, later[:factors])
    return jnp.concatenate([out[:factors], out[factors:] + later[factors:]], axis=0)


LINES = -(-(BINS + 2) // 8)


def finish(scale, rows_ref, packed_ref, smoothed_ref, hist_ref, held, sems):
    rows_out = pltpu.make_async_copy(rows_ref, smoothed_ref, sems.at[0])
    rows_out.start()
    packed = packed_ref[...] * scale
    width = packed.shape[1]
    parts = []
    for at in range(LINES):
        parts += [packed[at : at + 1], jnp.zeros((7, width), F32)]
    tall = jnp.concatenate(parts + [jnp.zeros((width - 8 * LINES, width), F32)], axis=0).T
    total = tall[:GROUPS]
    for j in range(1, 8):
        total = total + pltpu.roll(tall[j * GROUPS : (j + 1) * GROUPS], j, 1)
    held[...] = total[:, :BINS]
    hist_out = pltpu.make_async_copy(held, hist_ref, sems.at[1])
    hist_out.start()
    rows_out.wait()
    hist_out.wait()


def kernel(
    tms, sers,
    readings_in, present_in, loadings_in, prec_in, gain_in, frate_in, srate_in, regions_in,
    smoothed_ref, hist_ref,
    readings_ref, present_ref, loadings_ref, prec_ref, gain_ref, frate_ref, srate_ref, regions_ref,
    lt_s, sl_s, mem_s, score_s, send1, recv1, acc, recv2, cum, dmap, emaps, esend, smaps, ssend, lead_s,
    vin, vout, vcur, bin_s, lmaps, tsend, trecv, fown, fall, shown, shifts, table, hown, hall,
    ins, s1s, s1r, s2s, s2r, ds, dr, es, er, ss, sr, vs, vr, vls, ls, lr, bs, br, ts, tr, there, fs, fr, cs, cr, hs, hr,
):
    tm, ser = lax.axis_index("tm"), lax.axis_index("series")
    y, core = ser // 2, ser % 2
    ys = sers // 2
    local = readings_ref.shape[0]
    factors = loadings_ref.shape[1]
    rows = factors + 8
    hours = local // sers
    n = tms * sers
    me = tm * sers + ser
    pair, a = tm // 2, tm % 2
    pairs = tms // 2
    chips = 2 * ys
    g = a * ys + y
    leader = (pair == 0) & (g == chips - 1) & (core == 0)
    odd = pair % 2 == 1
    hands_map = (pair % 2 == 0) & (pair > 0) & (pair < pairs - 1)

    inputs = [
        pltpu.make_async_copy(src, dst, ins.at[i])
        for i, (src, dst) in enumerate(
            [
                (loadings_in, loadings_ref), (prec_in, prec_ref), (present_in, present_ref),
                (readings_in, readings_ref), (gain_in, gain_ref), (frate_in, frate_ref),
                (srate_in, srate_ref), (regions_in, regions_ref),
            ]
        )
    ]
    for item in inputs:
        item.start()

    barrier = pltpu.get_barrier_semaphore()

    plane = 2 * sers
    place_in = a * sers + ser

    def plane_peer(k):
        at = lax.rem(place_in + k, plane)
        return pair * 2 + at // sers, lax.rem(at, sers)

    for k in range(1, plane):
        pl.semaphore_signal(barrier, inc=1, device_id=plane_peer(k), device_id_type=MESH)
    @pl.when(pair > 0)
    def _():
        pl.semaphore_signal(barrier, inc=1, device_id=(tm - 2, ser), device_id_type=MESH)

    @pl.when(pair < pairs - 1)
    def _():
        pl.semaphore_signal(barrier, inc=1, device_id=(tm + 2, ser), device_id_type=MESH)

    @pl.when((pair == 1) & ((g < chips - 1) | (core == 1)))
    def _():
        pl.semaphore_signal(barrier, inc=1, device_id=(1, (ys - 1) * 2), device_id_type=MESH)

    for item in inputs[:2]:
        item.wait()

    turned_l = loadings_ref[...].T
    lt_s[...] = turned_l
    sl_s[...] = (turned_l.astype(F32) * prec_ref[...]).astype(BF16)
    for item in inputs[2:4]:
        item.wait()
    present = present_ref[...].astype(F32)
    read_f = readings_ref[...].astype(F32)
    score_s[0:local] = dot_t((read_f * present).astype(BF16), sl_s[...])
    score_s[local:] = jnp.zeros_like(score_s[local:])

    together_h = 2 if hours % 2 == 0 else 1
    sets = hours // together_h
    sub = lax.broadcasted_iota(jnp.int32, (factors, factors), 0)
    lane = lax.broadcasted_iota(jnp.int32, (factors, factors), 1)
    eye = sub == lane
    upper = lane > sub
    line = lax.broadcasted_iota(jnp.int32, (8, factors), 0)

    def hour_terms(base, dst, held):
        rights = []
        for j in range(len(held) * together_h):
            mask = present_ref[pl.ds(base + j, 1), :].astype(F32)
            mask = jnp.broadcast_to(mask, (16, mask.shape[1])).astype(BF16)
            right = sl_s[...].reshape(factors // 16, 16, mask.shape[1]) * mask[None]
            rights.append(right.reshape(factors, mask.shape[1]))
        out = dot_t(lt_s[...], jnp.concatenate(rights, axis=0))
        for place, h in enumerate(held):
            at = place * together_h
            first = out[:, at * factors : (at + 1) * factors]
            tail = jnp.zeros((8, factors), F32)
            if together_h == 2:
                second = out[:, (at + 1) * factors : (at + 2) * factors]
                dst[h, :factors] = jnp.where(upper, first, second)
                corner = jnp.sum(jnp.where(eye, first, 0.0), axis=0, keepdims=True)
                tail = jnp.where(line == together_h, corner, tail)
            else:
                dst[h, :factors] = first
            for j in range(together_h):
                row = jnp.broadcast_to(score_s[pl.ds(base + at + j, 1), :], (8, factors))
                tail = jnp.where(line == j, row, tail)
            dst[h, factors:] = tail

    def unpack(packed):
        block, tail = packed[:factors], packed[factors:]
        if together_h == 1:
            matrices = [block]
        else:
            turned = block.T
            matrices = [
                jnp.where(eye, tail[together_h : together_h + 1], jnp.where(upper, block, turned)),
                jnp.where(upper, turned, block),
            ]
        return [
            (matrices[j], jnp.where(line == 0, tail[j : j + 1], 0.0)) for j in range(together_h)
        ]

    used, sent = pl.ds(0, factors + 1), pl.ds(0, factors + together_h + 1)

    def copy1(k, h):
        return pltpu.make_async_remote_copy(
            send1.at[k, h, sent], recv1.at[k, h, sent], s1s.at[k, h], s1r.at[k, h],
            device_id=(tm, y * 2 + (1 - core)), device_id_type=MESH,
        )

    def copy2(k, h):
        return pltpu.make_async_remote_copy(
            acc.at[k, h, sent], recv2.at[k, h, sent], s2s.at[k, h], s2r.at[k, h],
            device_id=(tm, lax.rem(y + k, ys) * 2 + core), device_id_type=MESH,
        )

    order = list(range(1, ys)) + [0]
    for place, k in enumerate(order):
        owner = lax.rem(y + k, ys) * 2
        theirs, ours = (owner + (1 - core)) * hours, (owner + core) * hours
        groups = [[h] for h in range(sets)] if k else [list(range(sets))]
        for held in groups:
            hour_terms(theirs + held[0] * together_h, send1.at[k], held)
            if place == 0 and held[0] == 0:
                before = jnp.where(pair > 0, 1, 0)
                behind = jnp.where(pair < pairs - 1, 1, 0)
                extra = jnp.where(leader, 2 * chips - 1, 0)
                pl.semaphore_wait(barrier, plane - 1 + before + behind + extra)

                @pl.when(hands_map)
                def _():
                    pl.semaphore_signal(there, inc=1, device_id=(tm - 2, ser), device_id_type=MESH)

            for h in held:
                copy1(k, h).start()
        for held in groups:
            hour_terms(ours + held[0] * together_h, acc.at[k], held)
            for h in held if k else []:
                copy1(k, h).wait_recv()
                acc[k, h] = acc[k, h] + recv1[k, h]
                copy2(k, h).start()

    for item in inputs[4:]:
        item.wait()
    wide = lax.broadcasted_iota(jnp.int32, (factors, regions_ref.shape[1]), 0) % GROUPS
    mem_s[...] = jnp.where(wide == regions_ref[...], 1.0, 0.0).astype(F32).T.astype(BF16)
    gain = gain_ref[...]
    decays = jnp.exp(-frate_ref[...])
    srate = srate_ref[...]
    retain = jnp.exp(-srate)
    keep = 1.0 - retain * decays
    eye_f = jnp.where(eye, 1.0, 0.0).astype(F32)
    decay_col = jnp.sum(jnp.where(eye, decays, 0.0), axis=1, keepdims=True)
    for h in range(sets):
        copy1(0, h).wait_recv()

    maps = []
    for h in range(sets):
        total = acc[0, h] + recv1[0, h]
        for k in range(1, ys):
            copy2(k, h).wait_recv()
            total = total + recv2[k, h]
        fresh = [
            jnp.concatenate([decay_col * (eye_f - gain * inform), gain * scores], axis=0)
            for inform, scores in unpack(total)
        ]
        if together_h == 2:
            fresh[1] = compose(fresh[0], fresh[1], factors)
        if maps:
            fresh = [compose(maps[-1], item, factors) for item in fresh]
        maps += fresh
    dmap[core, 0] = maps[-1]

    def dcopy(part):
        return pltpu.make_async_remote_copy(
            dmap.at[core, part], dmap.at[core, part], ds.at[part], dr.at[part],
            device_id=(tm, y * 2 + (1 - core)), device_id_type=MESH,
        )

    dcopy(0).start()
    adds = keep * maps[0]
    for h in range(1, hours):
        adds = adds + keep * jnp.exp(-float(h) * srate) * maps[h]
    dmap[core, 1] = adds
    dcopy(1).start()
    for h in range(hours):
        cum[:, h * factors : (h + 1) * factors] = maps[h]
    dcopy(0).wait_recv()
    leads = core == 0
    first = dmap[0, 0]
    whole = compose(first, dmap[1, 0], factors)
    esend[...] = whole

    def slot_peer(slot):
        return pair * 2 + (a + slot // ys) % 2, lax.rem(y + slot % ys, ys) * 2 + core

    def slot_of(at):
        return ((a + 2 - at // ys) % 2) * ys + lax.rem(y + ys - at % ys, ys)

    def ecopy(slot):
        return pltpu.make_async_remote_copy(
            esend.at[used], emaps.at[slot, used], es.at[slot], er.at[slot],
            device_id=slot_peer(slot), device_id_type=MESH,
        )

    bcopy = pltpu.make_async_remote_copy(
        esend.at[pl.ds(factors, 1)], bin_s, bs, br,
        device_id=(1, (ys - 1) * 2), device_id_type=MESH,
    )
    heads = (pair == 0) & (g == 0) & (core == 0)
    half = factors // 2

    def lcopy(of, part):
        span = pl.ds(0, half) if part == 0 else pl.ds(half, rows - half)
        return pltpu.make_async_remote_copy(
            esend.at[span], lmaps.at[of, span], ls.at[part], lr.at[of, part],
            device_id=(1, (ys - 1) * 2), device_id_type=MESH,
        )

    helps = (pair == 0) & (g > 0) & (g < chips - 1)
    for part in range(2):

        @pl.when(helps & (core == part))
        def _(part=part):
            lcopy(g, part).start()

    @pl.when(heads)
    def _():
        bcopy.start()

    slots = [ys] + [slot for slot in range(1, chips) if slot != ys]
    for slot in slots:
        ecopy(slot).start()
    emaps[0] = whole
    dcopy(1).wait_recv()
    chip_adds = dmap[0, 1] + jnp.exp(-float(hours) * srate) * compose(first, dmap[1, 1], factors)
    ssend[...] = chip_adds

    def scopy(slot):
        return pltpu.make_async_remote_copy(
            ssend.at[used], smaps.at[slot, used], ss.at[slot], sr.at[slot],
            device_id=slot_peer(slot), device_id_type=MESH,
        )

    for slot in slots:
        scopy(slot).start()
    smaps[0] = chip_adds
    span = 2 * local
    after = (a + 1) * local
    hour_at = (
        lax.broadcasted_iota(jnp.int32, (plane, hours, factors), 0) * hours
        + lax.broadcasted_iota(jnp.int32, (plane, hours, factors), 1)
    )
    far = (hour_at - after).astype(F32)
    tail_w = jnp.where(far >= 0.0, keep[None] * jnp.exp(-jnp.maximum(far, 0.0) * srate[None]), 0.0)
    end_w = jnp.exp(-(span - after).astype(F32) * srate)
    span_w = jnp.exp(-float(span) * srate)
    def vcopy(far):
        return pltpu.make_async_remote_copy(
            vout, vin, vs.at[far - 1], vr,
            device_id=(lax.rem(tm + 2 * far, tms), ser), device_id_type=MESH,
        )

    def vstart(to):
        return pltpu.make_async_remote_copy(
            vout, vin, vls.at[to], vr,
            device_id=(2 + to // sers, to % sers), device_id_type=MESH,
        )

    def upright(vector):
        return jnp.sum(jnp.where(eye, vector, 0.0), axis=1, keepdims=True)

    def carry(column, matrix, shift):
        return jnp.sum(column * matrix, axis=0, keepdims=True) + shift

    @pl.when(leader)
    def _():
        bcopy.wait_recv()
        column = jnp.broadcast_to(upright(bin_s[...]), (factors, factors))
        for at in range(1, chips - 1):
            for part in range(2):
                lcopy(at, part).wait_recv()
            step = lmaps[at]
            column = upright(carry(column, step[:factors], step[factors : factors + 1]))
        vout[...] = carry(column, whole[:factors], whole[factors : factors + 1])
        if pairs > 1:
            for to in range(plane - 1, -1, -1):
                vstart(to).start()

    for slot in slots[:-1]:
        ecopy(slot).wait_recv()
    ecopy(slots[-1]).wait_recv()
    parts = [emaps[slot_of(at)] for at in range(chips)]
    level = parts
    while len(level) > 1:
        level = [
            compose(level[i], level[i + 1], factors) if i + 1 < len(level) else level[i]
            for i in range(0, len(level), 2)
        ]
    total = level[0]

    tcopy = pltpu.make_async_remote_copy(
        tsend.at[used], trecv.at[used], ts, tr, device_id=(lax.rem(tm + 2, tms), ser), device_id_type=MESH
    )

    @pl.when(hands_map)
    def _():
        tsend[...] = total
        tcopy.start()

    @pl.when(pair == 0)
    def _():
        vcur[...] = jnp.zeros_like(vcur)

    def forward():
        vcopy(1).wait_recv()
        vcur[...] = vin[...]

        @pl.when(odd & (pair > 1))
        def _():
            tcopy.wait_recv()
            vcur[...] = carry(upright(vin[...]), trecv[0:factors], trecv[factors : factors + 1])

        @pl.when(odd & (pair < pairs - 1))
        def _():
            vout[...] = carry(upright(vcur[...]), total[:factors], total[factors : factors + 1])

            @pl.when(pair < pairs - 2)
            def _():
                pl.semaphore_wait(there, 1)
                vcopy(2).start()

            vcopy(1).start()

    @pl.when(pair == 1)
    def _():
        forward()

    unit = jnp.concatenate([eye_f, jnp.zeros((8, factors), F32)], axis=0)
    start_map = unit
    before_chip = [parts[0]]
    for at in range(1, chips):
        start_map = jnp.where(g == at, before_chip[-1], start_map)
        if at + 1 < chips:
            before_chip.append(compose(before_chip[-1], parts[at], factors))
    start_map = jnp.where(leads, start_map, compose(start_map, first, factors))
    cums = cum[...]
    lead = dot3(start_map, cums[:factors])
    wide_at = hours * factors
    lead_s[:, :wide_at] = halves(lead[:factors])
    lead_b = lead[factors:] + cums[factors:]
    at_end = pair == pairs - 1
    for k in range(1, chips):
        scopy(k).wait_recv()
    group_adds = smaps[slot_of(0)] + jnp.where(at_end, span_w * decays, 0.0) * total
    for at in range(1, chips):
        group_adds = group_adds + jnp.exp(-float(2 * hours * at) * srate) * compose(
            before_chip[at - 1], smaps[slot_of(at)], factors
        )
    lead_s[:, wide_at:] = halves(group_adds[:factors])
    lead_b = jnp.concatenate([lead_b, group_adds[factors:]], axis=1)

    @pl.when(pair > 1)
    def _():
        forward()

    current = jnp.broadcast_to(vcur[...], (8, factors))
    filtered = dot_halves(current, lead_s[...]) + lead_b
    for h in range(hours):
        row = filtered[0:1, h * factors : (h + 1) * factors]
        fown[h : h + 1, :] = row
    shown[...] = filtered[:, hours * factors :]

    def ccopy(to, of):
        return pltpu.make_async_remote_copy(
            shown, shifts.at[of], cs.at[to], cr.at[of],
            device_id=(to * 2 + a, ser), device_id_type=MESH,
        )

    @pl.loop(0, pair)
    def _(to):
        ccopy(to, pair).start()

    fall[place_in] = fown[...]

    def fcopy(k):
        return pltpu.make_async_remote_copy(
            fown, fall.at[place_in], fs.at[k], fr.at[k],
            device_id=plane_peer(k), device_id_type=MESH,
        )

    for k in range(1, plane):
        fcopy(k).start()
    prec_root = jnp.sqrt(prec_ref[...])
    for k in range(1, plane):
        fcopy(k).wait_recv()
    together = fall[...]
    ending = decays * together[plane - 1][hours - 1 : hours]
    follow = jnp.sum(jnp.sum(together * tail_w, axis=0), axis=0, keepdims=True)

    def gather(of, held):
        total, weight = held
        ccopy(pair, of).wait_recv()
        return total + weight * shifts[of][0:1], weight * span_w

    beyond, _ = lax.fori_loop(
        pair + 1, pairs, gather, (jnp.where(at_end, ending, 0.0), jnp.ones_like(span_w))
    )
    follow = follow + end_w * beyond
    for s in range(sers - 1, -1, -1):
        block = fall[a * sers + s]
        for h in range(hours - 1, -1, -1):
            follow = keep * block[h : h + 1] + retain * follow
            smoothed_ref[s * hours + h : s * hours + h + 1, :] = follow

    fitted = jnp.dot(smoothed_ref[...].astype(BF16), lt_s[...], preferred_element_type=F32)
    standard = (readings_ref[...].astype(F32) - fitted) * prec_root
    probab = 0.5 * (1.0 + lax.erf(standard * 0.7071067811865476))
    spot = jnp.where(present_ref[...] > 0, probab * BINS - 0.5, -4.0)
    padded = table.shape[0]
    across = lax.broadcasted_iota(jnp.int32, (8, spot.shape[1]), 0)
    picks = [across % 2 == 0, across // 2 % 2 == 0, across < 4]

    def above(knot):
        if knot > BINS:
            return jnp.zeros((8, spot.shape[1]), F32)
        over = jnp.maximum(0.0, spot - knot)
        total = over[:8]
        for at in range(8, local, 8):
            total = total + over[at : at + 8]
        return total

    for at in range(0, padded, 8):
        level = [above(at + i - 1) for i in range(8)]
        for pick, shift in zip(picks, (1, 2, 4)):
            level = [
                jnp.where(pick, x, z) + pltpu.roll(jnp.where(pick, z, x), shift, 0)
                for x, z in zip(level[::2], level[1::2])
            ]
        table[at : at + 8, :] = level[0]
    sums = table[...]
    next_sums = pltpu.roll(sums, padded - 1, 0)
    bins = sums - 2.0 * next_sums + pltpu.roll(sums, padded - 2, 0)
    bins = jnp.where(lax.broadcasted_iota(jnp.int32, bins.shape, 0) < BINS, bins, 0.0)
    th, tl = split2(bins)
    tally = jnp.dot(
        jnp.concatenate([th, tl], axis=0), mem_s[...], preferred_element_type=F32
    )
    tally = tally[:padded] + tally[padded:]
    lane = lax.broadcasted_iota(jnp.int32, tally.shape, 1) // GROUPS
    sub = lax.broadcasted_iota(jnp.int32, tally.shape, 0) % 8
    tally = jnp.where(lane == sub, tally, 0.0).reshape(padded // 8, 8, tally.shape[1])
    hown[...] = jnp.sum(tally, axis=1)
    hall[me] = hown[...]

    def hsend(k):
        at = lax.rem(place_in + (plane - 1 - k % plane), plane)
        to = lax.rem(pair + (pairs - 1 - k // plane), pairs)
        pltpu.make_async_remote_copy(
            hown, hall.at[me], hs, hr,
            device_id=(to * 2 + at // sers, lax.rem(at, sers)), device_id_type=MESH,
        ).start()

    if n <= 64:
        for k in range(n - 1):
            hsend(k)
    else:
        pl.loop(0, n - 1)(hsend)

    for k in range(ys):
        for h in range(sets):
            copy1(k, h).wait_send()
            if k:
                copy2(k, h).wait_send()
    dcopy(0).wait_send()
    dcopy(1).wait_send()
    for k in range(1, chips):
        ecopy(k).wait_send()
        scopy(k).wait_send()

    @pl.when(odd & (pair < pairs - 1))
    def _():
        vcopy(1).wait_send()

    @pl.when(heads)
    def _():
        bcopy.wait_send()

    for part in range(2):

        @pl.when(helps & (core == part))
        def _(part=part):
            lcopy(g, part).wait_send()

    if pairs > 1:

        @pl.when(leader)
        def _():
            for to in range(plane):
                vstart(to).wait_send()

    @pl.when(odd & (pair < pairs - 2))
    def _():
        vcopy(2).wait_send()

    @pl.when(hands_map)
    def _():
        tcopy.wait_send()

    for k in range(1, plane):
        fcopy(k).wait_send()

    @pl.loop(0, pair)
    def _(to):
        ccopy(to, pair).wait_send()

    hdrain = pltpu.make_async_remote_copy(
        hall.at[pl.ds(0, n - 1)], hall.at[pl.ds(0, n - 1)], hs, hr,
        device_id=(tm, lax.rem(ser + 1, sers)), device_id_type=MESH,
    )
    hdrain.wait_recv()
    hdrain.wait_send()
    hist_ref[...] = jnp.sum(hall[...], axis=0)


def solution(mesh):
    tms, sers = mesh.shape["tm"], mesh.shape["series"]

    def body(readings, present, loadings, prec, gain, frate, srate, regions):
        local, series = readings.shape
        factors = loadings.shape[1]
        hours = local // sers
        n, ys = tms * sers, sers // 2
        chips = 2 * ys
        rows = factors + 8
        padded = -(-(BINS + 2) // 8) * 8
        together = 2 if hours % 2 == 0 else 1
        sets, packed_rows = hours // together, factors + 8
        vm = pltpu.VMEM
        dma = pltpu.SemaphoreType.DMA
        smoothed, packed = pl.pallas_call(
            functools.partial(kernel, tms, sers),
            out_shape=(
                vm((local, factors), F32),
                vm((padded // 8, 8 * GROUPS), F32),
            ),
            in_specs=[pl.BlockSpec(memory_space=pl.ANY)] * 8,
            out_specs=(pl.BlockSpec(memory_space=vm),) * 2,
            scratch_shapes=[
                vm((local, series), readings.dtype),
                vm((local, series), present.dtype),
                vm((series, factors), loadings.dtype),
                vm((1, series), F32),
                vm((1, factors), F32),
                vm((1, factors), F32),
                vm((1, factors), F32),
                vm((1, series), regions.dtype),
                vm((factors, series), BF16),
                vm((factors, series), BF16),
                vm((series, 8 * GROUPS), BF16),
                vm((local + 8, factors), F32),
                vm((ys, sets, packed_rows, factors), F32),
                vm((ys, sets, packed_rows, factors), F32),
                vm((ys, sets, packed_rows, factors), F32),
                vm((ys, sets, packed_rows, factors), F32),
                vm((rows, hours * factors), F32),
                vm((2, 2, rows, factors), F32),
                vm((chips, rows, factors), F32),
                vm((rows, factors), F32),
                vm((chips, rows, factors), F32),
                vm((rows, factors), F32),
                vm((3 * factors, (hours + 1) * factors), BF16),
                vm((1, factors), F32),
                vm((1, factors), F32),
                vm((1, factors), F32),
                vm((1, factors), F32),
                vm((chips, rows, factors), F32),
                vm((rows, factors), F32),
                vm((rows, factors), F32),
                vm((hours, factors), F32),
                vm((2 * sers, hours, factors), F32),
                vm((8, factors), F32),
                vm((tms // 2, 8, factors), F32),
                vm((padded, series), F32),
                vm((padded // 8, 8 * GROUPS), F32),
                vm((n, padded // 8, 8 * GROUPS), F32),
                dma((8,)),
                dma((ys, sets)),
                dma((ys, sets)),
                dma((ys, sets)),
                dma((ys, sets)),
                dma((2,)),
                dma((2,)),
                dma((chips,)),
                dma((chips,)),
                dma((chips,)),
                dma((chips,)),
                dma((2,)), dma, dma((2 * sers,)), dma((2,)), dma((chips, 2)), dma, dma, dma, dma, pltpu.SemaphoreType.REGULAR,
                dma((2 * sers,)),
                dma((2 * sers,)),
                dma((tms // 2,)),
                dma((tms // 2,)),
                dma, dma,
            ],
            compiler_params=pltpu.CompilerParams(collective_id=0, has_side_effects=True),
        )(
            readings, present, loadings, prec.reshape(1, -1), gain.reshape(1, -1),
            frate.reshape(1, -1), srate.reshape(1, -1), regions.reshape(1, -1),
        )
        scale = BINS * GROUPS / (local * tms * series * sers)
        return pl.pallas_call(
            functools.partial(finish, scale),
            out_shape=(
                jax.ShapeDtypeStruct((local, factors), F32),
                jax.ShapeDtypeStruct((GROUPS, BINS), F32),
            ),
            in_specs=[pl.BlockSpec(memory_space=vm)] * 2,
            out_specs=(pl.BlockSpec(memory_space=pl.ANY),) * 2,
            scratch_shapes=[vm((GROUPS, BINS), F32), dma((2,))],
        )(*(pltpu.with_memory_space_constraint(part, vm) for part in (smoothed, packed)))

    in_specs = (
        P("tm", "series"), P("tm", "series"), P("series", None), P("series"),
        P(), P(), P(), P("series"),
    )
    return jax.shard_map(
        body, mesh=mesh, in_specs=in_specs, out_specs=(P("tm", None), P()), check_vma=False
    )
```

```python
import functools

import jax
import jax.numpy as jnp
from jax import lax
from jax.experimental import pallas as pl
from jax.experimental.pallas import tpu as pltpu
from jax.sharding import PartitionSpec as P

BINS = 20
GROUPS = 16
MESH = pl.DeviceIdType.MESH
F32 = jnp.float32
BF16 = jnp.bfloat16


def split2(x):
    high = x.astype(BF16)
    return high, (x - high.astype(F32)).astype(BF16)


def halves(right):
    high, low = split2(right)
    return jnp.concatenate([high, low, high], axis=0)


def dot_halves(left, right):
    high, low = split2(left)
    return jnp.dot(
        jnp.concatenate([high, high, low], axis=1), right, preferred_element_type=F32
    )


def dot_t(left, right):
    return lax.dot_general(left, right, (((1,), (1,)), ((), ())), preferred_element_type=F32)


def dot3(left, right):
    return dot_halves(left, halves(right))


def compose(earlier, later, factors):
    out = dot3(earlier, later[:factors])
    return jnp.concatenate([out[:factors], out[factors:] + later[factors:]], axis=0)


LINES = -(-(BINS + 2) // 8)


def finish(scale, rows_ref, packed_ref, smoothed_ref, hist_ref, held, sems):
    rows_out = pltpu.make_async_copy(rows_ref, smoothed_ref, sems.at[0])
    rows_out.start()
    packed = packed_ref[...] * scale
    width = packed.shape[1]
    parts = []
    for at in range(LINES):
        parts += [packed[at : at + 1], jnp.zeros((7, width), F32)]
    tall = jnp.concatenate(parts + [jnp.zeros((width - 8 * LINES, width), F32)], axis=0).T
    total = tall[:GROUPS]
    for j in range(1, 8):
        total = total + pltpu.roll(tall[j * GROUPS : (j + 1) * GROUPS], j, 1)
    held[...] = total[:, :BINS]
    hist_out = pltpu.make_async_copy(held, hist_ref, sems.at[1])
    hist_out.start()
    rows_out.wait()
    hist_out.wait()


def kernel(
    tms, sers,
    readings_in, present_in, loadings_in, prec_in, gain_in, frate_in, srate_in, regions_in,
    smoothed_ref, hist_ref,
    readings_ref, present_ref, loadings_ref, prec_ref, gain_ref, frate_ref, srate_ref, regions_ref,
    lt_s, sl_s, mem_s, send1, recv1, acc, recv2, cum, dmap, emaps, esend, smaps, ssend, lead_s,
    vin, vout, vcur, bin_s, lmaps, tsend, trecv, fown, fall, shown, shifts, group_s, table, hown, hall,
    ins, s1s, s1r, s2s, s2r, ds, dr, es, er, ss, sr, vs, vr, vls, ls, lr, bs, br, ts, tr, there, fs, fr, cs, cr, hs, hr,
):
    tm, ser = lax.axis_index("tm"), lax.axis_index("series")
    y, core = ser // 2, ser % 2
    ys = sers // 2
    local = readings_ref.shape[0]
    factors = loadings_ref.shape[1]
    rows = factors + 8
    hours = local // sers
    n = tms * sers
    me = tm * sers + ser
    pair, a = tm // 2, tm % 2
    pairs = tms // 2
    chips = 2 * ys
    g = a * ys + y
    leader = (pair == 0) & (g == chips - 1) & (core == 0)
    odd = pair % 2 == 1
    hands_map = (pair % 2 == 0) & (pair > 0) & (pair < pairs - 1)

    inputs = [
        pltpu.make_async_copy(src, dst, ins.at[i])
        for i, (src, dst) in enumerate(
            [
                (loadings_in, loadings_ref), (prec_in, prec_ref), (present_in, present_ref),
                (readings_in, readings_ref), (gain_in, gain_ref), (frate_in, frate_ref),
                (srate_in, srate_ref), (regions_in, regions_ref),
            ]
        )
    ]
    for item in inputs:
        item.start()

    barrier = pltpu.get_barrier_semaphore()

    plane = 2 * sers
    place_in = a * sers + ser

    def plane_peer(k):
        at = lax.rem(place_in + k, plane)
        return pair * 2 + at // sers, lax.rem(at, sers)

    for k in range(1, plane):
        pl.semaphore_signal(barrier, inc=1, device_id=plane_peer(k), device_id_type=MESH)
    @pl.when(pair > 0)
    def _():
        pl.semaphore_signal(barrier, inc=1, device_id=(tm - 2, ser), device_id_type=MESH)

    @pl.when(pair < pairs - 1)
    def _():
        pl.semaphore_signal(barrier, inc=1, device_id=(tm + 2, ser), device_id_type=MESH)

    @pl.when((pair == 1) & ((g < chips - 1) | (core == 1)))
    def _():
        pl.semaphore_signal(barrier, inc=1, device_id=(1, (ys - 1) * 2), device_id_type=MESH)

    for item in inputs[:2]:
        item.wait()

    turned_l = loadings_ref[...].T
    lt_s[:factors] = turned_l
    sl_s[...] = (turned_l.astype(F32) * prec_ref[...]).astype(BF16)
    for item in inputs[2:4]:
        item.wait()
    lt_s[factors:] = readings_ref[...].astype(BF16)

    together_h = 2 if hours % 2 == 0 else 1
    sets = hours // together_h
    sub = lax.broadcasted_iota(jnp.int32, (factors, factors), 0)
    lane = lax.broadcasted_iota(jnp.int32, (factors, factors), 1)
    eye = sub == lane
    upper = lane > sub
    line = lax.broadcasted_iota(jnp.int32, (8, factors), 0)
    which = lax.broadcasted_iota(jnp.int32, (local, factors), 0)

    def hour_terms(base, dst, held):
        rights = []
        for j in range(len(held) * together_h):
            mask = present_ref[pl.ds(base + j, 1), :].astype(F32)
            mask = jnp.broadcast_to(mask, (16, mask.shape[1])).astype(BF16)
            right = sl_s[...].reshape(factors // 16, 16, mask.shape[1]) * mask[None]
            rights.append(right.reshape(factors, mask.shape[1]))
        out = dot_t(lt_s[...], jnp.concatenate(rights, axis=0))
        for place, h in enumerate(held):
            at = place * together_h
            first = out[:factors, at * factors : (at + 1) * factors]
            tail = jnp.zeros((8, factors), F32)
            if together_h == 2:
                second = out[:factors, (at + 1) * factors : (at + 2) * factors]
                dst[h, :factors] = jnp.where(upper, first, second)
                corner = jnp.sum(jnp.where(eye, first, 0.0), axis=0, keepdims=True)
                tail = jnp.where(line == together_h, corner, tail)
            else:
                dst[h, :factors] = first
            for j in range(together_h):
                row = out[factors:, (at + j) * factors : (at + j + 1) * factors]
                row = jnp.sum(jnp.where(which == base + at + j, row, 0.0), axis=0, keepdims=True)
                tail = jnp.where(line == j, row, tail)
            dst[h, factors:] = tail

    def unpack(packed):
        block, tail = packed[:factors], packed[factors:]
        if together_h == 1:
            matrices = [block]
        else:
            turned = block.T
            matrices = [
                jnp.where(eye, tail[together_h : together_h + 1], jnp.where(upper, block, turned)),
                jnp.where(upper, turned, block),
            ]
        return [
            (matrices[j], jnp.where(line == 0, tail[j : j + 1], 0.0)) for j in range(together_h)
        ]

    used, sent = pl.ds(0, factors + 1), pl.ds(0, factors + together_h + 1)

    def copy1(k, h):
        return pltpu.make_async_remote_copy(
            send1.at[k, h, sent], recv1.at[k, h, sent], s1s.at[k, h], s1r.at[k, h],
            device_id=(tm, y * 2 + (1 - core)), device_id_type=MESH,
        )

    def copy2(k, h):
        return pltpu.make_async_remote_copy(
            acc.at[k, h, sent], recv2.at[k, h, sent], s2s.at[k, h], s2r.at[k, h],
            device_id=(tm, lax.rem(y + k, ys) * 2 + core), device_id_type=MESH,
        )

    order = list(range(1, ys)) + [0]
    for place, k in enumerate(order):
        owner = lax.rem(y + k, ys) * 2
        theirs, ours = (owner + (1 - core)) * hours, (owner + core) * hours
        groups = [[h] for h in range(sets)] if k else [list(range(sets))]
        for held in groups:
            hour_terms(theirs + held[0] * together_h, send1.at[k], held)
            if place == 0 and held[0] == 0:
                before = jnp.where(pair > 0, 1, 0)
                behind = jnp.where(pair < pairs - 1, 1, 0)
                extra = jnp.where(leader, 2 * chips - 1, 0)
                pl.semaphore_wait(barrier, plane - 1 + before + behind + extra)

                @pl.when(hands_map)
                def _():
                    pl.semaphore_signal(there, inc=1, device_id=(tm - 2, ser), device_id_type=MESH)

            for h in held:
                copy1(k, h).start()
        for held in groups:
            hour_terms(ours + held[0] * together_h, acc.at[k], held)
            for h in held if k else []:
                copy1(k, h).wait_recv()
                acc[k, h] = acc[k, h] + recv1[k, h]
                copy2(k, h).start()

    for item in inputs[4:]:
        item.wait()
    wide = lax.broadcasted_iota(jnp.int32, (factors, regions_ref.shape[1]), 0) % GROUPS
    mem_s[...] = jnp.where(wide == regions_ref[...], 1.0, 0.0).astype(F32).T.astype(BF16)
    gain = gain_ref[...]
    decays = jnp.exp(-frate_ref[...])
    srate = srate_ref[...]
    retain = jnp.exp(-srate)
    keep = 1.0 - retain * decays
    eye_f = jnp.where(eye, 1.0, 0.0).astype(F32)
    decay_col = jnp.sum(jnp.where(eye, decays, 0.0), axis=1, keepdims=True)
    for h in range(sets):
        copy1(0, h).wait_recv()

    maps = []
    for h in range(sets):
        total = acc[0, h] + recv1[0, h]
        for k in range(1, ys):
            copy2(k, h).wait_recv()
            total = total + recv2[k, h]
        fresh = [
            jnp.concatenate([decay_col * (eye_f - gain * inform), gain * scores], axis=0)
            for inform, scores in unpack(total)
        ]
        if together_h == 2:
            fresh[1] = compose(fresh[0], fresh[1], factors)
        if maps:
            fresh = [compose(maps[-1], item, factors) for item in fresh]
        maps += fresh
    dmap[core, 0] = maps[-1]

    def dcopy(part):
        return pltpu.make_async_remote_copy(
            dmap.at[core, part], dmap.at[core, part], ds.at[part], dr.at[part],
            device_id=(tm, y * 2 + (1 - core)), device_id_type=MESH,
        )

    dcopy(0).start()
    adds = keep * maps[0]
    for h in range(1, hours):
        adds = adds + keep * jnp.exp(-float(h) * srate) * maps[h]
    dmap[core, 1] = adds
    dcopy(1).start()
    for h in range(hours):
        cum[:, h * factors : (h + 1) * factors] = maps[h]
    dcopy(0).wait_recv()
    leads = core == 0
    first = dmap[0, 0]
    whole = compose(first, dmap[1, 0], factors)
    esend[...] = whole

    def slot_peer(slot):
        return pair * 2 + (a + slot // ys) % 2, lax.rem(y + slot % ys, ys) * 2 + core

    def slot_of(at):
        return ((a + 2 - at // ys) % 2) * ys + lax.rem(y + ys - at % ys, ys)

    def ecopy(slot):
        return pltpu.make_async_remote_copy(
            esend.at[used], emaps.at[slot, used], es.at[slot], er.at[slot],
            device_id=slot_peer(slot), device_id_type=MESH,
        )

    bcopy = pltpu.make_async_remote_copy(
        esend.at[pl.ds(factors, 1)], bin_s, bs, br,
        device_id=(1, (ys - 1) * 2), device_id_type=MESH,
    )
    heads = (pair == 0) & (g == 0) & (core == 0)
    half = factors // 2

    def lcopy(of, part):
        span = pl.ds(0, half) if part == 0 else pl.ds(half, rows - half)
        return pltpu.make_async_remote_copy(
            esend.at[span], lmaps.at[of, span], ls.at[part], lr.at[of, part],
            device_id=(1, (ys - 1) * 2), device_id_type=MESH,
        )

    helps = (pair == 0) & (g > 0) & (g < chips - 1)
    for part in range(2):

        @pl.when(helps & (core == part))
        def _(part=part):
            lcopy(g, part).start()

    @pl.when(heads)
    def _():
        bcopy.start()

    slots = [ys] + [slot for slot in range(1, chips) if slot != ys]
    for slot in slots:
        ecopy(slot).start()
    emaps[0] = whole
    dcopy(1).wait_recv()
    chip_adds = dmap[0, 1] + jnp.exp(-float(hours) * srate) * compose(first, dmap[1, 1], factors)
    ssend[...] = chip_adds

    def scopy(slot, part):
        span = pl.ds(0, half) if part == 0 else pl.ds(half, half + 1)
        row, column = slot_peer(slot)
        return pltpu.make_async_remote_copy(
            ssend.at[span], smaps.at[slot, span], ss.at[slot], sr.at[slot, part],
            device_id=(row, column - core), device_id_type=MESH,
        )

    sums = (core == 0) & (pair > 0)
    for part in range(2):

        @pl.when((pair > 0) & (core == part))
        def _(part=part):
            for slot in slots:
                scopy(slot, part).start()

    smaps[0] = chip_adds
    span = 2 * local
    after = (a + 1) * local
    hour_at = (
        lax.broadcasted_iota(jnp.int32, (plane, hours, factors), 0) * hours
        + lax.broadcasted_iota(jnp.int32, (plane, hours, factors), 1)
    )
    far = (hour_at - after).astype(F32)
    tail_w = jnp.where(far >= 0.0, keep[None] * jnp.exp(-jnp.maximum(far, 0.0) * srate[None]), 0.0)
    end_w = jnp.exp(-(span - after).astype(F32) * srate)
    span_w = jnp.exp(-float(span) * srate)
    def vcopy(far):
        return pltpu.make_async_remote_copy(
            vout, vin, vs.at[far - 1], vr,
            device_id=(lax.rem(tm + 2 * far, tms), ser), device_id_type=MESH,
        )

    def vstart(to):
        return pltpu.make_async_remote_copy(
            vout, vin, vls.at[to], vr,
            device_id=(2 + to // sers, to % sers), device_id_type=MESH,
        )

    def upright(vector):
        return jnp.sum(jnp.where(eye, vector, 0.0), axis=1, keepdims=True)

    def carry(column, matrix, shift):
        return jnp.sum(column * matrix, axis=0, keepdims=True) + shift

    @pl.when(leader)
    def _():
        bcopy.wait_recv()
        column = jnp.broadcast_to(upright(bin_s[...]), (factors, factors))
        for at in range(1, chips - 1):
            for part in range(2):
                lcopy(at, part).wait_recv()
            step = lmaps[at]
            column = upright(carry(column, step[:factors], step[factors : factors + 1]))
        vout[...] = carry(column, whole[:factors], whole[factors : factors + 1])
        if pairs > 1:
            for to in range(plane - 1, -1, -1):
                vstart(to).start()

    for slot in slots[:-1]:
        ecopy(slot).wait_recv()
    ecopy(slots[-1]).wait_recv()
    parts = [emaps[slot_of(at)] for at in range(chips)]
    level = parts
    while len(level) > 1:
        level = [
            compose(level[i], level[i + 1], factors) if i + 1 < len(level) else level[i]
            for i in range(0, len(level), 2)
        ]
    total = level[0]

    tcopy = pltpu.make_async_remote_copy(
        tsend.at[used], trecv.at[used], ts, tr, device_id=(lax.rem(tm + 2, tms), ser), device_id_type=MESH
    )

    @pl.when(hands_map)
    def _():
        tsend[...] = total
        tcopy.start()

    @pl.when(pair == 0)
    def _():
        vcur[...] = jnp.zeros_like(vcur)

    def forward():
        vcopy(1).wait_recv()
        vcur[...] = vin[...]

        @pl.when(odd & (pair > 1))
        def _():
            tcopy.wait_recv()
            vcur[...] = carry(upright(vin[...]), trecv[0:factors], trecv[factors : factors + 1])

        @pl.when(odd & (pair < pairs - 1))
        def _():
            vout[...] = carry(upright(vcur[...]), total[:factors], total[factors : factors + 1])

            @pl.when(pair < pairs - 2)
            def _():
                pl.semaphore_wait(there, 1)
                vcopy(2).start()

            vcopy(1).start()

    @pl.when(pair == 1)
    def _():
        forward()

    unit = jnp.concatenate([eye_f, jnp.zeros((8, factors), F32)], axis=0)
    start_map = unit
    before_chip = [parts[0]]
    for at in range(1, chips):
        start_map = jnp.where(g == at, before_chip[-1], start_map)
        if at + 1 < chips:
            before_chip.append(compose(before_chip[-1], parts[at], factors))
    start_map = jnp.where(leads, start_map, compose(start_map, first, factors))
    cums = cum[...]
    lead = dot3(start_map, cums[:factors])
    lead_s[...] = halves(lead[:factors])
    lead_b = lead[factors:] + cums[factors:]
    at_end = pair == pairs - 1

    @pl.when(sums)
    def _():
        for slot in range(1, chips):
            for part in range(2):
                scopy(slot, part).wait_recv()
        group_adds = smaps[slot_of(0)] + jnp.where(at_end, span_w * decays, 0.0) * total
        for at in range(1, chips):
            group_adds = group_adds + jnp.exp(-float(2 * hours * at) * srate) * compose(
                before_chip[at - 1], smaps[slot_of(at)], factors
            )
        group_s[...] = group_adds

    @pl.when(pair > 1)
    def _():
        forward()

    def ccopy(to, of, side):
        return pltpu.make_async_remote_copy(
            shown, shifts.at[of], cs.at[to, side], cr.at[of],
            device_id=(to * 2 + a, y * 2 + side), device_id_type=MESH,
        )

    @pl.when(sums)
    def _():
        shown[...] = carry(
            upright(vcur[...]), group_s[0:factors], group_s[factors : factors + 1]
        )

        @pl.loop(0, pair)
        def _(to):
            for side in range(2):
                ccopy(to, pair, side).start()

    current = jnp.broadcast_to(vcur[...], (8, factors))
    filtered = dot_halves(current, lead_s[...]) + lead_b
    for h in range(hours):
        row = filtered[0:1, h * factors : (h + 1) * factors]
        fown[h : h + 1, :] = row
    fall[place_in] = fown[...]

    def fcopy(k):
        return pltpu.make_async_remote_copy(
            fown, fall.at[place_in], fs.at[k], fr.at[k],
            device_id=plane_peer(k), device_id_type=MESH,
        )

    for k in range(1, plane):
        fcopy(k).start()
    prec_root = jnp.sqrt(prec_ref[...])
    for k in range(1, plane):
        fcopy(k).wait_recv()
    together = fall[...]
    ending = decays * together[plane - 1][hours - 1 : hours]
    tail = jnp.sum(jnp.sum(together * tail_w, axis=0), axis=0, keepdims=True)
    rows_in = keep * jnp.concatenate([fall[a * sers + s] for s in range(sers)], axis=0)
    row_at = lax.broadcasted_iota(jnp.int32, (local, factors), 0)
    reach = 1
    while reach < local:
        later = jnp.where(row_at < local - reach, pltpu.roll(rows_in, local - reach, 0), 0.0)
        rows_in = rows_in + jnp.exp(-float(reach) * srate) * later
        reach *= 2
    fade = jnp.exp(-(local - row_at).astype(F32) * srate)
    rows_in = rows_in + fade * tail

    def gather(of, held):
        total, weight = held
        ccopy(pair, of, 0).wait_recv()
        return total + weight * shifts[of], weight * span_w

    beyond, _ = lax.fori_loop(
        pair + 1, pairs, gather, (jnp.where(at_end, ending, 0.0), jnp.ones_like(span_w))
    )
    smoothed_rows = rows_in + fade * (end_w * beyond)
    smoothed_ref[...] = smoothed_rows
    fitted = jnp.dot(smoothed_rows.astype(BF16), lt_s[:factors], preferred_element_type=F32)
    standard = (readings_ref[...].astype(F32) - fitted) * prec_root
    probab = 0.5 * (1.0 + lax.erf(standard * 0.7071067811865476))
    spot = jnp.where(present_ref[...] > 0, probab * BINS - 0.5, -4.0)
    padded = table.shape[0]
    across = lax.broadcasted_iota(jnp.int32, (8, spot.shape[1]), 0)
    picks = [across % 2 == 0, across // 2 % 2 == 0, across < 4]

    def above(knot):
        if knot > BINS:
            return jnp.zeros((8, spot.shape[1]), F32)
        over = jnp.maximum(0.0, spot - knot)
        total = over[:8]
        for at in range(8, local, 8):
            total = total + over[at : at + 8]
        return total

    for at in range(0, padded, 8):
        level = [above(at + i - 1) for i in range(8)]
        for pick, shift in zip(picks, (1, 2, 4)):
            level = [
                jnp.where(pick, x, z) + pltpu.roll(jnp.where(pick, z, x), shift, 0)
                for x, z in zip(level[::2], level[1::2])
            ]
        table[at : at + 8, :] = level[0]
    knots = table[...]
    next_knots = pltpu.roll(knots, padded - 1, 0)
    bins = knots - 2.0 * next_knots + pltpu.roll(knots, padded - 2, 0)
    bins = jnp.where(lax.broadcasted_iota(jnp.int32, bins.shape, 0) < BINS, bins, 0.0)
    th, tl = split2(bins)
    tally = jnp.dot(
        jnp.concatenate([th, tl], axis=0), mem_s[...], preferred_element_type=F32
    )
    tally = tally[:padded] + tally[padded:]
    lane = lax.broadcasted_iota(jnp.int32, tally.shape, 1) // GROUPS
    sub = lax.broadcasted_iota(jnp.int32, tally.shape, 0) % 8
    tally = jnp.where(lane == sub, tally, 0.0).reshape(padded // 8, 8, tally.shape[1])
    hown[...] = jnp.sum(tally, axis=1)
    hall[me] = hown[...]

    def hsend(k):
        at = lax.rem(place_in + (plane - 1 - k % plane), plane)
        turn = k // plane
        step = jnp.where(pair * 2 < pairs, pairs - 1 - turn, lax.rem(turn + 1, pairs))
        to = lax.rem(pair + step, pairs)
        pltpu.make_async_remote_copy(
            hown, hall.at[me], hs, hr,
            device_id=(to * 2 + at // sers, lax.rem(at, sers)), device_id_type=MESH,
        ).start()

    if n <= 64:
        for k in range(n - 1):
            hsend(k)
    else:
        pl.loop(0, n - 1)(hsend)

    for k in range(ys):
        for h in range(sets):
            copy1(k, h).wait_send()
            if k:
                copy2(k, h).wait_send()
    dcopy(0).wait_send()
    dcopy(1).wait_send()
    for k in range(1, chips):
        ecopy(k).wait_send()

    @pl.when(odd & (pair < pairs - 1))
    def _():
        vcopy(1).wait_send()

    for part in range(2):

        @pl.when((pair > 0) & (core == part))
        def _(part=part):
            for slot in slots:
                scopy(slot, part).wait_send()

    @pl.when(heads)
    def _():
        bcopy.wait_send()

    for part in range(2):

        @pl.when(helps & (core == part))
        def _(part=part):
            lcopy(g, part).wait_send()

    if pairs > 1:

        @pl.when(leader)
        def _():
            for to in range(plane):
                vstart(to).wait_send()

    @pl.when(odd & (pair < pairs - 2))
    def _():
        vcopy(2).wait_send()

    @pl.when(hands_map)
    def _():
        tcopy.wait_send()

    for k in range(1, plane):
        fcopy(k).wait_send()

    @pl.when(sums)
    def _():
        @pl.loop(0, pair)
        def _(to):
            for side in range(2):
                ccopy(to, pair, side).wait_send()

    hdrain = pltpu.make_async_remote_copy(
        hall.at[pl.ds(0, n - 1)], hall.at[pl.ds(0, n - 1)], hs, hr,
        device_id=(tm, lax.rem(ser + 1, sers)), device_id_type=MESH,
    )
    hdrain.wait_recv()
    hdrain.wait_send()
    hist_ref[...] = jnp.sum(hall[...], axis=0)


def solution(mesh):
    tms, sers = mesh.shape["tm"], mesh.shape["series"]

    def body(readings, present, loadings, prec, gain, frate, srate, regions):
        local, series = readings.shape
        factors = loadings.shape[1]
        hours = local // sers
        n, ys = tms * sers, sers // 2
        chips = 2 * ys
        rows = factors + 8
        padded = -(-(BINS + 2) // 8) * 8
        together = 2 if hours % 2 == 0 else 1
        sets, packed_rows = hours // together, factors + 8
        vm = pltpu.VMEM
        dma = pltpu.SemaphoreType.DMA
        smoothed, packed = pl.pallas_call(
            functools.partial(kernel, tms, sers),
            out_shape=(
                vm((local, factors), F32),
                vm((padded // 8, 8 * GROUPS), F32),
            ),
            in_specs=[pl.BlockSpec(memory_space=pl.ANY)] * 8,
            out_specs=(pl.BlockSpec(memory_space=vm),) * 2,
            scratch_shapes=[
                vm((local, series), readings.dtype),
                vm((local, series), present.dtype),
                vm((series, factors), loadings.dtype),
                vm((1, series), F32),
                vm((1, factors), F32),
                vm((1, factors), F32),
                vm((1, factors), F32),
                vm((1, series), regions.dtype),
                vm((factors + local, series), BF16),
                vm((factors, series), BF16),
                vm((series, 8 * GROUPS), BF16),
                vm((ys, sets, packed_rows, factors), F32),
                vm((ys, sets, packed_rows, factors), F32),
                vm((ys, sets, packed_rows, factors), F32),
                vm((ys, sets, packed_rows, factors), F32),
                vm((rows, hours * factors), F32),
                vm((2, 2, rows, factors), F32),
                vm((chips, rows, factors), F32),
                vm((rows, factors), F32),
                vm((chips, rows, factors), F32),
                vm((rows, factors), F32),
                vm((3 * factors, hours * factors), BF16),
                vm((1, factors), F32),
                vm((1, factors), F32),
                vm((1, factors), F32),
                vm((1, factors), F32),
                vm((chips, rows, factors), F32),
                vm((rows, factors), F32),
                vm((rows, factors), F32),
                vm((hours, factors), F32),
                vm((2 * sers, hours, factors), F32),
                vm((1, factors), F32),
                vm((tms // 2, 1, factors), F32),
                vm((rows, factors), F32),
                vm((padded, series), F32),
                vm((padded // 8, 8 * GROUPS), F32),
                vm((n, padded // 8, 8 * GROUPS), F32),
                dma((8,)),
                dma((ys, sets)),
                dma((ys, sets)),
                dma((ys, sets)),
                dma((ys, sets)),
                dma((2,)),
                dma((2,)),
                dma((chips,)),
                dma((chips,)),
                dma((chips,)),
                dma((chips, 2)),
                dma((2,)), dma, dma((2 * sers,)), dma((2,)), dma((chips, 2)), dma, dma, dma, dma, pltpu.SemaphoreType.REGULAR,
                dma((2 * sers,)),
                dma((2 * sers,)),
                dma((tms // 2, 2)),
                dma((tms // 2,)),
                dma, dma,
            ],
            compiler_params=pltpu.CompilerParams(collective_id=0, has_side_effects=True),
        )(
            readings, present, loadings, prec.reshape(1, -1), gain.reshape(1, -1),
            frate.reshape(1, -1), srate.reshape(1, -1), regions.reshape(1, -1),
        )
        scale = BINS * GROUPS / (local * tms * series * sers)
        return pl.pallas_call(
            functools.partial(finish, scale),
            out_shape=(
                jax.ShapeDtypeStruct((local, factors), F32),
                jax.ShapeDtypeStruct((GROUPS, BINS), F32),
            ),
            in_specs=[pl.BlockSpec(memory_space=vm)] * 2,
            out_specs=(pl.BlockSpec(memory_space=pl.ANY),) * 2,
            scratch_shapes=[vm((GROUPS, BINS), F32), dma((2,))],
        )(*(pltpu.with_memory_space_constraint(part, vm) for part in (smoothed, packed)))

    in_specs = (
        P("tm", "series"), P("tm", "series"), P("series", None), P("series"),
        P(), P(), P(), P("series"),
    )
    return jax.shard_map(
        body, mesh=mesh, in_specs=in_specs, out_specs=(P("tm", None), P()), check_vma=False
    )
```

```python
import functools

import jax
import jax.numpy as jnp
from jax import lax
from jax.experimental import pallas as pl
from jax.experimental.pallas import tpu as pltpu
from jax.sharding import PartitionSpec as P

BINS = 20
GROUPS = 16
MESH = pl.DeviceIdType.MESH
F32 = jnp.float32
BF16 = jnp.bfloat16


def split2(x):
    high = x.astype(BF16)
    return high, (x - high.astype(F32)).astype(BF16)


def halves(right):
    high, low = split2(right)
    return jnp.concatenate([high, low, high], axis=0)


def dot_halves(left, right):
    high, low = split2(left)
    return jnp.dot(
        jnp.concatenate([high, high, low], axis=1), right, preferred_element_type=F32
    )


def dot_t(left, right):
    return lax.dot_general(left, right, (((1,), (1,)), ((), ())), preferred_element_type=F32)


def dot3(left, right):
    return dot_halves(left, halves(right))


def compose(earlier, later, factors):
    out = dot3(earlier, later[:factors])
    return jnp.concatenate([out[:factors], out[factors:] + later[factors:]], axis=0)


LINES = -(-(BINS + 2) // 8)


def finish(scale, rows_ref, packed_ref, smoothed_ref, hist_ref, held, sems):
    rows_out = pltpu.make_async_copy(rows_ref, smoothed_ref, sems.at[0])
    rows_out.start()
    packed = packed_ref[...] * scale
    width = packed.shape[1]
    parts = []
    for at in range(LINES):
        parts += [packed[at : at + 1], jnp.zeros((7, width), F32)]
    tall = jnp.concatenate(parts + [jnp.zeros((width - 8 * LINES, width), F32)], axis=0).T
    total = tall[:GROUPS]
    for j in range(1, 8):
        total = total + pltpu.roll(tall[j * GROUPS : (j + 1) * GROUPS], j, 1)
    held[...] = total[:, :BINS]
    hist_out = pltpu.make_async_copy(held, hist_ref, sems.at[1])
    hist_out.start()
    rows_out.wait()
    hist_out.wait()


def kernel(
    tms, sers,
    readings_in, present_in, loadings_in, prec_in, gain_in, frate_in, srate_in, regions_in,
    smoothed_ref, hist_ref,
    readings_ref, present_ref, loadings_ref, prec_ref, gain_ref, frate_ref, srate_ref, regions_ref,
    lt_s, sl_s, mem_s, send1, recv1, acc, recv2, cum, dmap, emaps, esend, smaps, ssend, lead_s,
    vin, vout, vcur, bin_s, lmaps, tsend, trecv, fown, fall, shown, shifts, group_s, table, hown, hall,
    ins, s1s, s1r, s2s, s2r, ds, dr, es, er, ss, sr, vs, vr, vls, ls, lr, bs, br, ts, tr, there, fs, fr, cs, cr, hs, hr,
):
    tm, ser = lax.axis_index("tm"), lax.axis_index("series")
    y, core = ser // 2, ser % 2
    ys = sers // 2
    local = readings_ref.shape[0]
    factors = loadings_ref.shape[1]
    rows = factors + 8
    hours = local // sers
    n = tms * sers
    me = tm * sers + ser
    pair, a = tm // 2, tm % 2
    pairs = tms // 2
    chips = 2 * ys
    g = a * ys + y
    leader = (pair == 0) & (g == chips - 1) & (core == 0)
    odd = pair % 2 == 1
    hands_map = (pair % 2 == 0) & (pair > 0) & (pair < pairs - 1)

    inputs = [
        pltpu.make_async_copy(src, dst, ins.at[i])
        for i, (src, dst) in enumerate(
            [
                (loadings_in, loadings_ref), (prec_in, prec_ref), (present_in, present_ref),
                (readings_in, readings_ref), (gain_in, gain_ref), (frate_in, frate_ref),
                (srate_in, srate_ref), (regions_in, regions_ref),
            ]
        )
    ]
    for item in inputs:
        item.start()

    barrier = pltpu.get_barrier_semaphore()

    plane = 2 * sers
    place_in = a * sers + ser

    def plane_peer(k):
        at = lax.rem(place_in + k, plane)
        return pair * 2 + at // sers, lax.rem(at, sers)

    for k in range(1, plane):
        pl.semaphore_signal(barrier, inc=1, device_id=plane_peer(k), device_id_type=MESH)
    @pl.when(pair > 0)
    def _():
        pl.semaphore_signal(barrier, inc=1, device_id=(tm - 2, ser), device_id_type=MESH)

    @pl.when((pair > 0) & (core == 1))
    def _():
        pl.semaphore_signal(barrier, inc=1, device_id=(tm - 2, y * 2), device_id_type=MESH)

    @pl.when(pair < pairs - 1)
    def _():
        pl.semaphore_signal(barrier, inc=1, device_id=(tm + 2, ser), device_id_type=MESH)

    @pl.when((pair == 1) & ((g < chips - 1) | (core == 1)))
    def _():
        pl.semaphore_signal(barrier, inc=1, device_id=(1, (ys - 1) * 2), device_id_type=MESH)

    for item in inputs[:2]:
        item.wait()

    turned_l = loadings_ref[...].T
    lt_s[:factors] = turned_l
    sl_s[...] = (turned_l.astype(F32) * prec_ref[...]).astype(BF16)
    for item in inputs[2:4]:
        item.wait()
    lt_s[factors:] = readings_ref[...].astype(BF16)

    together_h = 2 if hours % 2 == 0 else 1
    sets = hours // together_h
    sub = lax.broadcasted_iota(jnp.int32, (factors, factors), 0)
    lane = lax.broadcasted_iota(jnp.int32, (factors, factors), 1)
    eye = sub == lane
    upper = lane > sub
    line = lax.broadcasted_iota(jnp.int32, (8, factors), 0)
    which = lax.broadcasted_iota(jnp.int32, (local, factors), 0)

    def hour_terms(base, dst, held):
        rights = []
        for j in range(len(held) * together_h):
            mask = present_ref[pl.ds(base + j, 1), :].astype(F32)
            mask = jnp.broadcast_to(mask, (16, mask.shape[1])).astype(BF16)
            right = sl_s[...].reshape(factors // 16, 16, mask.shape[1]) * mask[None]
            rights.append(right.reshape(factors, mask.shape[1]))
        out = dot_t(lt_s[...], jnp.concatenate(rights, axis=0))
        for place, h in enumerate(held):
            at = place * together_h
            first = out[:factors, at * factors : (at + 1) * factors]
            tail = jnp.zeros((8, factors), F32)
            if together_h == 2:
                second = out[:factors, (at + 1) * factors : (at + 2) * factors]
                dst[h, :factors] = jnp.where(upper, first, second)
                corner = jnp.sum(jnp.where(eye, first, 0.0), axis=0, keepdims=True)
                tail = jnp.where(line == together_h, corner, tail)
            else:
                dst[h, :factors] = first
            for j in range(together_h):
                row = out[factors:, (at + j) * factors : (at + j + 1) * factors]
                row = jnp.sum(jnp.where(which == base + at + j, row, 0.0), axis=0, keepdims=True)
                tail = jnp.where(line == j, row, tail)
            dst[h, factors:] = tail

    def unpack(packed):
        block, tail = packed[:factors], packed[factors:]
        if together_h == 1:
            matrices = [block]
        else:
            turned = block.T
            matrices = [
                jnp.where(eye, tail[together_h : together_h + 1], jnp.where(upper, block, turned)),
                jnp.where(upper, turned, block),
            ]
        return [
            (matrices[j], jnp.where(line == 0, tail[j : j + 1], 0.0)) for j in range(together_h)
        ]

    used, sent = pl.ds(0, factors + 1), pl.ds(0, factors + together_h + 1)

    def copy1(k, h):
        return pltpu.make_async_remote_copy(
            send1.at[k, h, sent], recv1.at[k, h, sent], s1s.at[k, h], s1r.at[k, h],
            device_id=(tm, y * 2 + (1 - core)), device_id_type=MESH,
        )

    def copy2(k, h):
        return pltpu.make_async_remote_copy(
            acc.at[k, h, sent], recv2.at[k, h, sent], s2s.at[k, h], s2r.at[k, h],
            device_id=(tm, lax.rem(y + k, ys) * 2 + core), device_id_type=MESH,
        )

    order = list(range(1, ys)) + [0]
    for place, k in enumerate(order):
        owner = lax.rem(y + k, ys) * 2
        theirs, ours = (owner + (1 - core)) * hours, (owner + core) * hours
        groups = [[h] for h in range(sets)] if k else [list(range(sets))]
        for held in groups:
            hour_terms(theirs + held[0] * together_h, send1.at[k], held)
            if place == 0 and held[0] == 0:
                before = jnp.where(pair > 0, 1, 0)
                behind = jnp.where(pair < pairs - 1, 2 - core, 0)
                extra = jnp.where(leader, 2 * chips - 1, 0)
                pl.semaphore_wait(barrier, plane - 1 + before + behind + extra)

                @pl.when(hands_map & (core == 0))
                def _():
                    pl.semaphore_signal(there, inc=1, device_id=(tm - 2, y * 2), device_id_type=MESH)

            for h in held:
                copy1(k, h).start()
        for held in groups:
            hour_terms(ours + held[0] * together_h, acc.at[k], held)
            for h in held if k else []:
                copy1(k, h).wait_recv()
                acc[k, h] = acc[k, h] + recv1[k, h]
                copy2(k, h).start()

    for item in inputs[4:]:
        item.wait()
    wide = lax.broadcasted_iota(jnp.int32, (factors, regions_ref.shape[1]), 0) % GROUPS
    mem_s[...] = jnp.where(wide == regions_ref[...], 1.0, 0.0).astype(F32).T.astype(BF16)
    gain = gain_ref[...]
    decays = jnp.exp(-frate_ref[...])
    srate = srate_ref[...]
    retain = jnp.exp(-srate)
    keep = 1.0 - retain * decays
    eye_f = jnp.where(eye, 1.0, 0.0).astype(F32)
    decay_col = jnp.sum(jnp.where(eye, decays, 0.0), axis=1, keepdims=True)
    for h in range(sets):
        copy1(0, h).wait_recv()

    maps = []
    for h in range(sets):
        total = acc[0, h] + recv1[0, h]
        for k in range(1, ys):
            copy2(k, h).wait_recv()
            total = total + recv2[k, h]
        fresh = [
            jnp.concatenate([decay_col * (eye_f - gain * inform), gain * scores], axis=0)
            for inform, scores in unpack(total)
        ]
        if together_h == 2:
            fresh[1] = compose(fresh[0], fresh[1], factors)
        if maps:
            fresh = [compose(maps[-1], item, factors) for item in fresh]
        maps += fresh
    dmap[core, 0] = maps[-1]

    def dcopy(part):
        return pltpu.make_async_remote_copy(
            dmap.at[core, part], dmap.at[core, part], ds.at[part], dr.at[part],
            device_id=(tm, y * 2 + (1 - core)), device_id_type=MESH,
        )

    dcopy(0).start()
    adds = keep * maps[0]
    for h in range(1, hours):
        adds = adds + keep * jnp.exp(-float(h) * srate) * maps[h]
    dmap[core, 1] = adds
    dcopy(1).start()
    for h in range(hours):
        cum[:, h * factors : (h + 1) * factors] = maps[h]
    dcopy(0).wait_recv()
    leads = core == 0
    first = dmap[0, 0]
    whole = compose(first, dmap[1, 0], factors)
    esend[...] = whole

    def slot_peer(slot):
        return pair * 2 + (a + slot // ys) % 2, lax.rem(y + slot % ys, ys) * 2 + core

    def slot_of(at):
        return ((a + 2 - at // ys) % 2) * ys + lax.rem(y + ys - at % ys, ys)

    half = factors // 2
    spans = [pl.ds(0, half), pl.ds(half, half + 1)]

    def ecopy(slot, side, part):
        row, column = slot_peer(slot)
        return pltpu.make_async_remote_copy(
            esend.at[spans[part]], emaps.at[slot, spans[part]],
            es.at[slot, side], er.at[slot, part],
            device_id=(row, column - core + side), device_id_type=MESH,
        )

    bcopy = pltpu.make_async_remote_copy(
        esend.at[pl.ds(factors, 1)], bin_s, bs, br,
        device_id=(1, (ys - 1) * 2), device_id_type=MESH,
    )
    heads = (pair == 0) & (g == 0) & (core == 0)

    def lcopy(of, part):
        span = pl.ds(0, half) if part == 0 else pl.ds(half, rows - half)
        return pltpu.make_async_remote_copy(
            esend.at[span], lmaps.at[of, span], ls.at[part], lr.at[of, part],
            device_id=(1, (ys - 1) * 2), device_id_type=MESH,
        )

    helps = (pair == 0) & (g > 0) & (g < chips - 1)
    for part in range(2):

        @pl.when(helps & (core == part))
        def _(part=part):
            lcopy(g, part).start()

    @pl.when(heads)
    def _():
        bcopy.start()

    slots = [ys] + [slot for slot in range(1, chips) if slot != ys]
    for part in range(2):

        @pl.when((core == part) & (pair > 0))
        def _(part=part):
            for side in range(2):
                for slot in slots:
                    ecopy(slot, side, part).start()

        @pl.when((core == part) & (pair == 0))
        def _(part=part):
            for slot in slots:
                for side in range(2):
                    ecopy(slot, side, part).start()

    emaps[0] = whole
    dcopy(1).wait_recv()
    chip_adds = dmap[0, 1] + jnp.exp(-float(hours) * srate) * compose(first, dmap[1, 1], factors)
    ssend[...] = chip_adds

    def scopy(slot, part):
        span = pl.ds(0, half) if part == 0 else pl.ds(half, half + 1)
        row, column = slot_peer(slot)
        return pltpu.make_async_remote_copy(
            ssend.at[span], smaps.at[slot, span], ss.at[slot], sr.at[slot, part],
            device_id=(row, column - core), device_id_type=MESH,
        )

    sums = (core == 0) & (pair > 0)
    for part in range(2):

        @pl.when((pair > 0) & (core == part))
        def _(part=part):
            for slot in slots:
                scopy(slot, part).start()

    smaps[0] = chip_adds
    span = 2 * local
    after = (a + 1) * local
    hour_at = (
        lax.broadcasted_iota(jnp.int32, (plane, hours, factors), 0) * hours
        + lax.broadcasted_iota(jnp.int32, (plane, hours, factors), 1)
    )
    far = (hour_at - after).astype(F32)
    tail_w = jnp.where(far >= 0.0, keep[None] * jnp.exp(-jnp.maximum(far, 0.0) * srate[None]), 0.0)
    end_w = jnp.exp(-(span - after).astype(F32) * srate)
    span_w = jnp.exp(-float(span) * srate)
    def vcopy(far, side):
        return pltpu.make_async_remote_copy(
            vout, vin, vs.at[far - 1, side], vr,
            device_id=(lax.rem(tm + 2 * far, tms), y * 2 + side), device_id_type=MESH,
        )

    def vstart(to):
        return pltpu.make_async_remote_copy(
            vout, vin, vls.at[to], vr,
            device_id=(2 + to // sers, to % sers), device_id_type=MESH,
        )

    def upright(vector):
        return jnp.sum(jnp.where(eye, vector, 0.0), axis=1, keepdims=True)

    def carry(column, matrix, shift):
        return jnp.sum(column * matrix, axis=0, keepdims=True) + shift

    @pl.when(leader)
    def _():
        bcopy.wait_recv()
        column = jnp.broadcast_to(upright(bin_s[...]), (factors, factors))
        for at in range(1, chips - 1):
            for part in range(2):
                lcopy(at, part).wait_recv()
            step = lmaps[at]
            column = upright(carry(column, step[:factors], step[factors : factors + 1]))
        vout[...] = carry(column, whole[:factors], whole[factors : factors + 1])
        if pairs > 1:
            for to in range(plane):
                vstart(to).start()

    for slot in slots[:-1]:
        for part in range(2):
            ecopy(slot, 0, part).wait_recv()
    for part in range(2):
        ecopy(slots[-1], 0, part).wait_recv()
    parts = [emaps[slot_of(at)] for at in range(chips)]
    level = parts
    while len(level) > 1:
        level = [
            compose(level[i], level[i + 1], factors) if i + 1 < len(level) else level[i]
            for i in range(0, len(level), 2)
        ]
    total = level[0]

    def tcopy(side):
        return pltpu.make_async_remote_copy(
            tsend.at[used], trecv.at[used], ts.at[side], tr,
            device_id=(lax.rem(tm + 2, tms), y * 2 + side), device_id_type=MESH,
        )

    @pl.when(hands_map & (core == 0))
    def _():
        tsend[...] = total
        for side in range(2):
            tcopy(side).start()

    @pl.when(pair == 0)
    def _():
        vcur[...] = jnp.zeros_like(vcur)

    def forward():
        vcopy(1, 0).wait_recv()
        vcur[...] = vin[...]

        @pl.when(odd & (pair > 1))
        def _():
            tcopy(0).wait_recv()
            vcur[...] = carry(upright(vin[...]), trecv[0:factors], trecv[factors : factors + 1])

        @pl.when(odd & (pair < pairs - 1) & (core == 0))
        def _():
            vout[...] = carry(upright(vcur[...]), total[:factors], total[factors : factors + 1])

            @pl.when(pair < pairs - 2)
            def _():
                pl.semaphore_wait(there, 1)
                for side in range(2):
                    vcopy(2, side).start()

            for side in range(2):
                vcopy(1, side).start()

    @pl.when(pair == 1)
    def _():
        forward()

    unit = jnp.concatenate([eye_f, jnp.zeros((8, factors), F32)], axis=0)
    start_map = unit
    before_chip = [parts[0]]
    for at in range(1, chips):
        start_map = jnp.where(g == at, before_chip[-1], start_map)
        if at + 1 < chips:
            before_chip.append(compose(before_chip[-1], parts[at], factors))
    start_map = jnp.where(leads, start_map, compose(start_map, first, factors))
    cums = cum[...]
    lead = dot3(start_map, cums[:factors])
    lead_s[...] = halves(lead[:factors])
    lead_b = lead[factors:] + cums[factors:]
    at_end = pair == pairs - 1

    @pl.when(sums)
    def _():
        for slot in range(1, chips):
            for part in range(2):
                scopy(slot, part).wait_recv()
        group_adds = smaps[slot_of(0)] + jnp.where(at_end, span_w * decays, 0.0) * total
        for at in range(1, chips):
            group_adds = group_adds + jnp.exp(-float(2 * hours * at) * srate) * compose(
                before_chip[at - 1], smaps[slot_of(at)], factors
            )
        group_s[...] = group_adds

    @pl.when(pair > 1)
    def _():
        forward()

    def ccopy(to, of, side):
        return pltpu.make_async_remote_copy(
            shown, shifts.at[of], cs.at[to, side], cr.at[of],
            device_id=(to * 2 + a, y * 2 + side), device_id_type=MESH,
        )

    @pl.when(sums)
    def _():
        shown[...] = carry(
            upright(vcur[...]), group_s[0:factors], group_s[factors : factors + 1]
        )

        @pl.loop(0, pair)
        def _(to):
            for side in range(2):
                ccopy(to, pair, side).start()

    current = jnp.broadcast_to(vcur[...], (8, factors))
    filtered = dot_halves(current, lead_s[...]) + lead_b
    for h in range(hours):
        row = filtered[0:1, h * factors : (h + 1) * factors]
        fown[h : h + 1, :] = row
    fall[place_in] = fown[...]

    def fcopy(k):
        return pltpu.make_async_remote_copy(
            fown, fall.at[place_in], fs.at[k], fr.at[k],
            device_id=plane_peer(k), device_id_type=MESH,
        )

    for k in range(1, plane):
        fcopy(k).start()
    prec_root = jnp.sqrt(prec_ref[...])
    for k in range(1, plane):
        fcopy(k).wait_recv()
    together = fall[...]
    ending = decays * together[plane - 1][hours - 1 : hours]
    tail = jnp.sum(jnp.sum(together * tail_w, axis=0), axis=0, keepdims=True)
    rows_in = keep * jnp.concatenate([fall[a * sers + s] for s in range(sers)], axis=0)
    row_at = lax.broadcasted_iota(jnp.int32, (local, factors), 0)
    reach = 1
    while reach < local:
        later = jnp.where(row_at < local - reach, pltpu.roll(rows_in, local - reach, 0), 0.0)
        rows_in = rows_in + jnp.exp(-float(reach) * srate) * later
        reach *= 2
    fade = jnp.exp(-(local - row_at).astype(F32) * srate)
    rows_in = rows_in + fade * tail

    def gather(of, held):
        total, weight = held
        ccopy(pair, of, 0).wait_recv()
        return total + weight * shifts[of], weight * span_w

    beyond, _ = lax.fori_loop(
        pair + 1, pairs, gather, (jnp.where(at_end, ending, 0.0), jnp.ones_like(span_w))
    )
    smoothed_rows = rows_in + fade * (end_w * beyond)
    smoothed_ref[...] = smoothed_rows
    fitted = jnp.dot(smoothed_rows.astype(BF16), lt_s[:factors], preferred_element_type=F32)
    standard = (readings_ref[...].astype(F32) - fitted) * prec_root
    probab = 0.5 * (1.0 + lax.erf(standard * 0.7071067811865476))
    spot = jnp.where(present_ref[...] > 0, probab * BINS - 0.5, -4.0)
    padded = table.shape[0]
    across = lax.broadcasted_iota(jnp.int32, (8, spot.shape[1]), 0)
    picks = [across % 2 == 0, across // 2 % 2 == 0, across < 4]

    def above(knot):
        if knot > BINS:
            return jnp.zeros((8, spot.shape[1]), F32)
        over = jnp.maximum(0.0, spot - knot)
        total = over[:8]
        for at in range(8, local, 8):
            total = total + over[at : at + 8]
        return total

    for at in range(0, padded, 8):
        level = [above(at + i - 1) for i in range(8)]
        for pick, shift in zip(picks, (1, 2, 4)):
            level = [
                jnp.where(pick, x, z) + pltpu.roll(jnp.where(pick, z, x), shift, 0)
                for x, z in zip(level[::2], level[1::2])
            ]
        table[at : at + 8, :] = level[0]
    knots = table[...]
    next_knots = pltpu.roll(knots, padded - 1, 0)
    bins = knots - 2.0 * next_knots + pltpu.roll(knots, padded - 2, 0)
    bins = jnp.where(lax.broadcasted_iota(jnp.int32, bins.shape, 0) < BINS, bins, 0.0)
    th, tl = split2(bins)
    tally = jnp.dot(
        jnp.concatenate([th, tl], axis=0), mem_s[...], preferred_element_type=F32
    )
    tally = tally[:padded] + tally[padded:]
    lane = lax.broadcasted_iota(jnp.int32, tally.shape, 1) // GROUPS
    sub = lax.broadcasted_iota(jnp.int32, tally.shape, 0) % 8
    tally = jnp.where(lane == sub, tally, 0.0).reshape(padded // 8, 8, tally.shape[1])
    hown[...] = jnp.sum(tally, axis=1)
    hall[me] = hown[...]

    def hsend(k):
        at = lax.rem(place_in + (plane - 1 - k % plane), plane)
        turn = k // plane
        step = jnp.where(pair * 2 < pairs, pairs - 1 - turn, lax.rem(turn + 1, pairs))
        to = lax.rem(pair + step, pairs)
        pltpu.make_async_remote_copy(
            hown, hall.at[me], hs, hr,
            device_id=(to * 2 + at // sers, lax.rem(at, sers)), device_id_type=MESH,
        ).start()

    if n <= 64:
        for k in range(n - 1):
            hsend(k)
    else:
        pl.loop(0, n - 1)(hsend)

    for k in range(ys):
        for h in range(sets):
            copy1(k, h).wait_send()
            if k:
                copy2(k, h).wait_send()
    dcopy(0).wait_send()
    dcopy(1).wait_send()
    for part in range(2):

        @pl.when(core == part)
        def _(part=part):
            for side in range(2):
                for slot in slots:
                    ecopy(slot, side, part).wait_send()


    @pl.when(odd & (pair < pairs - 1) & (core == 0))
    def _():
        for side in range(2):
            vcopy(1, side).wait_send()

    for part in range(2):

        @pl.when((pair > 0) & (core == part))
        def _(part=part):
            for slot in slots:
                scopy(slot, part).wait_send()

    @pl.when(heads)
    def _():
        bcopy.wait_send()

    for part in range(2):

        @pl.when(helps & (core == part))
        def _(part=part):
            lcopy(g, part).wait_send()

    if pairs > 1:

        @pl.when(leader)
        def _():
            for to in range(plane):
                vstart(to).wait_send()

    @pl.when(odd & (pair < pairs - 2) & (core == 0))
    def _():
        for side in range(2):
            vcopy(2, side).wait_send()

    @pl.when(hands_map & (core == 0))
    def _():
        for side in range(2):
            tcopy(side).wait_send()

    for k in range(1, plane):
        fcopy(k).wait_send()

    @pl.when(sums)
    def _():
        @pl.loop(0, pair)
        def _(to):
            for side in range(2):
                ccopy(to, pair, side).wait_send()

    hdrain = pltpu.make_async_remote_copy(
        hall.at[pl.ds(0, n - 1)], hall.at[pl.ds(0, n - 1)], hs, hr,
        device_id=(tm, lax.rem(ser + 1, sers)), device_id_type=MESH,
    )
    hdrain.wait_recv()
    hdrain.wait_send()
    hist_ref[...] = jnp.sum(hall[...], axis=0)


def solution(mesh):
    tms, sers = mesh.shape["tm"], mesh.shape["series"]

    def body(readings, present, loadings, prec, gain, frate, srate, regions):
        local, series = readings.shape
        factors = loadings.shape[1]
        hours = local // sers
        n, ys = tms * sers, sers // 2
        chips = 2 * ys
        rows = factors + 8
        padded = -(-(BINS + 2) // 8) * 8
        together = 2 if hours % 2 == 0 else 1
        sets, packed_rows = hours // together, factors + 8
        vm = pltpu.VMEM
        dma = pltpu.SemaphoreType.DMA
        smoothed, packed = pl.pallas_call(
            functools.partial(kernel, tms, sers),
            out_shape=(
                vm((local, factors), F32),
                vm((padded // 8, 8 * GROUPS), F32),
            ),
            in_specs=[pl.BlockSpec(memory_space=pl.ANY)] * 8,
            out_specs=(pl.BlockSpec(memory_space=vm),) * 2,
            scratch_shapes=[
                vm((local, series), readings.dtype),
                vm((local, series), present.dtype),
                vm((series, factors), loadings.dtype),
                vm((1, series), F32),
                vm((1, factors), F32),
                vm((1, factors), F32),
                vm((1, factors), F32),
                vm((1, series), regions.dtype),
                vm((factors + local, series), BF16),
                vm((factors, series), BF16),
                vm((series, 8 * GROUPS), BF16),
                vm((ys, sets, packed_rows, factors), F32),
                vm((ys, sets, packed_rows, factors), F32),
                vm((ys, sets, packed_rows, factors), F32),
                vm((ys, sets, packed_rows, factors), F32),
                vm((rows, hours * factors), F32),
                vm((2, 2, rows, factors), F32),
                vm((chips, rows, factors), F32),
                vm((rows, factors), F32),
                vm((chips, rows, factors), F32),
                vm((rows, factors), F32),
                vm((3 * factors, hours * factors), BF16),
                vm((1, factors), F32),
                vm((1, factors), F32),
                vm((1, factors), F32),
                vm((1, factors), F32),
                vm((chips, rows, factors), F32),
                vm((rows, factors), F32),
                vm((rows, factors), F32),
                vm((hours, factors), F32),
                vm((2 * sers, hours, factors), F32),
                vm((1, factors), F32),
                vm((tms // 2, 1, factors), F32),
                vm((rows, factors), F32),
                vm((padded, series), F32),
                vm((padded // 8, 8 * GROUPS), F32),
                vm((n, padded // 8, 8 * GROUPS), F32),
                dma((8,)),
                dma((ys, sets)),
                dma((ys, sets)),
                dma((ys, sets)),
                dma((ys, sets)),
                dma((2,)),
                dma((2,)),
                dma((chips, 2)),
                dma((chips, 2)),
                dma((chips,)),
                dma((chips, 2)),
                dma((2, 2)), dma, dma((2 * sers,)), dma((2,)), dma((chips, 2)), dma, dma, dma((2,)), dma, pltpu.SemaphoreType.REGULAR,
                dma((2 * sers,)),
                dma((2 * sers,)),
                dma((tms // 2, 2)),
                dma((tms // 2,)),
                dma, dma,
            ],
            compiler_params=pltpu.CompilerParams(collective_id=0, has_side_effects=True),
        )(
            readings, present, loadings, prec.reshape(1, -1), gain.reshape(1, -1),
            frate.reshape(1, -1), srate.reshape(1, -1), regions.reshape(1, -1),
        )
        scale = BINS * GROUPS / (local * tms * series * sers)
        return pl.pallas_call(
            functools.partial(finish, scale),
            out_shape=(
                jax.ShapeDtypeStruct((local, factors), F32),
                jax.ShapeDtypeStruct((GROUPS, BINS), F32),
            ),
            in_specs=[pl.BlockSpec(memory_space=vm)] * 2,
            out_specs=(pl.BlockSpec(memory_space=pl.ANY),) * 2,
            scratch_shapes=[vm((GROUPS, BINS), F32), dma((2,))],
        )(*(pltpu.with_memory_space_constraint(part, vm) for part in (smoothed, packed)))

    in_specs = (
        P("tm", "series"), P("tm", "series"), P("series", None), P("series"),
        P(), P(), P(), P("series"),
    )
    return jax.shard_map(
        body, mesh=mesh, in_specs=in_specs, out_specs=(P("tm", None), P()), check_vma=False
    )
```

```python
import functools

import jax
import jax.numpy as jnp
from jax import lax
from jax.experimental import pallas as pl
from jax.experimental.pallas import tpu as pltpu
from jax.sharding import PartitionSpec as P

BINS = 20
GROUPS = 16
MESH = pl.DeviceIdType.MESH
F32 = jnp.float32
BF16 = jnp.bfloat16


def split2(x):
    high = x.astype(BF16)
    return high, (x - high.astype(F32)).astype(BF16)


def halves(right):
    high, low = split2(right)
    return jnp.concatenate([high, low, high], axis=0)


def dot_halves(left, right):
    high, low = split2(left)
    return jnp.dot(
        jnp.concatenate([high, high, low], axis=1), right, preferred_element_type=F32
    )


def dot_t(left, right):
    return lax.dot_general(left, right, (((1,), (1,)), ((), ())), preferred_element_type=F32)


def dot3(left, right):
    return dot_halves(left, halves(right))


def compose(earlier, later, factors):
    out = dot3(earlier, later[:factors])
    return jnp.concatenate([out[:factors], out[factors:] + later[factors:]], axis=0)


LINES = -(-(BINS + 2) // 8)


def finish(scale, rows_ref, packed_ref, smoothed_ref, hist_ref, held, sems):
    rows_out = pltpu.make_async_copy(rows_ref, smoothed_ref, sems.at[0])
    rows_out.start()
    packed = packed_ref[...] * scale
    width = packed.shape[1]
    parts = []
    for at in range(LINES):
        parts += [packed[at : at + 1], jnp.zeros((7, width), F32)]
    tall = jnp.concatenate(parts, axis=0).T
    tall = jnp.concatenate([tall, jnp.zeros((width, width - 8 * LINES), F32)], axis=1)
    total = tall[:GROUPS]
    for j in range(1, 8):
        total = total + pltpu.roll(tall[j * GROUPS : (j + 1) * GROUPS], j, 1)
    held[...] = total[:, :BINS]
    hist_out = pltpu.make_async_copy(held, hist_ref, sems.at[1])
    hist_out.start()
    rows_out.wait()
    hist_out.wait()


def kernel(
    tms, sers,
    readings_in, present_in, loadings_in, prec_in, gain_in, frate_in, srate_in, regions_in,
    smoothed_ref, hist_ref,
    readings_ref, present_ref, loadings_ref, prec_ref, gain_ref, frate_ref, srate_ref, regions_ref,
    lt_s, sl_s, mem_s, send1, recv1, acc, recv2, cum, dmap, emaps, esend, smaps, ssend, lead_s,
    vin, vout, vcur, bin_s, lmaps, tsend, trecv, fown, fall, shown, shifts, group_s, table, hown, hall,
    ins, s1s, s1r, s2s, s2r, ds, dr, es, er, ss, sr, vs, vr, vls, ls, lr, bs, br, ts, tr, there, fs, fr, cs, cr, hs, hr,
):
    tm, ser = lax.axis_index("tm"), lax.axis_index("series")
    y, core = ser // 2, ser % 2
    ys = sers // 2
    local = readings_ref.shape[0]
    factors = loadings_ref.shape[1]
    rows = factors + 8
    hours = local // sers
    n = tms * sers
    me = tm * sers + ser
    pair, a = tm // 2, tm % 2
    pairs = tms // 2
    chips = 2 * ys
    g = a * ys + y
    leader = (pair == 0) & (g == chips - 1) & (core == 0)
    odd = pair % 2 == 1
    hands_map = (pair % 2 == 0) & (pair > 0) & (pair < pairs - 1)

    inputs = [
        pltpu.make_async_copy(src, dst, ins.at[i])
        for i, (src, dst) in enumerate(
            [
                (loadings_in, loadings_ref), (prec_in, prec_ref), (present_in, present_ref),
                (readings_in, readings_ref), (gain_in, gain_ref), (frate_in, frate_ref),
                (srate_in, srate_ref), (regions_in, regions_ref),
            ]
        )
    ]
    for item in inputs:
        item.start()

    barrier = pltpu.get_barrier_semaphore()

    plane = 2 * sers
    place_in = a * sers + ser

    def plane_peer(k):
        at = lax.rem(place_in + k, plane)
        return pair * 2 + at // sers, lax.rem(at, sers)

    for k in range(1, plane):
        pl.semaphore_signal(barrier, inc=1, device_id=plane_peer(k), device_id_type=MESH)
    @pl.when(pair > 0)
    def _():
        pl.semaphore_signal(barrier, inc=1, device_id=(tm - 2, ser), device_id_type=MESH)

    @pl.when((pair > 0) & (core == 1))
    def _():
        pl.semaphore_signal(barrier, inc=1, device_id=(tm - 2, y * 2), device_id_type=MESH)

    @pl.when(pair < pairs - 1)
    def _():
        pl.semaphore_signal(barrier, inc=1, device_id=(tm + 2, ser), device_id_type=MESH)

    @pl.when((pair == 1) & ((g < chips - 1) | (core == 1)))
    def _():
        pl.semaphore_signal(barrier, inc=1, device_id=(1, (ys - 1) * 2), device_id_type=MESH)

    for item in inputs[:2]:
        item.wait()

    turned_l = loadings_ref[...].T
    lt_s[:factors] = turned_l
    sl_s[...] = (turned_l.astype(F32) * prec_ref[...]).astype(BF16)
    for item in inputs[2:4]:
        item.wait()
    lt_s[factors:] = readings_ref[...].astype(BF16)

    together_h = 2 if hours % 2 == 0 else 1
    sets = hours // together_h
    sub = lax.broadcasted_iota(jnp.int32, (factors, factors), 0)
    lane = lax.broadcasted_iota(jnp.int32, (factors, factors), 1)
    eye = sub == lane
    upper = lane > sub
    line = lax.broadcasted_iota(jnp.int32, (8, factors), 0)
    which = lax.broadcasted_iota(jnp.int32, (local, factors), 0)

    def hour_terms(base, dst, held):
        rights = []
        for j in range(len(held) * together_h):
            mask = present_ref[pl.ds(base + j, 1), :].astype(F32)
            mask = jnp.broadcast_to(mask, (16, mask.shape[1])).astype(BF16)
            right = sl_s[...].reshape(factors // 16, 16, mask.shape[1]) * mask[None]
            rights.append(right.reshape(factors, mask.shape[1]))
        out = dot_t(lt_s[...], jnp.concatenate(rights, axis=0))
        for place, h in enumerate(held):
            at = place * together_h
            first = out[:factors, at * factors : (at + 1) * factors]
            tail = jnp.zeros((8, factors), F32)
            if together_h == 2:
                second = out[:factors, (at + 1) * factors : (at + 2) * factors]
                dst[h, :factors] = jnp.where(upper, first, second)
                corner = jnp.sum(jnp.where(eye, first, 0.0), axis=0, keepdims=True)
                tail = jnp.where(line == together_h, corner, tail)
            else:
                dst[h, :factors] = first
            for j in range(together_h):
                row = out[factors:, (at + j) * factors : (at + j + 1) * factors]
                row = jnp.sum(jnp.where(which == base + at + j, row, 0.0), axis=0, keepdims=True)
                tail = jnp.where(line == j, row, tail)
            dst[h, factors:] = tail

    def unpack(packed):
        block, tail = packed[:factors], packed[factors:]
        if together_h == 1:
            matrices = [block]
        else:
            turned = block.T
            matrices = [
                jnp.where(eye, tail[together_h : together_h + 1], jnp.where(upper, block, turned)),
                jnp.where(upper, turned, block),
            ]
        return [
            (matrices[j], jnp.where(line == 0, tail[j : j + 1], 0.0)) for j in range(together_h)
        ]

    used, sent = pl.ds(0, factors + 1), pl.ds(0, factors + together_h + 1)

    def copy1(k, h):
        return pltpu.make_async_remote_copy(
            send1.at[k, h, sent], recv1.at[k, h, sent], s1s.at[k, h], s1r.at[k, h],
            device_id=(tm, y * 2 + (1 - core)), device_id_type=MESH,
        )

    def copy2(k, h):
        return pltpu.make_async_remote_copy(
            acc.at[k, h, sent], recv2.at[k, h, sent], s2s.at[k, h], s2r.at[k, h],
            device_id=(tm, lax.rem(y + k, ys) * 2 + core), device_id_type=MESH,
        )

    order = list(range(1, ys)) + [0]
    for place, k in enumerate(order):
        owner = lax.rem(y + k, ys) * 2
        theirs, ours = (owner + (1 - core)) * hours, (owner + core) * hours
        groups = [[h] for h in range(sets)] if k else [list(range(sets))]
        for held in groups:
            hour_terms(theirs + held[0] * together_h, send1.at[k], held)
            if place == 0 and held[0] == 0:
                before = jnp.where(pair > 0, 1, 0)
                behind = jnp.where(pair < pairs - 1, 2 - core, 0)
                extra = jnp.where(leader, 2 * chips - 1, 0)
                pl.semaphore_wait(barrier, plane - 1 + before + behind + extra)

                @pl.when(hands_map & (core == 0))
                def _():
                    pl.semaphore_signal(there, inc=1, device_id=(tm - 2, y * 2), device_id_type=MESH)

            for h in held:
                copy1(k, h).start()
        for held in groups:
            hour_terms(ours + held[0] * together_h, acc.at[k], held)
            for h in held if k else []:
                copy1(k, h).wait_recv()
                acc[k, h] = acc[k, h] + recv1[k, h]
                copy2(k, h).start()

    for item in inputs[4:]:
        item.wait()
    wide = lax.broadcasted_iota(jnp.int32, (factors, regions_ref.shape[1]), 0) % GROUPS
    mem_s[...] = jnp.where(wide == regions_ref[...], 1.0, 0.0).astype(F32).T.astype(BF16)
    gain = gain_ref[...]
    decays = jnp.exp(-frate_ref[...])
    srate = srate_ref[...]
    retain = jnp.exp(-srate)
    keep = 1.0 - retain * decays
    eye_f = jnp.where(eye, 1.0, 0.0).astype(F32)
    decay_col = jnp.sum(jnp.where(eye, decays, 0.0), axis=1, keepdims=True)
    for h in range(sets):
        copy1(0, h).wait_recv()

    maps = []
    for h in range(sets):
        total = acc[0, h] + recv1[0, h]
        for k in range(1, ys):
            copy2(k, h).wait_recv()
            total = total + recv2[k, h]
        fresh = [
            jnp.concatenate([decay_col * (eye_f - gain * inform), gain * scores], axis=0)
            for inform, scores in unpack(total)
        ]
        if together_h == 2:
            fresh[1] = compose(fresh[0], fresh[1], factors)
        if maps:
            fresh = [compose(maps[-1], item, factors) for item in fresh]
        maps += fresh
    dmap[core, 0] = maps[-1]

    def dcopy(part):
        return pltpu.make_async_remote_copy(
            dmap.at[core, part], dmap.at[core, part], ds.at[part], dr.at[part],
            device_id=(tm, y * 2 + (1 - core)), device_id_type=MESH,
        )

    dcopy(0).start()
    adds = keep * maps[0]
    for h in range(1, hours):
        adds = adds + keep * jnp.exp(-float(h) * srate) * maps[h]
    dmap[core, 1] = adds
    dcopy(1).start()
    for h in range(hours):
        cum[:, h * factors : (h + 1) * factors] = maps[h]
    dcopy(0).wait_recv()
    leads = core == 0
    first = dmap[0, 0]
    whole = compose(first, dmap[1, 0], factors)
    esend[...] = whole

    def slot_peer(slot):
        return pair * 2 + (a + slot // ys) % 2, lax.rem(y + slot % ys, ys) * 2 + core

    def slot_of(at):
        return ((a + 2 - at // ys) % 2) * ys + lax.rem(y + ys - at % ys, ys)

    half = factors // 2
    spans = [pl.ds(0, half), pl.ds(half, half + 1)]

    def ecopy(slot, side, part):
        row, column = slot_peer(slot)
        return pltpu.make_async_remote_copy(
            esend.at[spans[part]], emaps.at[slot, spans[part]],
            es.at[slot, side], er.at[slot, part],
            device_id=(row, column - core + side), device_id_type=MESH,
        )

    bcopy = pltpu.make_async_remote_copy(
        esend.at[pl.ds(factors, 1)], bin_s, bs, br,
        device_id=(1, (ys - 1) * 2), device_id_type=MESH,
    )
    heads = (pair == 0) & (g == 0) & (core == 0)

    def lcopy(of, part):
        span = pl.ds(0, half) if part == 0 else pl.ds(half, rows - half)
        return pltpu.make_async_remote_copy(
            esend.at[span], lmaps.at[of, span], ls.at[part], lr.at[of, part],
            device_id=(1, (ys - 1) * 2), device_id_type=MESH,
        )

    helps = (pair == 0) & (g > 0) & (g < chips - 1)
    for part in range(2):

        @pl.when(helps & (core == part))
        def _(part=part):
            lcopy(g, part).start()

    @pl.when(heads)
    def _():
        bcopy.start()

    slots = [ys] + [slot for slot in range(1, chips) if slot != ys]
    for part in range(2):

        @pl.when((core == part) & (pair > 0))
        def _(part=part):
            for side in range(2):
                for slot in slots:
                    ecopy(slot, side, part).start()

        @pl.when((core == part) & (pair == 0))
        def _(part=part):
            for slot in slots:
                for side in range(2):
                    ecopy(slot, side, part).start()

    emaps[0] = whole
    dcopy(1).wait_recv()
    chip_adds = dmap[0, 1] + jnp.exp(-float(hours) * srate) * compose(first, dmap[1, 1], factors)
    ssend[...] = chip_adds

    def scopy(slot, part):
        span = pl.ds(0, half) if part == 0 else pl.ds(half, half + 1)
        row, column = slot_peer(slot)
        return pltpu.make_async_remote_copy(
            ssend.at[span], smaps.at[slot, span], ss.at[slot], sr.at[slot, part],
            device_id=(row, column - core), device_id_type=MESH,
        )

    sums = (core == 0) & (pair > 0)
    for part in range(2):

        @pl.when((pair > 0) & (core == part))
        def _(part=part):
            for slot in slots:
                scopy(slot, part).start()

    smaps[0] = chip_adds
    span = 2 * local
    after = (a + 1) * local
    hour_at = (
        lax.broadcasted_iota(jnp.int32, (plane, hours, factors), 0) * hours
        + lax.broadcasted_iota(jnp.int32, (plane, hours, factors), 1)
    )
    far = (hour_at - after).astype(F32)
    tail_w = jnp.where(far >= 0.0, keep[None] * jnp.exp(-jnp.maximum(far, 0.0) * srate[None]), 0.0)
    end_w = jnp.exp(-(span - after).astype(F32) * srate)
    span_w = jnp.exp(-float(span) * srate)
    def vcopy(far, side):
        return pltpu.make_async_remote_copy(
            vout, vin, vs.at[far - 1, side], vr,
            device_id=(lax.rem(tm + 2 * far, tms), y * 2 + side), device_id_type=MESH,
        )

    def vstart(to):
        return pltpu.make_async_remote_copy(
            vout, vin, vls.at[to], vr,
            device_id=(2 + to // sers, to % sers), device_id_type=MESH,
        )

    def upright(vector):
        return jnp.sum(jnp.where(eye, vector, 0.0), axis=1, keepdims=True)

    def carry(column, matrix, shift):
        return jnp.sum(column * matrix, axis=0, keepdims=True) + shift

    @pl.when(leader)
    def _():
        bcopy.wait_recv()
        column = jnp.broadcast_to(upright(bin_s[...]), (factors, factors))
        for at in range(1, chips - 1):
            for part in range(2):
                lcopy(at, part).wait_recv()
            step = lmaps[at]
            column = upright(carry(column, step[:factors], step[factors : factors + 1]))
        vout[...] = carry(column, whole[:factors], whole[factors : factors + 1])
        if pairs > 1:
            for to in range(plane):
                vstart(to).start()

    for slot in slots[:-1]:
        for part in range(2):
            ecopy(slot, 0, part).wait_recv()
    for part in range(2):
        ecopy(slots[-1], 0, part).wait_recv()
    parts = [emaps[slot_of(at)] for at in range(chips)]
    level = parts
    while len(level) > 1:
        level = [
            compose(level[i], level[i + 1], factors) if i + 1 < len(level) else level[i]
            for i in range(0, len(level), 2)
        ]
    total = level[0]

    def tcopy(side):
        return pltpu.make_async_remote_copy(
            tsend.at[used], trecv.at[used], ts.at[side], tr,
            device_id=(lax.rem(tm + 2, tms), y * 2 + side), device_id_type=MESH,
        )

    @pl.when(hands_map & (core == 0))
    def _():
        tsend[...] = total
        for side in range(2):
            tcopy(side).start()

    @pl.when(pair == 0)
    def _():
        vcur[...] = jnp.zeros_like(vcur)

    def forward():
        vcopy(1, 0).wait_recv()
        vcur[...] = vin[...]

        @pl.when(odd & (pair > 1))
        def _():
            tcopy(0).wait_recv()
            vcur[...] = carry(upright(vin[...]), trecv[0:factors], trecv[factors : factors + 1])

        @pl.when(odd & (pair < pairs - 1) & (core == 0))
        def _():
            vout[...] = carry(upright(vcur[...]), total[:factors], total[factors : factors + 1])

            @pl.when(pair < pairs - 2)
            def _():
                pl.semaphore_wait(there, 1)
                for side in range(2):
                    vcopy(2, side).start()

            for side in range(2):
                vcopy(1, side).start()

    @pl.when(pair == 1)
    def _():
        forward()

    unit = jnp.concatenate([eye_f, jnp.zeros((8, factors), F32)], axis=0)
    start_map = unit
    before_chip = [parts[0]]
    for at in range(1, chips):
        start_map = jnp.where(g == at, before_chip[-1], start_map)
        if at + 1 < chips:
            before_chip.append(compose(before_chip[-1], parts[at], factors))
    start_map = jnp.where(leads, start_map, compose(start_map, first, factors))
    cums = cum[...]
    lead = dot3(start_map, cums[:factors])
    lead_s[...] = halves(lead[:factors])
    lead_b = lead[factors:] + cums[factors:]
    at_end = pair == pairs - 1

    @pl.when(sums)
    def _():
        for slot in range(1, chips):
            for part in range(2):
                scopy(slot, part).wait_recv()
        group_adds = smaps[slot_of(0)] + jnp.where(at_end, span_w * decays, 0.0) * total
        for at in range(1, chips):
            group_adds = group_adds + jnp.exp(-float(2 * hours * at) * srate) * compose(
                before_chip[at - 1], smaps[slot_of(at)], factors
            )
        group_s[...] = group_adds

    @pl.when(pair > 1)
    def _():
        forward()

    def ccopy(to, of, side):
        return pltpu.make_async_remote_copy(
            shown, shifts.at[of], cs.at[to, side], cr.at[of],
            device_id=(to * 2 + a, y * 2 + side), device_id_type=MESH,
        )

    @pl.when(sums)
    def _():
        shown[...] = carry(
            upright(vcur[...]), group_s[0:factors], group_s[factors : factors + 1]
        )

        @pl.loop(0, pair)
        def _(to):
            for side in range(2):
                ccopy(to, pair, side).start()

    current = jnp.broadcast_to(vcur[...], (8, factors))
    filtered = dot_halves(current, lead_s[...]) + lead_b
    for h in range(hours):
        row = filtered[0:1, h * factors : (h + 1) * factors]
        fown[h : h + 1, :] = row
    fall[place_in] = fown[...]

    def fcopy(k):
        return pltpu.make_async_remote_copy(
            fown, fall.at[place_in], fs.at[k], fr.at[k],
            device_id=plane_peer(k), device_id_type=MESH,
        )

    for k in range(1, plane):
        fcopy(k).start()
    prec_root = jnp.sqrt(prec_ref[...])
    for k in range(1, plane):
        fcopy(k).wait_recv()
    together = fall[...]
    ending = decays * together[plane - 1][hours - 1 : hours]
    tail = jnp.sum(jnp.sum(together * tail_w, axis=0), axis=0, keepdims=True)
    rows_in = keep * jnp.concatenate([fall[a * sers + s] for s in range(sers)], axis=0)
    row_at = lax.broadcasted_iota(jnp.int32, (local, factors), 0)
    reach = 1
    while reach < local:
        later = jnp.where(row_at < local - reach, pltpu.roll(rows_in, local - reach, 0), 0.0)
        rows_in = rows_in + jnp.exp(-float(reach) * srate) * later
        reach *= 2
    fade = jnp.exp(-(local - row_at).astype(F32) * srate)
    rows_in = rows_in + fade * tail

    def gather(of, held):
        total, weight = held
        ccopy(pair, of, 0).wait_recv()
        return total + weight * shifts[of], weight * span_w

    beyond, _ = lax.fori_loop(
        pair + 1, pairs, gather, (jnp.where(at_end, ending, 0.0), jnp.ones_like(span_w))
    )
    smoothed_rows = rows_in + fade * (end_w * beyond)
    smoothed_ref[...] = smoothed_rows
    fitted = jnp.dot(smoothed_rows.astype(BF16), lt_s[:factors], preferred_element_type=F32)
    standard = (readings_ref[...].astype(F32) - fitted) * prec_root
    probab = 0.5 * (1.0 + lax.erf(standard * 0.7071067811865476))
    spot = jnp.where(present_ref[...] > 0, probab * BINS - 0.5, -4.0)
    padded = table.shape[0]
    across = lax.broadcasted_iota(jnp.int32, (8, spot.shape[1]), 0)
    picks = [across % 2 == 0, across // 2 % 2 == 0, across < 4]

    def above(knot):
        if knot > BINS:
            return jnp.zeros((8, spot.shape[1]), F32)
        over = jnp.maximum(0.0, spot - knot)
        total = over[:8]
        for at in range(8, local, 8):
            total = total + over[at : at + 8]
        return total

    for at in range(0, padded, 8):
        level = [above(at + i - 1) for i in range(8)]
        for pick, shift in zip(picks, (1, 2, 4)):
            level = [
                jnp.where(pick, x, z) + pltpu.roll(jnp.where(pick, z, x), shift, 0)
                for x, z in zip(level[::2], level[1::2])
            ]
        table[at : at + 8, :] = level[0]
    knots = table[...]
    next_knots = pltpu.roll(knots, padded - 1, 0)
    bins = knots - 2.0 * next_knots + pltpu.roll(knots, padded - 2, 0)
    bins = jnp.where(lax.broadcasted_iota(jnp.int32, bins.shape, 0) < BINS, bins, 0.0)
    th, tl = split2(bins)
    tally = jnp.dot(
        jnp.concatenate([th, tl], axis=0), mem_s[...], preferred_element_type=F32
    )
    tally = tally[:padded] + tally[padded:]
    lane = lax.broadcasted_iota(jnp.int32, tally.shape, 1) // GROUPS
    sub = lax.broadcasted_iota(jnp.int32, tally.shape, 0) % 8
    tally = jnp.where(lane == sub, tally, 0.0).reshape(padded // 8, 8, tally.shape[1])
    hown[...] = jnp.sum(tally, axis=1)
    hall[me] = hown[...]

    def hsend(k):
        at = lax.rem(place_in + (plane - 1 - k % plane), plane)
        turn = k // plane
        step = jnp.where(pair * 2 < pairs, pairs - 1 - turn, lax.rem(turn + 1, pairs))
        to = lax.rem(pair + step, pairs)
        pltpu.make_async_remote_copy(
            hown, hall.at[me], hs, hr,
            device_id=(to * 2 + at // sers, lax.rem(at, sers)), device_id_type=MESH,
        ).start()

    if n <= 64:
        for k in range(n - 1):
            hsend(k)
    else:
        pl.loop(0, n - 1)(hsend)

    for k in range(ys):
        for h in range(sets):
            copy1(k, h).wait_send()
            if k:
                copy2(k, h).wait_send()
    dcopy(0).wait_send()
    dcopy(1).wait_send()
    for part in range(2):

        @pl.when(core == part)
        def _(part=part):
            for side in range(2):
                for slot in slots:
                    ecopy(slot, side, part).wait_send()


    @pl.when(odd & (pair < pairs - 1) & (core == 0))
    def _():
        for side in range(2):
            vcopy(1, side).wait_send()

    for part in range(2):

        @pl.when((pair > 0) & (core == part))
        def _(part=part):
            for slot in slots:
                scopy(slot, part).wait_send()

    @pl.when(heads)
    def _():
        bcopy.wait_send()

    for part in range(2):

        @pl.when(helps & (core == part))
        def _(part=part):
            lcopy(g, part).wait_send()

    if pairs > 1:

        @pl.when(leader)
        def _():
            for to in range(plane):
                vstart(to).wait_send()

    @pl.when(odd & (pair < pairs - 2) & (core == 0))
    def _():
        for side in range(2):
            vcopy(2, side).wait_send()

    @pl.when(hands_map & (core == 0))
    def _():
        for side in range(2):
            tcopy(side).wait_send()

    for k in range(1, plane):
        fcopy(k).wait_send()

    @pl.when(sums)
    def _():
        @pl.loop(0, pair)
        def _(to):
            for side in range(2):
                ccopy(to, pair, side).wait_send()

    hdrain = pltpu.make_async_remote_copy(
        hall.at[pl.ds(0, n - 1)], hall.at[pl.ds(0, n - 1)], hs, hr,
        device_id=(tm, lax.rem(ser + 1, sers)), device_id_type=MESH,
    )
    hdrain.wait_recv()
    hdrain.wait_send()
    hist_ref[...] = jnp.sum(hall[...], axis=0)


def solution(mesh):
    tms, sers = mesh.shape["tm"], mesh.shape["series"]

    def body(readings, present, loadings, prec, gain, frate, srate, regions):
        local, series = readings.shape
        factors = loadings.shape[1]
        hours = local // sers
        n, ys = tms * sers, sers // 2
        chips = 2 * ys
        rows = factors + 8
        padded = -(-(BINS + 2) // 8) * 8
        together = 2 if hours % 2 == 0 else 1
        sets, packed_rows = hours // together, factors + 8
        vm = pltpu.VMEM
        dma = pltpu.SemaphoreType.DMA
        smoothed, packed = pl.pallas_call(
            functools.partial(kernel, tms, sers),
            out_shape=(
                vm((local, factors), F32),
                vm((padded // 8, 8 * GROUPS), F32),
            ),
            in_specs=[pl.BlockSpec(memory_space=pl.ANY)] * 8,
            out_specs=(pl.BlockSpec(memory_space=vm),) * 2,
            scratch_shapes=[
                vm((local, series), readings.dtype),
                vm((local, series), present.dtype),
                vm((series, factors), loadings.dtype),
                vm((1, series), F32),
                vm((1, factors), F32),
                vm((1, factors), F32),
                vm((1, factors), F32),
                vm((1, series), regions.dtype),
                vm((factors + local, series), BF16),
                vm((factors, series), BF16),
                vm((series, 8 * GROUPS), BF16),
                vm((ys, sets, packed_rows, factors), F32),
                vm((ys, sets, packed_rows, factors), F32),
                vm((ys, sets, packed_rows, factors), F32),
                vm((ys, sets, packed_rows, factors), F32),
                vm((rows, hours * factors), F32),
                vm((2, 2, rows, factors), F32),
                vm((chips, rows, factors), F32),
                vm((rows, factors), F32),
                vm((chips, rows, factors), F32),
                vm((rows, factors), F32),
                vm((3 * factors, hours * factors), BF16),
                vm((1, factors), F32),
                vm((1, factors), F32),
                vm((1, factors), F32),
                vm((1, factors), F32),
                vm((chips, rows, factors), F32),
                vm((rows, factors), F32),
                vm((rows, factors), F32),
                vm((hours, factors), F32),
                vm((2 * sers, hours, factors), F32),
                vm((1, factors), F32),
                vm((tms // 2, 1, factors), F32),
                vm((rows, factors), F32),
                vm((padded, series), F32),
                vm((padded // 8, 8 * GROUPS), F32),
                vm((n, padded // 8, 8 * GROUPS), F32),
                dma((8,)),
                dma((ys, sets)),
                dma((ys, sets)),
                dma((ys, sets)),
                dma((ys, sets)),
                dma((2,)),
                dma((2,)),
                dma((chips, 2)),
                dma((chips, 2)),
                dma((chips,)),
                dma((chips, 2)),
                dma((2, 2)), dma, dma((2 * sers,)), dma((2,)), dma((chips, 2)), dma, dma, dma((2,)), dma, pltpu.SemaphoreType.REGULAR,
                dma((2 * sers,)),
                dma((2 * sers,)),
                dma((tms // 2, 2)),
                dma((tms // 2,)),
                dma, dma,
            ],
            compiler_params=pltpu.CompilerParams(collective_id=0, has_side_effects=True),
        )(
            readings, present, loadings, prec.reshape(1, -1), gain.reshape(1, -1),
            frate.reshape(1, -1), srate.reshape(1, -1), regions.reshape(1, -1),
        )
        scale = BINS * GROUPS / (local * tms * series * sers)
        return pl.pallas_call(
            functools.partial(finish, scale),
            out_shape=(
                jax.ShapeDtypeStruct((local, factors), F32),
                jax.ShapeDtypeStruct((GROUPS, BINS), F32),
            ),
            in_specs=[pl.BlockSpec(memory_space=vm)] * 2,
            out_specs=(pl.BlockSpec(memory_space=pl.ANY),) * 2,
            scratch_shapes=[vm((GROUPS, BINS), F32), dma((2,))],
        )(*(pltpu.with_memory_space_constraint(part, vm) for part in (smoothed, packed)))

    in_specs = (
        P("tm", "series"), P("tm", "series"), P("series", None), P("series"),
        P(), P(), P(), P("series"),
    )
    return jax.shard_map(
        body, mesh=mesh, in_specs=in_specs, out_specs=(P("tm", None), P()), check_vma=False
    )
```
